32 devices in a mesh: groups: 2 (over x), expert: 16 (over z, y, core).
Axes of the slice: x: 2, y: 2, z: 4, core: 2. Of those that a mesh axis runs over, the one named last changes fastest.
Arguments:
- h_rows: bfloat16 [4096, 8, 768], P(('groups', 'expert')), parts along dimension 0, may hold values from -6 to 6
- gates: float32 [4096, 8], P(('groups', 'expert')), parts along dimension 0, may hold values from 0.05 to 0.5
- expert_ids: int32 [4096, 8], P(('groups', 'expert')), parts along dimension 0, may hold values from 0 to 15, all different within a row; in each aligned block of 128 rows (0 to 127, 128 to 255, ...) at most 96 rows name the same one
- cotangent: bfloat16 [4096, 2048], P(('groups', 'expert')), parts along dimension 0, may hold values from -1.1953125 to 1.1953125
- down_weight: bfloat16 [16, 768, 2048], P('expert'), may hold values from -0.21875 to 0.21875
- swapped: int32 [8], replicated, may hold values 0 or 1
Outputs:
- mixed: bfloat16 [4096, 2048], P(('groups', 'expert')), parts along dimension 0
- gate_grad: float32 [4096, 8], P(('groups', 'expert')), parts along dimension 0
- h_grad: bfloat16 [4096, 8, 768], P(('groups', 'expert')), parts along dimension 0
- weight_grad: bfloat16 [32, 768, 2048], P(('groups', 'expert')), parts along dimension 0
The draws below stay inside these ranges and needn't reach their ends.
There are 2 independent parts, one for each index of `groups`. The reference program is written for one: setup_inputs(seed, part) draws one part's arguments, and reference() takes and returns one part's arrays. A program takes and returns all parts, laid end to end along the dimension named above; an argument that names none is the same for every part. Nothing has to cross between parts.
Inputs may be any that keep to these rules, and one draw needn't show every extreme that they name: `expert_ids`: among the rows of one device, no expert is named by more than 96 of the (token, choice) pairs, and in every draw some expert is named by exactly 96 of them on some device; each token names 8 different experts.
All inputs are finite; a program needn't handle non-finite values.
Results may differ from the reference program's by a relative error of at most 0.008.
Values may be sent and summed in bfloat16 or wider, within the bound.
No kernel may reach another device: no remote copies, remote signals or barrier semaphores. Data moves between devices by JAX's collectives and lax.ppermute only.
A program may use at most 128 MiB of HBM per device.

```python
import math
import jax
import jax.numpy as jnp
import numpy as np
from jax import lax

D = 2048
FF = 768
TOP = 8
TOK_DEV = 128
EXPERTS = 16
TOKENS = 2048
CAP = 96
N_EXPERT = 16


def with_ends(drawn, stream_key, low, top_value):
    place = [jax.random.randint(jax.random.fold_in(stream_key, axis), (), 0, length) for axis, length in enumerate(drawn.shape)]
    longest = drawn.shape.index(max(drawn.shape))
    neighbour = place[:longest] + [(place[longest] + 1) % drawn.shape[longest]] + place[longest + 1:]
    return drawn.at[tuple(place)].set(low).at[tuple(neighbour)].set(top_value)


def levels(own_key, dims, pieces, smallest, largest):
    def one(dim, parts):
        heights = jax.random.uniform(jax.random.fold_in(jax.random.fold_in(own_key, 6), dim), (parts,), jnp.float32, smallest / len(pieces), largest / len(pieces))
        return jnp.repeat(jnp.exp(heights), dims[dim] // parts).reshape((-1,) + (1,) * (len(dims) - dim - 1))

    level = one(*pieces[0])
    for cut in pieces[1:]:
        level = level * one(*cut)
    return level


def routed_block(rng, own, number, rows, number_of, top, reach, skew):
    ranking = jax.random.permutation(rng, number_of)
    heavy_load, ordinary = load_shares(number_of, rows * top, reach, skew, True), load_shares(number_of, rows * top, reach, skew, False)
    places = jnp.arange(number_of)

    def named(sizes, turn):
        used = int((sizes > 0).sum())
        fixed = max(1, used // 4)
        moved = fixed + (places - fixed + turn * (used - fixed)) % max(1, number_of - fixed)
        return jnp.zeros((number_of,), jnp.int32).at[ranking[jnp.where(places < fixed, places, moved)]].set(jnp.asarray(sizes, jnp.int32))

    sizes = jnp.where(number % 4 == 0, named(heavy_load, number // 4), named(ordinary, number - number // 4 - 1))
    mixed = jax.random.permutation(jax.random.fold_in(own, 3), number_of)
    giver, taker = mixed[0:number_of // 2 * 2:2], mixed[1:number_of // 2 * 2:2]
    room = jnp.minimum(sizes[giver] - 1, reach - sizes[taker]) // 2
    room = jnp.where((giver == ranking[0]) | (taker == ranking[0]) | (sizes[taker] == 0), 0, jnp.maximum(room, 0))
    moved = jax.random.randint(jax.random.fold_in(own, 4), (number_of // 2,), 0, 1 << 20) % (room + 1)
    sizes = sizes.at[giver].add(-moved).at[taker].add(moved)
    items = jnp.searchsorted(jnp.cumsum(sizes), jnp.arange(rows * top), side="right").astype(jnp.int32)
    listing = items.reshape(top, rows).T
    listing = listing[jax.random.permutation(jax.random.fold_in(own, 1), rows)]
    turn = jax.random.randint(jax.random.fold_in(own, 2), (rows, 1), 0, top)
    return jnp.take_along_axis(listing, (jnp.arange(top)[None, :] + turn) % top, axis=1)


def load_shares(count, total, bound, skew, full):
    portions = [(1 << 20) // math.isqrt(standing ** skew) + 1 for standing in range(1, count + 1)]
    largest = bound if full else min(bound, max(-(-total // count), total * portions[0] // sum(portions)))
    least = 1 if total - largest >= count - 1 else 0
    counts, rest = [largest] + [least] * (count - 1), total - largest - least * (count - 1)
    while rest > 0:
        candidates = [i for i in range(1, count) if counts[i] < largest] or [i for i in range(1, count) if counts[i] < bound]
        whole, budget = sum([portions[i] for i in candidates]), rest
        for i in candidates:
            addition = min(bound - counts[i], max(1, budget * portions[i] // whole), rest)
            counts[i] = counts[i] + addition
            rest = rest - addition
    return np.array(counts)


def centred(rng, extent, deviation, reach, pieces=(), kind=jnp.bfloat16):
    loudness = levels(rng, extent, pieces, -0.22, 0.18) if pieces else 1.0
    array = jax.random.normal(rng, extent, jnp.float32) * deviation * loudness
    return jnp.minimum(jnp.maximum(array, -reach), reach).astype(kind)


def setup_inputs(seed: int = 0, part: int = 0) -> dict:
    keys = jax.random.split(jax.random.key(seed), 7)
    part_keys = jax.random.split(jax.random.fold_in(keys[6], part), 7)
    h_rows = centred(part_keys[0], (TOKENS, TOP, FF), 1.0, 6.0, ((0, 16),))
    gates = jnp.clip(0.05 + 0.45 * jax.random.uniform(part_keys[1], (TOKENS, TOP), jnp.float32) ** levels(part_keys[1], (TOKENS, TOP), ((0, 16),), -0.2, 0.2), 0.05, 0.5)
    expert_ids_keys = jax.random.split(jax.random.fold_in(part_keys[2], 1), TOKENS // TOK_DEV)
    expert_ids_turns = jax.random.permutation(jax.random.fold_in(part_keys[2], 3), TOKENS // TOK_DEV)
    expert_ids = jax.vmap(lambda own, number: routed_block(jax.random.fold_in(part_keys[2], 2), own, number, TOK_DEV, EXPERTS, TOP, CAP, 1))(expert_ids_keys, expert_ids_turns).reshape((TOKENS, TOP))
    cotangent = centred(part_keys[3], (TOKENS, D), 0.2, 1.1953125, ((0, 16),))
    down_weight = centred(keys[4], (EXPERTS, FF, D), FF ** -0.5, 0.21875, ((0, 16),))
    swapped = with_ends((jax.random.randint(keys[5], (EXPERTS // 2,), 0, 2) < 1).astype(jnp.int32), jax.random.fold_in(keys[5], 1), 0, 1)
    return dict(h_rows=h_rows, gates=gates, expert_ids=expert_ids, cotangent=cotangent, down_weight=down_weight, swapped=swapped)


def reference(h_rows, gates, expert_ids, cotangent, down_weight, swapped):
    half_way = EXPERTS // 2
    experts = jnp.arange(EXPERTS, dtype=jnp.int32)
    table = ((experts + half_way * swapped[experts % half_way]) % EXPERTS).astype(jnp.int32)
    flat_ids = expert_ids.reshape(-1).astype(jnp.int32)
    onehot = (flat_ids[:, None] == experts[None, :]).astype(jnp.int32)
    ranks = jnp.sum((jnp.cumsum(onehot, axis=0) - onehot) * onehot, axis=1).astype(jnp.int32)
    slots = N_EXPERT * CAP
    rows_h = jnp.zeros((EXPERTS, slots, FF), h_rows.dtype).at[flat_ids, ranks].set(h_rows.reshape(-1, FF))
    scaled = (gates[:, :, None] * cotangent[:, None, :].astype(jnp.float32)).astype(jnp.bfloat16)
    rows_z = jnp.zeros((EXPERTS, slots, D), scaled.dtype).at[flat_ids, ranks].set(scaled.reshape(-1, D))

    def per_expert(items):
        block_h, block_z, slot = items
        weight = lax.dynamic_index_in_dim(down_weight, slot, 0, keepdims=False)
        out = jnp.dot(block_h, weight, preferred_element_type=jnp.float32).astype(jnp.bfloat16)
        grad = jnp.dot(block_h.T, block_z, preferred_element_type=jnp.float32).astype(jnp.bfloat16)
        back = jnp.dot(block_z, weight.T, preferred_element_type=jnp.float32).astype(jnp.bfloat16)
        return out, grad, back

    outs, grads, backs = lax.map(per_expert, (rows_h, rows_z, table))
    out_rows = outs[flat_ids, ranks].reshape(TOKENS, TOP, D)
    mixed = jnp.einsum("tk,tkd->td", gates, out_rows.astype(jnp.float32)).astype(jnp.bfloat16)
    gate_grad = jnp.einsum("td,tkd->tk", cotangent.astype(jnp.float32), out_rows.astype(jnp.float32))
    h_grad = backs[flat_ids, ranks].reshape(TOKENS, TOP, FF)
    weight_grad = grads[table]
    return (mixed, gate_grad, h_grad, weight_grad)
```

```python
import jax
import jax.numpy as jnp
from jax import lax
from jax.sharding import PartitionSpec as P


def place_rows(values, target, ranks, devices, capacity):
    buffer = jnp.zeros((devices, capacity, values.shape[-1]), values.dtype)
    return buffer.at[target, ranks].set(values)


def shards(h_rows, gates, expert_ids, cotangent, down_weight, swapped):
    devices = lax.axis_size("expert")
    half_way = devices // 2
    tokens_here, top_count, hidden = h_rows.shape
    width = cotangent.shape[1]
    capacity = min(tokens_here, 3 * tokens_here * top_count // (2 * devices))
    experts = jnp.arange(devices, dtype=jnp.int32)
    named = expert_ids.reshape(-1)
    weight = down_weight[0]
    table = (experts + half_way * swapped[experts % half_way]) % devices
    flat_ids = jnp.sum(jnp.where(named[:, None] == experts[None, :], table[None, :], 0), axis=1)
    onehot = (flat_ids[:, None] == experts[None, :]).astype(jnp.int32)
    ranks = jnp.sum((jnp.cumsum(onehot, axis=0) - onehot) * onehot, axis=1)
    send_h = place_rows(h_rows.reshape(-1, hidden), flat_ids, ranks, devices, capacity)
    received = lax.all_to_all(send_h, "expert", split_axis=0, concat_axis=0, tiled=True)
    result = jnp.einsum("sch,hd->scd", received, weight, preferred_element_type=jnp.float32)
    results = result.astype(jnp.bfloat16)
    returned = lax.all_to_all(results, "expert", split_axis=0, concat_axis=0, tiled=True)
    out_rows = returned[flat_ids, ranks].reshape(tokens_here, top_count, width)
    mixed = jnp.einsum("tk,tkd->td", gates, out_rows.astype(jnp.float32)).astype(jnp.bfloat16)
    gate_grad = jnp.einsum("td,tkd->tk", cotangent, out_rows, preferred_element_type=jnp.float32)
    scaled = (gates[:, :, None] * cotangent[:, None, :].astype(jnp.float32)).astype(jnp.bfloat16)
    send_z = place_rows(scaled.reshape(-1, width), flat_ids, ranks, devices, capacity)
    recv_z = lax.all_to_all(send_z, "expert", split_axis=0, concat_axis=0, tiled=True)
    flat_z = recv_z.reshape(-1, width)
    flat_h = received.reshape(-1, hidden)
    grad_sum = lax.dot_general(
        flat_h, flat_z, (((0,), (0,)), ((), ())), preferred_element_type=jnp.float32
    )
    back = lax.dot_general(
        flat_z, weight, (((1,), (1,)), ((), ())), preferred_element_type=jnp.float32
    ).astype(jnp.bfloat16)
    back_rows = lax.all_to_all(
        back.reshape(devices, capacity, hidden), "expert", split_axis=0, concat_axis=0, tiled=True
    )
    h_grad = back_rows[flat_ids, ranks].reshape(tokens_here, top_count, hidden)
    weight_grad = grad_sum.astype(jnp.bfloat16)[None]
    return (mixed, gate_grad, h_grad, weight_grad)


def solution(mesh):
    in_specs = (
        P(("groups", "expert"), None, None),
        P(("groups", "expert"), None),
        P(("groups", "expert"), None),
        P(("groups", "expert"), None),
        P("expert", None, None),
        P(),
    )
    out_specs = (
        P(("groups", "expert"), None),
        P(("groups", "expert"), None),
        P(("groups", "expert"), None, None),
        P(("groups", "expert"), None, None),
    )
    return jax.shard_map(shards, mesh=mesh, in_specs=in_specs, out_specs=out_specs, check_vma=False)
```

```python
import functools

import jax
import jax.numpy as jnp
from jax import lax
from jax.experimental import pallas as pl
from jax.experimental.pallas import tpu as pltpu
from jax.sharding import PartitionSpec as P

F32 = jnp.float32
BF16 = jnp.bfloat16
MIB = 1 << 20


def slots_of(ids, swapped, devices):
    half_way = devices // 2
    table = jnp.arange(devices, dtype=jnp.int32)
    table = (table + half_way * swapped[table % half_way]) % devices
    return jnp.sum(jnp.where(ids[..., None] == jnp.arange(devices, dtype=jnp.int32), table, 0), axis=-1)


def place_rows(values, target, ranks, devices, capacity):
    buffer = jnp.zeros((devices, capacity, values.shape[-1]), values.dtype)
    return buffer.at[target, ranks].set(values)


def sparse_shards(h_rows, gates, expert_ids, cotangent, down_weight, swapped):
    devices = lax.axis_size("expert")
    tokens_here, top_count, hidden = h_rows.shape
    width = cotangent.shape[1]
    capacity = min(tokens_here, 3 * tokens_here * top_count // (2 * devices))
    experts = jnp.arange(devices, dtype=jnp.int32)
    weight = down_weight[0]
    flat_ids = slots_of(expert_ids.reshape(-1), swapped, devices)
    onehot = (flat_ids[:, None] == experts[None, :]).astype(jnp.int32)
    ranks = jnp.sum((jnp.cumsum(onehot, axis=0) - onehot) * onehot, axis=1)
    send_h = place_rows(h_rows.reshape(-1, hidden), flat_ids, ranks, devices, capacity)
    received = lax.all_to_all(send_h, "expert", split_axis=0, concat_axis=0, tiled=True)
    result = jnp.einsum("sch,hd->scd", received, weight, preferred_element_type=F32)
    results = result.astype(BF16)
    returned = lax.all_to_all(results, "expert", split_axis=0, concat_axis=0, tiled=True)
    out_rows = returned[flat_ids, ranks].reshape(tokens_here, top_count, width)
    mixed = jnp.einsum("tk,tkd->td", gates, out_rows.astype(F32)).astype(BF16)
    gate_grad = jnp.einsum("td,tkd->tk", cotangent, out_rows, preferred_element_type=F32)
    scaled = (gates[:, :, None] * cotangent[:, None, :].astype(F32)).astype(BF16)
    send_z = place_rows(scaled.reshape(-1, width), flat_ids, ranks, devices, capacity)
    recv_z = lax.all_to_all(send_z, "expert", split_axis=0, concat_axis=0, tiled=True)
    flat_z = recv_z.reshape(-1, width)
    flat_h = received.reshape(-1, hidden)
    grad_sum = lax.dot_general(flat_h, flat_z, (((0,), (0,)), ((), ())), preferred_element_type=F32)
    back = lax.dot_general(flat_z, weight, (((1,), (1,)), ((), ())), preferred_element_type=F32).astype(BF16)
    back_rows = lax.all_to_all(
        back.reshape(devices, capacity, hidden), "expert", split_axis=0, concat_axis=0, tiled=True
    )
    h_grad = back_rows[flat_ids, ranks].reshape(tokens_here, top_count, hidden)
    return (mixed, gate_grad, h_grad, grad_sum.astype(BF16)[None])


def upper(size):
    rows = lax.broadcasted_iota(jnp.int32, (size, size), 0)
    columns = lax.broadcasted_iota(jnp.int32, (size, size), 1)
    return (rows < columns).astype(F32).astype(BF16)


def pack_kernel(devices, capacity, ids_ref, h_ref, place_ref, sent_ref, place_scratch):
    pairs = ids_ref.shape[1]
    rows = sent_ref.shape[0]

    @pl.when(pl.program_id(0) == 0)
    def _():
        before = jnp.zeros((devices, 1), F32)
        for tile in range(pairs // 128):
            ids = ids_ref[:, tile * 128:(tile + 1) * 128]
            named = lax.broadcasted_iota(jnp.int32, (devices, 128), 0) == ids
            ones = jnp.where(named, 1.0, 0.0)
            rank = jnp.dot(ones.astype(BF16), upper(128), preferred_element_type=F32) + before
            before = before + jnp.sum(ones, axis=1, keepdims=True)
            rank = jnp.sum(jnp.where(named, rank, 0.0), axis=0, keepdims=True)
            place_scratch[:, tile * 128:(tile + 1) * 128] = ids * capacity + rank.astype(jnp.int32)
        place_ref[...] = place_scratch[...]

    first = pl.program_id(0) * rows
    wanted = lax.broadcasted_iota(jnp.int32, (rows, pairs), 0) + first
    chosen = jnp.where(wanted == place_scratch[...], 1.0, 0.0).astype(BF16)
    sent_ref[...] = jnp.dot(chosen, h_ref[...], preferred_element_type=F32).astype(BF16)


def pack(ids, h_flat, devices, capacity, steps=4):
    pairs, hidden = h_flat.shape
    rows = devices * capacity // steps
    return pl.pallas_call(
        functools.partial(pack_kernel, devices, capacity),
        grid=(steps,),
        in_specs=[
            pl.BlockSpec((1, pairs), lambda i: (0, 0)),
            pl.BlockSpec((pairs, hidden), lambda i: (0, 0)),
        ],
        out_specs=[
            pl.BlockSpec((1, pairs), lambda i: (0, 0)),
            pl.BlockSpec((rows, hidden), lambda i: (i, 0)),
        ],
        out_shape=[
            jax.ShapeDtypeStruct((1, pairs), jnp.int32),
            jax.ShapeDtypeStruct((devices * capacity, hidden), BF16),
        ],
        scratch_shapes=[pltpu.VMEM((1, pairs), jnp.int32)],
        compiler_params=pltpu.CompilerParams(vmem_limit_bytes=48 * MIB),
        cost_estimate=pl.CostEstimate(
            flops=2 * devices * capacity * pairs * hidden, transcendentals=0,
            bytes_accessed=2 * hidden * (pairs + devices * capacity),
        ),
        name="pack",
    )(ids, h_flat)


def unpack_kernel(slots, place_ref, gate_ref, h_ref, back_ref, grad_ref, gate_grad_ref):
    rows = place_ref.shape[0]
    chosen = lax.broadcasted_iota(jnp.int32, (rows, slots), 1) == place_ref[...]
    grad = jnp.dot(jnp.where(chosen, 1.0, 0.0).astype(BF16), back_ref[...], preferred_element_type=F32)
    grad_ref[...] = grad.astype(BF16)
    gate_grad_ref[...] = jnp.sum(grad * h_ref[...].astype(F32), axis=1, keepdims=True) / gate_ref[...]


def unpack(place, gates, h_flat, back_rows, steps=4):
    pairs, hidden = h_flat.shape
    slots = back_rows.shape[0]
    rows = pairs // steps
    return pl.pallas_call(
        functools.partial(unpack_kernel, slots),
        grid=(steps,),
        in_specs=[
            pl.BlockSpec((rows, 1), lambda i: (i, 0)),
            pl.BlockSpec((rows, 1), lambda i: (i, 0)),
            pl.BlockSpec((rows, hidden), lambda i: (i, 0)),
            pl.BlockSpec((slots, hidden), lambda i: (0, 0)),
        ],
        out_specs=[
            pl.BlockSpec((rows, hidden), lambda i: (i, 0)),
            pl.BlockSpec((rows, 1), lambda i: (i, 0)),
        ],
        out_shape=[
            jax.ShapeDtypeStruct((pairs, hidden), BF16),
            jax.ShapeDtypeStruct((pairs, 1), F32),
        ],
        compiler_params=pltpu.CompilerParams(vmem_limit_bytes=48 * MIB),
        cost_estimate=pl.CostEstimate(
            flops=2 * slots * pairs * hidden, transcendentals=0,
            bytes_accessed=2 * hidden * (2 * pairs + slots),
        ),
        name="unpack",
    )(place, gates, h_flat, back_rows)


def route_kernel(devices, top, here_ref, routing_ref, rank_ref, gate_ref):
    mine = here_ref[0].astype(F32)
    marks, picked = [], []
    for source in range(devices):
        ids = routing_ref[2 * top * source:2 * top * source + top, :]
        gates = routing_ref[2 * top * source + top:2 * top * (source + 1), :]
        named = ids == mine
        marks.append(jnp.sum(jnp.where(named, 1.0, 0.0), axis=0, keepdims=True))
        picked.append(jnp.sum(jnp.where(named, gates, 0.0), axis=0, keepdims=True))
    mark = jnp.concatenate(marks, axis=0)
    rank = jnp.dot(mark.astype(BF16), upper(mark.shape[1]), preferred_element_type=F32)
    rank_ref[...] = jnp.where(mark > 0, rank, -1.0).astype(jnp.int32)
    gate_ref[...] = jnp.concatenate(picked, axis=0)


def route(here, routing, devices, top):
    tokens = routing.shape[1]
    return pl.pallas_call(
        functools.partial(route_kernel, devices, top),
        in_specs=[pl.BlockSpec(memory_space=pltpu.SMEM), pl.BlockSpec(memory_space=pltpu.VMEM)],
        out_specs=[pl.BlockSpec(memory_space=pltpu.VMEM)] * 2,
        out_shape=[
            jax.ShapeDtypeStruct((devices, tokens), jnp.int32),
            jax.ShapeDtypeStruct((devices, tokens), F32),
        ],
        name="route",
    )(here, routing)


def picks(rank_ref, gate_ref, source, capacity):
    rank = rank_ref[pl.ds(source, 1), :]
    chosen = lax.broadcasted_iota(jnp.int32, (capacity, rank.shape[1]), 0) == rank
    gate = jnp.sum(jnp.where(chosen, gate_ref[pl.ds(source, 1), :], 0.0), axis=1, keepdims=True)
    return jnp.where(chosen, 1.0, 0.0).astype(BF16), gate


def back_kernel(capacity, rank_ref, gate_ref, cot_ref, weight_ref, z_ref, back_ref):
    each = cot_ref.shape[0]
    for j in range(each):
        chosen, gate = picks(rank_ref, gate_ref, pl.program_id(0) * each + j, capacity)
        rows = jnp.dot(chosen, cot_ref[j], preferred_element_type=F32)
        z_ref[j * capacity:(j + 1) * capacity, :] = (rows * gate).astype(BF16)
    back_ref[...] = jnp.dot(z_ref[...], weight_ref[...], preferred_element_type=F32).astype(BF16)


def backward_rows(rank, gate, cotangents, weight_t, capacity, each=4):
    devices, tokens, width = cotangents.shape
    hidden = weight_t.shape[1]
    rows = each * capacity
    return pl.pallas_call(
        functools.partial(back_kernel, capacity),
        grid=(devices // each,),
        in_specs=[
            pl.BlockSpec((devices, tokens), lambda i: (0, 0)),
            pl.BlockSpec((devices, tokens), lambda i: (0, 0)),
            pl.BlockSpec((each, tokens, width), lambda i: (i, 0, 0)),
            pl.BlockSpec((width, hidden), lambda i: (0, 0)),
        ],
        out_specs=[
            pl.BlockSpec((rows, width), lambda i: (i, 0)),
            pl.BlockSpec((rows, hidden), lambda i: (i, 0)),
        ],
        out_shape=[
            jax.ShapeDtypeStruct((devices * capacity, width), BF16),
            jax.ShapeDtypeStruct((devices * capacity, hidden), BF16),
        ],
        compiler_params=pltpu.CompilerParams(vmem_limit_bytes=48 * MIB),
        cost_estimate=pl.CostEstimate(
            flops=2 * devices * capacity * width * (hidden + tokens), transcendentals=0,
            bytes_accessed=2 * devices * (tokens * width + capacity * (width + hidden)) + 2 * width * hidden,
        ),
        name="backward_rows",
    )(rank, gate, cotangents, weight_t)


def forward_kernel(capacity, rank_ref, gate_ref, h_ref, weight_ref, part_ref):
    each = part_ref.shape[0]
    out = jnp.dot(h_ref[...], weight_ref[...], preferred_element_type=F32)
    out = out.astype(BF16).astype(F32)
    for j in range(each):
        chosen, gate = picks(rank_ref, gate_ref, pl.program_id(0) * each + j, capacity)
        rows = (out[j * capacity:(j + 1) * capacity, :] * gate).astype(BF16)
        part = lax.dot_general(chosen, rows, (((0,), (0,)), ((), ())), preferred_element_type=F32)
        part_ref[j] = part.astype(BF16)


def forward_parts(rank, gate, rows_h, weight, capacity, each=8, columns=512):
    devices, tokens = rank.shape
    hidden, width = weight.shape
    rows = each * capacity
    return pl.pallas_call(
        functools.partial(forward_kernel, capacity),
        grid=(devices // each, width // columns),
        in_specs=[
            pl.BlockSpec((devices, tokens), lambda i, j: (0, 0)),
            pl.BlockSpec((devices, tokens), lambda i, j: (0, 0)),
            pl.BlockSpec((rows, hidden), lambda i, j: (i, 0)),
            pl.BlockSpec((hidden, columns), lambda i, j: (0, j)),
        ],
        out_specs=pl.BlockSpec((each, tokens, columns), lambda i, j: (i, 0, j)),
        out_shape=jax.ShapeDtypeStruct((devices, tokens, width), BF16),
        compiler_params=pltpu.CompilerParams(vmem_limit_bytes=48 * MIB),
        cost_estimate=pl.CostEstimate(
            flops=2 * devices * capacity * width * (hidden + tokens), transcendentals=0,
            bytes_accessed=2 * devices * (tokens * width + capacity * hidden) + 2 * width * hidden,
        ),
        name="forward_parts",
    )(rank, gate, rows_h, weight)


def dense_shards(h_rows, gates, expert_ids, cotangent, down_weight, swapped):
    devices = lax.axis_size("expert")
    here = lax.axis_index("expert")
    tokens, top, hidden = h_rows.shape
    width = cotangent.shape[1]
    capacity = min(tokens, 3 * tokens * top // (2 * devices))
    weight = down_weight[0]
    slot_ids = slots_of(expert_ids, swapped, devices)
    h_flat = h_rows.reshape(-1, hidden)

    cotangents = lax.all_gather(cotangent, "expert", axis=0, tiled=False)
    routing = jnp.concatenate([slot_ids.T.astype(F32), gates.T], axis=0)
    routing = lax.all_gather(routing, "expert", axis=0, tiled=True)
    place, send_h = pack(slot_ids.reshape(1, -1), h_flat, devices, capacity)
    rows_h = lax.all_to_all(
        send_h.reshape(devices, capacity, hidden), "expert", split_axis=0, concat_axis=0, tiled=True
    ).reshape(-1, hidden)
    rank, gate = route(here.reshape(1), routing, devices, top)

    z_rows, back = backward_rows(rank, gate, cotangents, weight.T, capacity)
    back_rows = lax.all_to_all(
        back.reshape(devices, capacity, hidden), "expert", split_axis=0, concat_axis=0, tiled=True
    ).reshape(-1, hidden)
    parts = forward_parts(rank, gate, rows_h, weight, capacity)
    mixed = lax.psum_scatter(parts.reshape(-1, width), "expert", scatter_dimension=0, tiled=True)
    grad_sum = lax.dot_general(rows_h, z_rows, (((0,), (0,)), ((), ())), preferred_element_type=F32)
    h_grad, gate_grad = unpack(place.reshape(-1, 1), gates.reshape(-1, 1), h_flat, back_rows)
    return (
        mixed,
        gate_grad.reshape(tokens, top),
        h_grad.reshape(tokens, top, hidden),
        grad_sum.astype(BF16)[None],
    )


def shards(h_rows, *rest):
    devices = lax.axis_size("expert")
    dense = devices <= 2 * h_rows.shape[1]
    return (dense_shards if dense else sparse_shards)(h_rows, *rest)


def solution(mesh):
    in_specs = (
        P(("groups", "expert"), None, None),
        P(("groups", "expert"), None),
        P(("groups", "expert"), None),
        P(("groups", "expert"), None),
        P("expert", None, None),
        P(),
    )
    out_specs = (
        P(("groups", "expert"), None),
        P(("groups", "expert"), None),
        P(("groups", "expert"), None, None),
        P(("groups", "expert"), None, None),
    )
    return jax.shard_map(shards, mesh=mesh, in_specs=in_specs, out_specs=out_specs, check_vma=False)
```

```python
import functools

import jax
import jax.numpy as jnp
from jax import lax
from jax.experimental import pallas as pl
from jax.experimental.pallas import tpu as pltpu
from jax.sharding import PartitionSpec as P

F32 = jnp.float32
BF16 = jnp.bfloat16
MIB = 1 << 20


def slots_of(ids, swapped, devices):
    half_way = devices // 2
    table = jnp.arange(devices, dtype=jnp.int32)
    table = (table + half_way * swapped[table % half_way]) % devices
    return jnp.sum(jnp.where(ids[..., None] == jnp.arange(devices, dtype=jnp.int32), table, 0), axis=-1)


def place_rows(values, target, ranks, devices, capacity):
    buffer = jnp.zeros((devices, capacity, values.shape[-1]), values.dtype)
    return buffer.at[target, ranks].set(values)


def sparse_shards(h_rows, gates, expert_ids, cotangent, down_weight, swapped):
    devices = lax.axis_size("expert")
    tokens_here, top_count, hidden = h_rows.shape
    width = cotangent.shape[1]
    capacity = min(tokens_here, 3 * tokens_here * top_count // (2 * devices))
    experts = jnp.arange(devices, dtype=jnp.int32)
    weight = down_weight[0]
    flat_ids = slots_of(expert_ids.reshape(-1), swapped, devices)
    onehot = (flat_ids[:, None] == experts[None, :]).astype(jnp.int32)
    ranks = jnp.sum((jnp.cumsum(onehot, axis=0) - onehot) * onehot, axis=1)
    send_h = place_rows(h_rows.reshape(-1, hidden), flat_ids, ranks, devices, capacity)
    received = lax.all_to_all(send_h, "expert", split_axis=0, concat_axis=0, tiled=True)
    result = jnp.einsum("sch,hd->scd", received, weight, preferred_element_type=F32)
    results = result.astype(BF16)
    returned = lax.all_to_all(results, "expert", split_axis=0, concat_axis=0, tiled=True)
    out_rows = returned[flat_ids, ranks].reshape(tokens_here, top_count, width)
    mixed = jnp.einsum("tk,tkd->td", gates, out_rows.astype(F32)).astype(BF16)
    gate_grad = jnp.einsum("td,tkd->tk", cotangent, out_rows, preferred_element_type=F32)
    scaled = (gates[:, :, None] * cotangent[:, None, :].astype(F32)).astype(BF16)
    send_z = place_rows(scaled.reshape(-1, width), flat_ids, ranks, devices, capacity)
    recv_z = lax.all_to_all(send_z, "expert", split_axis=0, concat_axis=0, tiled=True)
    flat_z = recv_z.reshape(-1, width)
    flat_h = received.reshape(-1, hidden)
    grad_sum = lax.dot_general(flat_h, flat_z, (((0,), (0,)), ((), ())), preferred_element_type=F32)
    back = lax.dot_general(flat_z, weight, (((1,), (1,)), ((), ())), preferred_element_type=F32).astype(BF16)
    back_rows = lax.all_to_all(
        back.reshape(devices, capacity, hidden), "expert", split_axis=0, concat_axis=0, tiled=True
    )
    h_grad = back_rows[flat_ids, ranks].reshape(tokens_here, top_count, hidden)
    return (mixed, gate_grad, h_grad, grad_sum.astype(BF16)[None])


def upper(size):
    rows = lax.broadcasted_iota(jnp.int32, (size, size), 0)
    columns = lax.broadcasted_iota(jnp.int32, (size, size), 1)
    return (rows < columns).astype(F32).astype(BF16)


def pack_kernel(devices, capacity, ids_ref, h_ref, place_ref, sent_ref, place_scratch):
    pairs = ids_ref.shape[1]
    rows = sent_ref.shape[0]

    @pl.when(pl.program_id(0) == 0)
    def _():
        before = jnp.zeros((devices, 1), F32)
        for tile in range(pairs // 128):
            ids = ids_ref[:, tile * 128:(tile + 1) * 128]
            named = lax.broadcasted_iota(jnp.int32, (devices, 128), 0) == ids
            ones = jnp.where(named, 1.0, 0.0)
            rank = jnp.dot(ones.astype(BF16), upper(128), preferred_element_type=F32) + before
            before = before + jnp.sum(ones, axis=1, keepdims=True)
            rank = jnp.sum(jnp.where(named, rank, 0.0), axis=0, keepdims=True)
            place_scratch[:, tile * 128:(tile + 1) * 128] = ids * capacity + rank.astype(jnp.int32)
        place_ref[...] = place_scratch[...]

    first = pl.program_id(0) * rows
    wanted = lax.broadcasted_iota(jnp.int32, (rows, pairs), 0) + first
    chosen = jnp.where(wanted == place_scratch[...], 1.0, 0.0).astype(BF16)
    sent_ref[...] = jnp.dot(chosen, h_ref[...], preferred_element_type=F32).astype(BF16)


def pack(ids, h_flat, devices, capacity, steps=4):
    pairs, hidden = h_flat.shape
    rows = devices * capacity // steps
    return pl.pallas_call(
        functools.partial(pack_kernel, devices, capacity),
        grid=(steps,),
        in_specs=[
            pl.BlockSpec((1, pairs), lambda i: (0, 0)),
            pl.BlockSpec((pairs, hidden), lambda i: (0, 0)),
        ],
        out_specs=[
            pl.BlockSpec((1, pairs), lambda i: (0, 0)),
            pl.BlockSpec((rows, hidden), lambda i: (i, 0)),
        ],
        out_shape=[
            jax.ShapeDtypeStruct((1, pairs), jnp.int32),
            jax.ShapeDtypeStruct((devices * capacity, hidden), BF16),
        ],
        scratch_shapes=[pltpu.VMEM((1, pairs), jnp.int32)],
        compiler_params=pltpu.CompilerParams(vmem_limit_bytes=48 * MIB),
        cost_estimate=pl.CostEstimate(
            flops=2 * devices * capacity * pairs * hidden, transcendentals=0,
            bytes_accessed=2 * hidden * (pairs + devices * capacity),
        ),
        name="pack",
    )(ids, h_flat)


def unpack_kernel(slots, place_ref, gate_ref, h_ref, back_ref, grad_ref, gate_grad_ref):
    rows = place_ref.shape[0]
    chosen = lax.broadcasted_iota(jnp.int32, (rows, slots), 1) == place_ref[...]
    grad = jnp.dot(jnp.where(chosen, 1.0, 0.0).astype(BF16), back_ref[...], preferred_element_type=F32)
    grad_ref[...] = grad.astype(BF16)
    gate_grad_ref[...] = jnp.sum(grad * h_ref[...].astype(F32), axis=1, keepdims=True) / gate_ref[...]


def unpack(place, gates, h_flat, back_rows, steps=4):
    pairs, hidden = h_flat.shape
    slots = back_rows.shape[0]
    rows = pairs // steps
    return pl.pallas_call(
        functools.partial(unpack_kernel, slots),
        grid=(steps,),
        in_specs=[
            pl.BlockSpec((rows, 1), lambda i: (i, 0)),
            pl.BlockSpec((rows, 1), lambda i: (i, 0)),
            pl.BlockSpec((rows, hidden), lambda i: (i, 0)),
            pl.BlockSpec((slots, hidden), lambda i: (0, 0)),
        ],
        out_specs=[
            pl.BlockSpec((rows, hidden), lambda i: (i, 0)),
            pl.BlockSpec((rows, 1), lambda i: (i, 0)),
        ],
        out_shape=[
            jax.ShapeDtypeStruct((pairs, hidden), BF16),
            jax.ShapeDtypeStruct((pairs, 1), F32),
        ],
        compiler_params=pltpu.CompilerParams(vmem_limit_bytes=48 * MIB),
        cost_estimate=pl.CostEstimate(
            flops=2 * slots * pairs * hidden, transcendentals=0,
            bytes_accessed=2 * hidden * (2 * pairs + slots),
        ),
        name="unpack",
    )(place, gates, h_flat, back_rows)


def line_slots(position):
    near = jnp.minimum(position, 3 - position)
    turned = (near, near + 1, near + 2, 3 - 3 * near)
    return [jnp.where(position < 2, slot, 3 - slot) for slot in turned]


def route_kernel(devices, top, here_ref, routing_ref, rank_ref, gate_ref):
    for side in range(2):
        mine = (here_ref[0] ^ side).astype(F32)
        marks, picked = [], []
        for source in range(devices):
            ids = routing_ref[source, :top, :]
            gates = routing_ref[source, top:, :]
            named = ids == mine
            marks.append(jnp.sum(jnp.where(named, 1.0, 0.0), axis=0, keepdims=True))
            picked.append(jnp.sum(jnp.where(named, gates, 0.0), axis=0, keepdims=True))
        mark = jnp.concatenate(marks, axis=0)
        rank = jnp.dot(mark.astype(BF16), upper(mark.shape[1]), preferred_element_type=F32)
        rank_ref[side] = jnp.where(mark > 0, rank, -1.0).astype(jnp.int32)
        gate_ref[side] = jnp.concatenate(picked, axis=0)


def route(here, routing, top):
    devices, _, tokens = routing.shape
    return pl.pallas_call(
        functools.partial(route_kernel, devices, top),
        in_specs=[pl.BlockSpec(memory_space=pltpu.SMEM), pl.BlockSpec(memory_space=pltpu.VMEM)],
        out_specs=[pl.BlockSpec(memory_space=pltpu.VMEM)] * 2,
        out_shape=[
            jax.ShapeDtypeStruct((2, devices, tokens), jnp.int32),
            jax.ShapeDtypeStruct((2, devices, tokens), F32),
        ],
        cost_estimate=pl.CostEstimate(flops=1 << 21, transcendentals=0, bytes_accessed=1 << 19),
        name="route",
    )(here, routing)


def chosen_rows(rank_ref, side, source, capacity):
    rank = rank_ref[side, pl.ds(source, 1), :]
    return lax.broadcasted_iota(jnp.int32, (capacity, rank.shape[1]), 0) == rank


def gate_column(gate_ref, chosen, side, source):
    return jnp.sum(jnp.where(chosen, gate_ref[side, pl.ds(source, 1), :], 0.0), axis=1, keepdims=True)


def one_hot(chosen):
    return jnp.where(chosen, 1.0, 0.0).astype(BF16)


def lane_sources(here, slots, lane):
    line, across = here // 4, (here // 2) % 2
    places = line_slots(line)
    return [places[slot] * 4 + (across ^ turn) * 2 + lane for slot in slots for turn in range(2)]


def place_out(pieces, sem):
    copies = [pltpu.make_async_copy(source, target, sem.at[i]) for i, (source, target) in enumerate(pieces)]
    for copy in copies:
        copy.start()
    return copies


def scale_kernel(capacity, slots, held, here_ref, rank_ref, gate_ref, weight_ref, *refs):
    count = 2 * len(slots)
    blocks, refs = refs[:count], refs[count + held:]
    z_ref, back_ref, sibling_ref, z_scratch, back_scratch, z_sem, back_sem = refs
    sources = lane_sources(here_ref[0], slots, here_ref[0] % 2)
    for i, source in enumerate(sources):
        chosen = [chosen_rows(rank_ref, side, source, capacity) for side in range(2)]
        gates = [gate_column(gate_ref, chosen[side], side, source) for side in range(2)]
        both = jnp.concatenate([one_hot(chosen[0]), one_hot(chosen[1])], axis=0)
        rows = jnp.dot(both, blocks[i][...], preferred_element_type=F32)
        z_scratch[i] = (rows[:capacity] * gates[0]).astype(BF16)
        sibling_ref[i] = (rows[capacity:] * gates[1]).astype(BF16)
    copies = place_out([(z_scratch.at[i], z_ref.at[source]) for i, source in enumerate(sources)], z_sem)
    flat = z_scratch[...].reshape(count * capacity, z_scratch.shape[2])
    back = lax.dot_general(flat, weight_ref[...], (((1,), (1,)), ((), ())), preferred_element_type=F32)
    back_scratch[...] = back.astype(BF16).reshape(back_scratch.shape)
    copies += place_out([(back_scratch.at[i], back_ref.at[source]) for i, source in enumerate(sources)], back_sem)
    for copy in copies:
        copy.wait()


def scaled_rows(here, rank, gate, weight, blocks, slots, capacity, buffers):
    devices = rank.shape[1]
    hidden, width = weight.shape
    count = len(blocks)
    tokens = blocks[0].shape[0]
    vmem, anywhere = pl.BlockSpec(memory_space=pltpu.VMEM), pl.BlockSpec(memory_space=pl.ANY)
    return pl.pallas_call(
        functools.partial(scale_kernel, capacity, slots, len(buffers)),
        in_specs=[pl.BlockSpec(memory_space=pltpu.SMEM)] + [vmem] * (3 + count) + [anywhere] * len(buffers),
        out_specs=[anywhere, anywhere, vmem],
        out_shape=[
            jax.ShapeDtypeStruct((devices, capacity, width), BF16),
            jax.ShapeDtypeStruct((devices, capacity, hidden), BF16),
            jax.ShapeDtypeStruct((count, capacity, width), BF16),
        ],
        scratch_shapes=[
            pltpu.VMEM((count, capacity, width), BF16),
            pltpu.VMEM((count, capacity, hidden), BF16),
            pltpu.SemaphoreType.DMA((count,)),
            pltpu.SemaphoreType.DMA((count,)),
        ],
        input_output_aliases={4 + count + i: i for i in range(len(buffers))},
        compiler_params=pltpu.CompilerParams(vmem_limit_bytes=40 * MIB),
        cost_estimate=pl.CostEstimate(
            flops=2 * count * capacity * width * (hidden + 2 * tokens), transcendentals=0,
            bytes_accessed=2 * count * (tokens * width + capacity * (2 * width + hidden)) + 2 * width * hidden,
        ),
        name="scaled_rows",
    )(here, rank, gate, weight, *blocks, *buffers)


def sibling_kernel(capacity, slots, here_ref, weight_ref, rows_ref, _z, _back, z_ref, back_ref, back_scratch, z_sem, back_sem):
    count = 2 * len(slots)
    sources = lane_sources(here_ref[0], slots, 1 - here_ref[0] % 2)
    copies = place_out([(rows_ref.at[i], z_ref.at[source]) for i, source in enumerate(sources)], z_sem)
    flat = rows_ref[...].reshape(count * capacity, rows_ref.shape[2])
    back = lax.dot_general(flat, weight_ref[...], (((1,), (1,)), ((), ())), preferred_element_type=F32)
    back_scratch[...] = back.astype(BF16).reshape(back_scratch.shape)
    copies += place_out([(back_scratch.at[i], back_ref.at[source]) for i, source in enumerate(sources)], back_sem)
    for copy in copies:
        copy.wait()


def sibling_rows(here, weight, rows, slots, z_rows, back):
    count, capacity, width = rows.shape
    hidden = weight.shape[0]
    vmem, anywhere = pl.BlockSpec(memory_space=pltpu.VMEM), pl.BlockSpec(memory_space=pl.ANY)
    return pl.pallas_call(
        functools.partial(sibling_kernel, capacity, slots),
        in_specs=[pl.BlockSpec(memory_space=pltpu.SMEM), vmem, vmem, anywhere, anywhere],
        out_specs=[anywhere, anywhere],
        out_shape=[jax.ShapeDtypeStruct(z_rows.shape, BF16), jax.ShapeDtypeStruct(back.shape, BF16)],
        scratch_shapes=[
            pltpu.VMEM((count, capacity, hidden), BF16),
            pltpu.SemaphoreType.DMA((count,)),
            pltpu.SemaphoreType.DMA((count,)),
        ],
        input_output_aliases={3: 0, 4: 1},
        compiler_params=pltpu.CompilerParams(vmem_limit_bytes=40 * MIB),
        cost_estimate=pl.CostEstimate(
            flops=2 * count * capacity * width * hidden, transcendentals=0,
            bytes_accessed=2 * count * capacity * (2 * width + hidden) + 2 * width * hidden,
        ),
        name="sibling_rows",
    )(here, weight, rows, z_rows, back)


def forward_kernel(capacity, turn, here_ref, rank_ref, gate_ref, h_ref, weight_ref, out_ref):
    each = out_ref.shape[0]
    lane = (here_ref[0] % 2) ^ turn
    flat = h_ref[...].reshape(each * capacity, h_ref.shape[3])
    out = jnp.dot(flat, weight_ref[...], preferred_element_type=F32).astype(BF16).astype(F32)
    for j in range(each):
        source = (pl.program_id(0) * each + j) * 2 + lane
        gate = gate_column(gate_ref, chosen_rows(rank_ref, 0, source, capacity), 0, source)
        out_ref[j] = (out[j * capacity:(j + 1) * capacity, :] * gate).astype(BF16)


def forward_rows(here, rank, gate, rows_h, weight, turn, each=4):
    devices, capacity, hidden = rows_h.shape
    width = weight.shape[1]
    whole = pl.BlockSpec(rank.shape, lambda i, here: (0, 0, 0))
    return pl.pallas_call(
        functools.partial(forward_kernel, capacity, turn),
        grid_spec=pltpu.PrefetchScalarGridSpec(
            num_scalar_prefetch=1,
            grid=(devices // 2 // each,),
            in_specs=[
                whole,
                whole,
                pl.BlockSpec((each, 1, capacity, hidden), lambda i, here: (i, (here[0] % 2) ^ turn, 0, 0)),
                pl.BlockSpec((hidden, width), lambda i, here: (0, 0)),
            ],
            out_specs=pl.BlockSpec((each, capacity, width), lambda i, here: (i, 0, 0)),
        ),
        out_shape=jax.ShapeDtypeStruct((devices // 2, capacity, width), BF16),
        compiler_params=pltpu.CompilerParams(vmem_limit_bytes=40 * MIB),
        cost_estimate=pl.CostEstimate(
            flops=devices * capacity * width * hidden, transcendentals=0,
            bytes_accessed=devices * capacity * (width + hidden) + 2 * width * hidden,
        ),
        name="forward_rows",
    )(here, rank, gate, rows_h.reshape(devices // 2, 2, capacity, hidden), weight)


ORDER = (3, 2, 1, 0)


def sum_kernel(capacity, turn, here_ref, rank_ref, own_ref, other_ref, *part_refs):
    for step, slot in enumerate(ORDER):

        @pl.when(pl.program_id(0) == step)
        def _():
            source = lane_sources(here_ref[0], (slot,), here_ref[0] % 2)[turn]
            both = [one_hot(chosen_rows(rank_ref, side, source, capacity)) for side in range(2)]
            rows = jnp.concatenate([own_ref[0], other_ref[0]], axis=0)
            part = lax.dot_general(
                jnp.concatenate(both, axis=0), rows, (((0,), (0,)), ((), ())), preferred_element_type=F32
            )
            part_refs[step][...] = part.astype(BF16)


def summed(here, rank, own, other, turn):
    _, capacity, width = own.shape
    tokens = rank.shape[2]

    def block(i, here):
        place = jnp.int32(0)
        for step, slot in enumerate(ORDER):
            place = jnp.where(i == step, lane_sources(here[0], (slot,), 0)[turn] // 2, place)
        return (place, 0, 0)

    return pl.pallas_call(
        functools.partial(sum_kernel, capacity, turn),
        grid_spec=pltpu.PrefetchScalarGridSpec(
            num_scalar_prefetch=1,
            grid=(len(ORDER),),
            in_specs=[
                pl.BlockSpec(rank.shape, lambda i, here: (0, 0, 0)),
                pl.BlockSpec((1, capacity, width), block),
                pl.BlockSpec((1, capacity, width), block),
            ],
            out_specs=[pl.BlockSpec((tokens, width), lambda i, here: (0, 0))] * len(ORDER),
        ),
        out_shape=[jax.ShapeDtypeStruct((tokens, width), BF16)] * len(ORDER),
        compiler_params=pltpu.CompilerParams(vmem_limit_bytes=40 * MIB),
        cost_estimate=pl.CostEstimate(
            flops=16 * tokens * capacity * width, transcendentals=0,
            bytes_accessed=8 * width * (tokens + 2 * capacity),
        ),
        name="summed",
    )(here, rank, own, other)


def added(*values):
    total = values[0].astype(F32)
    for value in values[1:]:
        total = total + value.astype(F32)
    return total.astype(BF16)


def passed(pairs, value):
    return lax.ppermute(value, "expert", [(a * 4 + lane, b * 4 + lane) for a, b in pairs for lane in range(4)])


def swapped_with(value, bit):
    devices = lax.axis_size("expert")
    return lax.ppermute(value, "expert", [(i, i ^ bit) for i in range(devices)])


OUTER, INNER, ENDS = ((0, 1), (3, 2)), ((1, 2), (2, 1)), ((1, 0), (2, 3))


def dense_shards(h_rows, gates, expert_ids, cotangent, down_weight, swapped):
    devices = lax.axis_size("expert")
    here = lax.axis_index("expert").reshape(1)
    tokens, top, hidden = h_rows.shape
    capacity = min(tokens, 3 * tokens * top // (2 * devices))
    weight = down_weight[0]
    slot_ids = slots_of(expert_ids, swapped, devices)
    h_flat = h_rows.reshape(-1, hidden)

    routing = jnp.concatenate([slot_ids.T.astype(F32), gates.T], axis=0)
    routing = jnp.broadcast_to(routing, (devices,) + routing.shape)
    routing = lax.all_to_all(routing, "expert", split_axis=0, concat_axis=0, tiled=True)
    rank, gate = route(here, routing, top)

    own = cotangent
    from_end = passed(OUTER, own)
    from_inner = passed(INNER, own)
    near = added(from_inner, passed(ENDS, own))
    own_y = swapped_with(own, 2)
    from_far = passed(INNER, from_end)
    middle = added(from_far, passed(ENDS, from_inner))
    near_y = swapped_with(near, 2)
    last = added(from_end, passed(ENDS, from_far))
    middle_y = swapped_with(middle, 2)
    last_y = swapped_with(last, 2)

    place, send_h = pack(slot_ids.reshape(1, -1), h_flat, devices, capacity)
    rows_h = lax.all_to_all(
        send_h.reshape(devices, capacity, hidden), "expert", split_axis=0, concat_axis=0, tiled=True
    )

    z_rows, back, sibling = scaled_rows(here, rank, gate, weight, [own, own_y, near, near_y], (0, 1), capacity, [])
    sibling = swapped_with(sibling, 1)
    z_rows, back, sibling_last = scaled_rows(
        here, rank, gate, weight, [middle, middle_y, last, last_y], (2, 3), capacity, [z_rows, back]
    )
    sibling_last = swapped_with(sibling_last, 1)
    z_rows, back = sibling_rows(here, weight, sibling, (0, 1), z_rows, back)
    z_rows, back = sibling_rows(here, weight, sibling_last, (2, 3), z_rows, back)
    back_rows = lax.all_to_all(back, "expert", split_axis=0, concat_axis=0, tiled=True).reshape(-1, hidden)

    other = swapped_with(forward_rows(here, rank, gate, rows_h, weight, 1), 1)
    mine = forward_rows(here, rank, gate, rows_h, weight, 0)
    across = [swapped_with(part, 2) for part in summed(here, rank, mine, other, 1)]
    beside = summed(here, rank, mine, other, 0)
    far, mid, close, kept = zip(beside, across)
    outer1 = passed(OUTER, added(*far))
    mid = added(*mid, outer1)
    outer2, inner2 = passed(OUTER, mid), passed(INNER, mid)
    close = added(*close, outer2)
    outer3, inner3 = passed(OUTER, close), passed(INNER, close)
    ends3 = passed(ENDS, added(*far, inner2))
    mixed = added(*kept, outer3, inner3, ends3)

    grad_sum = lax.dot_general(
        rows_h.reshape(-1, hidden), z_rows.reshape(devices * capacity, -1), (((0,), (0,)), ((), ())),
        preferred_element_type=F32,
    )
    h_grad, gate_grad = unpack(place.reshape(-1, 1), gates.reshape(-1, 1), h_flat, back_rows)
    return (
        mixed,
        gate_grad.reshape(tokens, top),
        h_grad.reshape(tokens, top, hidden),
        grad_sum.astype(BF16)[None],
    )


def shards(h_rows, *rest):
    devices = lax.axis_size("expert")
    dense = devices == 16 and devices <= 2 * h_rows.shape[1]
    return (dense_shards if dense else sparse_shards)(h_rows, *rest)


def solution(mesh):
    in_specs = (
        P(("groups", "expert"), None, None),
        P(("groups", "expert"), None),
        P(("groups", "expert"), None),
        P(("groups", "expert"), None),
        P("expert", None, None),
        P(),
    )
    out_specs = (
        P(("groups", "expert"), None),
        P(("groups", "expert"), None),
        P(("groups", "expert"), None, None),
        P(("groups", "expert"), None, None),
    )
    return jax.shard_map(shards, mesh=mesh, in_specs=in_specs, out_specs=out_specs, check_vma=False)
```

```python
import functools

import jax
import jax.numpy as jnp
from jax import lax
from jax.experimental import pallas as pl
from jax.experimental.pallas import tpu as pltpu
from jax.sharding import PartitionSpec as P

F32 = jnp.float32
BF16 = jnp.bfloat16
MIB = 1 << 20


def slots_of(ids, swapped, devices):
    half_way = devices // 2
    table = jnp.arange(devices, dtype=jnp.int32)
    table = (table + half_way * swapped[table % half_way]) % devices
    return jnp.sum(jnp.where(ids[..., None] == jnp.arange(devices, dtype=jnp.int32), table, 0), axis=-1)


def place_rows(values, target, ranks, devices, capacity):
    buffer = jnp.zeros((devices, capacity, values.shape[-1]), values.dtype)
    return buffer.at[target, ranks].set(values)


def sparse_shards(h_rows, gates, expert_ids, cotangent, down_weight, swapped):
    devices = lax.axis_size("expert")
    tokens_here, top_count, hidden = h_rows.shape
    width = cotangent.shape[1]
    capacity = min(tokens_here, 3 * tokens_here * top_count // (2 * devices))
    experts = jnp.arange(devices, dtype=jnp.int32)
    weight = down_weight[0]
    flat_ids = slots_of(expert_ids.reshape(-1), swapped, devices)
    onehot = (flat_ids[:, None] == experts[None, :]).astype(jnp.int32)
    ranks = jnp.sum((jnp.cumsum(onehot, axis=0) - onehot) * onehot, axis=1)
    send_h = place_rows(h_rows.reshape(-1, hidden), flat_ids, ranks, devices, capacity)
    received = lax.all_to_all(send_h, "expert", split_axis=0, concat_axis=0, tiled=True)
    result = jnp.einsum("sch,hd->scd", received, weight, preferred_element_type=F32)
    results = result.astype(BF16)
    returned = lax.all_to_all(results, "expert", split_axis=0, concat_axis=0, tiled=True)
    out_rows = returned[flat_ids, ranks].reshape(tokens_here, top_count, width)
    mixed = jnp.einsum("tk,tkd->td", gates, out_rows.astype(F32)).astype(BF16)
    gate_grad = jnp.einsum("td,tkd->tk", cotangent, out_rows, preferred_element_type=F32)
    scaled = (gates[:, :, None] * cotangent[:, None, :].astype(F32)).astype(BF16)
    send_z = place_rows(scaled.reshape(-1, width), flat_ids, ranks, devices, capacity)
    recv_z = lax.all_to_all(send_z, "expert", split_axis=0, concat_axis=0, tiled=True)
    flat_z = recv_z.reshape(-1, width)
    flat_h = received.reshape(-1, hidden)
    grad_sum = lax.dot_general(flat_h, flat_z, (((0,), (0,)), ((), ())), preferred_element_type=F32)
    back = lax.dot_general(flat_z, weight, (((1,), (1,)), ((), ())), preferred_element_type=F32).astype(BF16)
    back_rows = lax.all_to_all(
        back.reshape(devices, capacity, hidden), "expert", split_axis=0, concat_axis=0, tiled=True
    )
    h_grad = back_rows[flat_ids, ranks].reshape(tokens_here, top_count, hidden)
    return (mixed, gate_grad, h_grad, grad_sum.astype(BF16)[None])


def upper(size):
    rows = lax.broadcasted_iota(jnp.int32, (size, size), 0)
    columns = lax.broadcasted_iota(jnp.int32, (size, size), 1)
    return (rows < columns).astype(F32).astype(BF16)


def pack_kernel(devices, capacity, ids_ref, h_ref, place_ref, sent_ref, place_scratch):
    pairs = ids_ref.shape[1]
    rows = sent_ref.shape[0]

    @pl.when(pl.program_id(0) == 0)
    def _():
        before = jnp.zeros((devices, 1), F32)
        for tile in range(pairs // 128):
            ids = ids_ref[:, tile * 128:(tile + 1) * 128]
            named = lax.broadcasted_iota(jnp.int32, (devices, 128), 0) == ids
            ones = jnp.where(named, 1.0, 0.0)
            rank = jnp.dot(ones.astype(BF16), upper(128), preferred_element_type=F32) + before
            before = before + jnp.sum(ones, axis=1, keepdims=True)
            rank = jnp.sum(jnp.where(named, rank, 0.0), axis=0, keepdims=True)
            place_scratch[:, tile * 128:(tile + 1) * 128] = ids * capacity + rank.astype(jnp.int32)
        place_ref[...] = place_scratch[...]

    first = pl.program_id(0) * rows
    wanted = lax.broadcasted_iota(jnp.int32, (rows, pairs), 0) + first
    chosen = jnp.where(wanted == place_scratch[...], 1.0, 0.0).astype(BF16)
    sent_ref[...] = jnp.dot(chosen, h_ref[...], preferred_element_type=F32).astype(BF16)


def pack(ids, h_flat, devices, capacity, steps=4):
    pairs, hidden = h_flat.shape
    rows = devices * capacity // steps
    return pl.pallas_call(
        functools.partial(pack_kernel, devices, capacity),
        grid=(steps,),
        in_specs=[
            pl.BlockSpec((1, pairs), lambda i: (0, 0)),
            pl.BlockSpec((pairs, hidden), lambda i: (0, 0)),
        ],
        out_specs=[
            pl.BlockSpec((1, pairs), lambda i: (0, 0)),
            pl.BlockSpec((rows, hidden), lambda i: (i, 0)),
        ],
        out_shape=[
            jax.ShapeDtypeStruct((1, pairs), jnp.int32),
            jax.ShapeDtypeStruct((devices * capacity, hidden), BF16),
        ],
        scratch_shapes=[pltpu.VMEM((1, pairs), jnp.int32)],
        compiler_params=pltpu.CompilerParams(vmem_limit_bytes=48 * MIB),
        cost_estimate=pl.CostEstimate(
            flops=2 * devices * capacity * pairs * hidden, transcendentals=0,
            bytes_accessed=2 * hidden * (pairs + devices * capacity),
        ),
        name="pack",
    )(ids, h_flat)


def unpack_kernel(slots, place_ref, gate_ref, h_ref, back_ref, grad_ref, gate_grad_ref):
    rows = place_ref.shape[0]
    chosen = lax.broadcasted_iota(jnp.int32, (rows, slots), 1) == place_ref[...]
    grad = jnp.dot(jnp.where(chosen, 1.0, 0.0).astype(BF16), back_ref[...], preferred_element_type=F32)
    grad_ref[...] = grad.astype(BF16)
    gate_grad_ref[...] = jnp.sum(grad * h_ref[...].astype(F32), axis=1, keepdims=True) / gate_ref[...]


def unpack(place, gates, h_flat, back_rows, steps=4):
    pairs, hidden = h_flat.shape
    slots = back_rows.shape[0]
    rows = pairs // steps
    return pl.pallas_call(
        functools.partial(unpack_kernel, slots),
        grid=(steps,),
        in_specs=[
            pl.BlockSpec((rows, 1), lambda i: (i, 0)),
            pl.BlockSpec((rows, 1), lambda i: (i, 0)),
            pl.BlockSpec((rows, hidden), lambda i: (i, 0)),
            pl.BlockSpec((slots, hidden), lambda i: (0, 0)),
        ],
        out_specs=[
            pl.BlockSpec((rows, hidden), lambda i: (i, 0)),
            pl.BlockSpec((rows, 1), lambda i: (i, 0)),
        ],
        out_shape=[
            jax.ShapeDtypeStruct((pairs, hidden), BF16),
            jax.ShapeDtypeStruct((pairs, 1), F32),
        ],
        compiler_params=pltpu.CompilerParams(vmem_limit_bytes=48 * MIB),
        cost_estimate=pl.CostEstimate(
            flops=2 * slots * pairs * hidden, transcendentals=0,
            bytes_accessed=2 * hidden * (2 * pairs + slots),
        ),
        name="unpack",
    )(place, gates, h_flat, back_rows)


def line_slots(position):
    near = jnp.minimum(position, 3 - position)
    turned = (near, near + 1, near + 2, 3 - 3 * near)
    return [jnp.where(position < 2, slot, 3 - slot) for slot in turned]


def route_kernel(devices, top, here_ref, routing_ref, rank_ref, gate_ref):
    for side in range(2):
        mine = (here_ref[0] ^ side).astype(F32)
        marks, picked = [], []
        for source in range(devices):
            ids = routing_ref[source, :top, :]
            gates = routing_ref[source, top:, :]
            named = ids == mine
            marks.append(jnp.sum(jnp.where(named, 1.0, 0.0), axis=0, keepdims=True))
            picked.append(jnp.sum(jnp.where(named, gates, 0.0), axis=0, keepdims=True))
        mark = jnp.concatenate(marks, axis=0)
        rank = jnp.dot(mark.astype(BF16), upper(mark.shape[1]), preferred_element_type=F32)
        rank_ref[side] = jnp.where(mark > 0, rank, -1.0).astype(jnp.int32)
        gate_ref[side] = jnp.concatenate(picked, axis=0)


def route(here, routing, top):
    devices, _, tokens = routing.shape
    return pl.pallas_call(
        functools.partial(route_kernel, devices, top),
        in_specs=[pl.BlockSpec(memory_space=pltpu.SMEM), pl.BlockSpec(memory_space=pltpu.VMEM)],
        out_specs=[pl.BlockSpec(memory_space=pltpu.VMEM)] * 2,
        out_shape=[
            jax.ShapeDtypeStruct((2, devices, tokens), jnp.int32),
            jax.ShapeDtypeStruct((2, devices, tokens), F32),
        ],
        cost_estimate=pl.CostEstimate(flops=1 << 21, transcendentals=0, bytes_accessed=1 << 19),
        name="route",
    )(here, routing)


def chosen_rows(rank_ref, side, source, capacity):
    rank = rank_ref[side, pl.ds(source, 1), :]
    return lax.broadcasted_iota(jnp.int32, (capacity, rank.shape[1]), 0) == rank


def gate_column(gate_ref, chosen, side, source):
    return jnp.sum(jnp.where(chosen, gate_ref[side, pl.ds(source, 1), :], 0.0), axis=1, keepdims=True)


def one_hot(chosen):
    return jnp.where(chosen, 1.0, 0.0).astype(BF16)


def lane_sources(here, slots, lane):
    line, across = here // 4, (here // 2) % 2
    places = line_slots(line)
    return [places[slot] * 4 + (across ^ turn) * 2 + lane for slot in slots for turn in range(2)]


def back_kernel(capacity, rank_ref, gate_ref, cot_ref, weight_ref, z_ref, back_ref):
    each = cot_ref.shape[0]
    for j in range(each):
        source = pl.program_id(0) * each + j
        chosen = chosen_rows(rank_ref, 0, source, capacity)
        gate = gate_column(gate_ref, chosen, 0, source)
        rows = jnp.dot(one_hot(chosen), cot_ref[j], preferred_element_type=F32)
        z_ref[j * capacity:(j + 1) * capacity, :] = (rows * gate).astype(BF16)
    back = lax.dot_general(z_ref[...], weight_ref[...], (((1,), (1,)), ((), ())), preferred_element_type=F32)
    back_ref[...] = back.astype(BF16)


def backward_rows(rank, gate, cotangents, weight, capacity, each=4):
    devices, tokens, width = cotangents.shape
    hidden = weight.shape[0]
    rows = each * capacity
    return pl.pallas_call(
        functools.partial(back_kernel, capacity),
        grid=(devices // each,),
        in_specs=[
            pl.BlockSpec(rank.shape, lambda i: (0, 0, 0)),
            pl.BlockSpec(rank.shape, lambda i: (0, 0, 0)),
            pl.BlockSpec((each, tokens, width), lambda i: (i, 0, 0)),
            pl.BlockSpec((hidden, width), lambda i: (0, 0)),
        ],
        out_specs=[
            pl.BlockSpec((rows, width), lambda i: (i, 0)),
            pl.BlockSpec((rows, hidden), lambda i: (i, 0)),
        ],
        out_shape=[
            jax.ShapeDtypeStruct((devices * capacity, width), BF16),
            jax.ShapeDtypeStruct((devices * capacity, hidden), BF16),
        ],
        compiler_params=pltpu.CompilerParams(vmem_limit_bytes=48 * MIB),
        cost_estimate=pl.CostEstimate(
            flops=2 * devices * capacity * width * (hidden + tokens), transcendentals=0,
            bytes_accessed=2 * devices * (tokens * width + capacity * (width + hidden)) + 2 * width * hidden,
        ),
        name="backward_rows",
    )(rank, gate, cotangents, weight)


def forward_kernel(capacity, turn, here_ref, rank_ref, gate_ref, h_ref, weight_ref, out_ref):
    each = out_ref.shape[0]
    lane = (here_ref[0] % 2) ^ turn
    flat = h_ref[...].reshape(each * capacity, h_ref.shape[3])
    out = jnp.dot(flat, weight_ref[...], preferred_element_type=F32).astype(BF16).astype(F32)
    for j in range(each):
        source = (pl.program_id(0) * each + j) * 2 + lane
        gate = gate_column(gate_ref, chosen_rows(rank_ref, 0, source, capacity), 0, source)
        out_ref[j] = (out[j * capacity:(j + 1) * capacity, :] * gate).astype(BF16)


def forward_rows(here, rank, gate, rows_h, weight, turn, each=4):
    devices, capacity, hidden = rows_h.shape
    width = weight.shape[1]
    whole = pl.BlockSpec(rank.shape, lambda i, here: (0, 0, 0))
    return pl.pallas_call(
        functools.partial(forward_kernel, capacity, turn),
        grid_spec=pltpu.PrefetchScalarGridSpec(
            num_scalar_prefetch=1,
            grid=(devices // 2 // each,),
            in_specs=[
                whole,
                whole,
                pl.BlockSpec((each, 1, capacity, hidden), lambda i, here: (i, (here[0] % 2) ^ turn, 0, 0)),
                pl.BlockSpec((hidden, width), lambda i, here: (0, 0)),
            ],
            out_specs=pl.BlockSpec((each, capacity, width), lambda i, here: (i, 0, 0)),
        ),
        out_shape=jax.ShapeDtypeStruct((devices // 2, capacity, width), BF16),
        compiler_params=pltpu.CompilerParams(vmem_limit_bytes=40 * MIB),
        cost_estimate=pl.CostEstimate(
            flops=devices * capacity * width * hidden, transcendentals=0,
            bytes_accessed=devices * capacity * (width + hidden) + 2 * width * hidden,
        ),
        name="forward_rows",
    )(here, rank, gate, rows_h.reshape(devices // 2, 2, capacity, hidden), weight)


ORDER = (3, 2, 1, 0)


def sum_kernel(capacity, turn, here_ref, rank_ref, own_ref, other_ref, *part_refs):
    for step, slot in enumerate(ORDER):

        @pl.when(pl.program_id(0) == step)
        def _():
            source = lane_sources(here_ref[0], (slot,), here_ref[0] % 2)[turn]
            both = [one_hot(chosen_rows(rank_ref, side, source, capacity)) for side in range(2)]
            rows = jnp.concatenate([own_ref[0], other_ref[0]], axis=0)
            part = lax.dot_general(
                jnp.concatenate(both, axis=0), rows, (((0,), (0,)), ((), ())), preferred_element_type=F32
            )
            part_refs[step][...] = part.astype(BF16)


def summed(here, rank, own, other, turn):
    _, capacity, width = own.shape
    tokens = rank.shape[2]

    def block(i, here):
        place = jnp.int32(0)
        for step, slot in enumerate(ORDER):
            place = jnp.where(i == step, lane_sources(here[0], (slot,), 0)[turn] // 2, place)
        return (place, 0, 0)

    return pl.pallas_call(
        functools.partial(sum_kernel, capacity, turn),
        grid_spec=pltpu.PrefetchScalarGridSpec(
            num_scalar_prefetch=1,
            grid=(len(ORDER),),
            in_specs=[
                pl.BlockSpec(rank.shape, lambda i, here: (0, 0, 0)),
                pl.BlockSpec((1, capacity, width), block),
                pl.BlockSpec((1, capacity, width), block),
            ],
            out_specs=[pl.BlockSpec((tokens, width), lambda i, here: (0, 0))] * len(ORDER),
        ),
        out_shape=[jax.ShapeDtypeStruct((tokens, width), BF16)] * len(ORDER),
        compiler_params=pltpu.CompilerParams(vmem_limit_bytes=40 * MIB),
        cost_estimate=pl.CostEstimate(
            flops=16 * tokens * capacity * width, transcendentals=0,
            bytes_accessed=8 * width * (tokens + 2 * capacity),
        ),
        name="summed",
    )(here, rank, own, other)


def added(*values):
    total = values[0].astype(F32)
    for value in values[1:]:
        total = total + value.astype(F32)
    return total.astype(BF16)


def passed(pairs, value):
    return lax.ppermute(value, "expert", [(a * 4 + lane, b * 4 + lane) for a, b in pairs for lane in range(4)])


def swapped_with(value, bit):
    devices = lax.axis_size("expert")
    return lax.ppermute(value, "expert", [(i, i ^ bit) for i in range(devices)])


OUTER, INNER = ((0, 1), (3, 2)), ((1, 2), (2, 1))
ENDS, ENDS_SWAP = ((1, 0), (2, 3)), ((0, 3), (3, 0))


def dense_shards(h_rows, gates, expert_ids, cotangent, down_weight, swapped):
    devices = lax.axis_size("expert")
    here = lax.axis_index("expert").reshape(1)
    tokens, top, hidden = h_rows.shape
    capacity = min(tokens, 3 * tokens * top // (2 * devices))
    weight = down_weight[0]
    slot_ids = slots_of(expert_ids, swapped, devices)
    h_flat = h_rows.reshape(-1, hidden)

    routing = jnp.concatenate([slot_ids.T.astype(F32), gates.T], axis=0)
    routing = jnp.broadcast_to(routing, (devices,) + routing.shape)
    routing = lax.all_to_all(routing, "expert", split_axis=0, concat_axis=0, tiled=True)
    rank, gate = route(here, routing, top)

    cotangents = lax.all_gather(cotangent, "expert", axis=0, tiled=False)
    place, send_h = pack(slot_ids.reshape(1, -1), h_flat, devices, capacity)
    rows_h = lax.all_to_all(
        send_h.reshape(devices, capacity, hidden), "expert", split_axis=0, concat_axis=0, tiled=True
    )

    z_rows, back = backward_rows(rank, gate, cotangents, weight, capacity)
    back = back.reshape(devices, capacity, hidden)
    back_rows = lax.all_to_all(back, "expert", split_axis=0, concat_axis=0, tiled=True).reshape(-1, hidden)

    other = swapped_with(forward_rows(here, rank, gate, rows_h, weight, 1), 1)
    mine = forward_rows(here, rank, gate, rows_h, weight, 0)
    across = [swapped_with(part, 2) for part in summed(here, rank, mine, other, 1)]
    beside = summed(here, rank, mine, other, 0)
    far, mid, close, kept = zip(beside, across)
    far, mid, close = added(*far), added(*mid), added(*close)
    ends = passed(ENDS_SWAP, far)
    mid_outer, mid_inner = passed(OUTER, mid), passed(INNER, mid)
    close_outer = passed(OUTER, close)
    close_inner = passed(INNER, added(close, mid_outer))
    far_ends = passed(ENDS, added(far, mid_inner))
    mixed = added(*kept, ends, close_outer, close_inner, far_ends)

    grad_sum = lax.dot_general(flat_h, flat_z, (((0,), (0,)), ((), ())), preferred_element_type=F32)
    back = lax.dot_general(flat_z, weight, (((1,), (1,)), ((), ())), preferred_element_type=F32).astype(BF16)
    back_rows = lax.all_to_all(
        back.reshape(devices, capacity, hidden), "expert", split_axis=0, concat_axis=0, tiled=True
    )
    h_grad = back_rows[flat_ids, ranks].reshape(tokens_here, top_count, hidden)
    return (mixed, gate_grad, h_grad, grad_sum.astype(BF16)[None])


def upper(size):
    rows = lax.broadcasted_iota(jnp.int32, (size, size), 0)
    columns = lax.broadcasted_iota(jnp.int32, (size, size), 1)
    return (rows < columns).astype(F32).astype(BF16)


def pack_kernel(devices, capacity, ids_ref, h_ref, place_ref, sent_ref, place_scratch):
    pairs = ids_ref.shape[1]
    rows = sent_ref.shape[0]

    @pl.when(pl.program_id(0) == 0)
    def _():
        before = jnp.zeros((devices, 1), F32)
        for tile in range(pairs // 128):
            ids = ids_ref[:, tile * 128:(tile + 1) * 128]
            named = lax.broadcasted_iota(jnp.int32, (devices, 128), 0) == ids
            ones = jnp.where(named, 1.0, 0.0)
            rank = jnp.dot(ones.astype(BF16), upper(128), preferred_element_type=F32) + before
            before = before + jnp.sum(ones, axis=1, keepdims=True)
            rank = jnp.sum(jnp.where(named, rank, 0.0), axis=0, keepdims=True)
            place_scratch[:, tile * 128:(tile + 1) * 128] = ids * capacity + rank.astype(jnp.int32)
        place_ref[...] = place_scratch[...]

    first = pl.program_id(0) * rows
    wanted = lax.broadcasted_iota(jnp.int32, (rows, pairs), 0) + first
    chosen = jnp.where(wanted == place_scratch[...], 1.0, 0.0).astype(BF16)
    sent_ref[...] = jnp.dot(chosen, h_ref[...], preferred_element_type=F32).astype(BF16)


def pack(ids, h_flat, devices, capacity, steps=4):
    pairs, hidden = h_flat.shape
    rows = devices * capacity // steps
    return pl.pallas_call(
        functools.partial(pack_kernel, devices, capacity),
        grid=(steps,),
        in_specs=[
            pl.BlockSpec((1, pairs), lambda i: (0, 0)),
            pl.BlockSpec((pairs, hidden), lambda i: (0, 0)),
        ],
        out_specs=[
            pl.BlockSpec((1, pairs), lambda i: (0, 0)),
            pl.BlockSpec((rows, hidden), lambda i: (i, 0)),
        ],
        out_shape=[
            jax.ShapeDtypeStruct((1, pairs), jnp.int32),
            jax.ShapeDtypeStruct((devices * capacity, hidden), BF16),
        ],
        scratch_shapes=[pltpu.VMEM((1, pairs), jnp.int32)],
        compiler_params=pltpu.CompilerParams(vmem_limit_bytes=48 * MIB),
        cost_estimate=pl.CostEstimate(
            flops=2 * devices * capacity * pairs * hidden, transcendentals=0,
            bytes_accessed=2 * hidden * (pairs + devices * capacity),
        ),
        name="pack",
    )(ids, h_flat)


def unpack_kernel(slots, place_ref, gate_ref, h_ref, back_ref, grad_ref, gate_grad_ref):
    rows = place_ref.shape[0]
    chosen = lax.broadcasted_iota(jnp.int32, (rows, slots), 1) == place_ref[...]
    grad = jnp.dot(jnp.where(chosen, 1.0, 0.0).astype(BF16), back_ref[...], preferred_element_type=F32)
    grad_ref[...] = grad.astype(BF16)
    gate_grad_ref[...] = jnp.sum(grad * h_ref[...].astype(F32), axis=1, keepdims=True) / gate_ref[...]


def unpack(place, gates, h_flat, back_rows, steps=4):
    pairs, hidden = h_flat.shape
    slots = back_rows.shape[0]
    rows = pairs // steps
    return pl.pallas_call(
        functools.partial(unpack_kernel, slots),
        grid=(steps,),
        in_specs=[
            pl.BlockSpec((rows, 1), lambda i: (i, 0)),
            pl.BlockSpec((rows, 1), lambda i: (i, 0)),
            pl.BlockSpec((rows, hidden), lambda i: (i, 0)),
            pl.BlockSpec((slots, hidden), lambda i: (0, 0)),
        ],
        out_specs=[
            pl.BlockSpec((rows, hidden), lambda i: (i, 0)),
            pl.BlockSpec((rows, 1), lambda i: (i, 0)),
        ],
        out_shape=[
            jax.ShapeDtypeStruct((pairs, hidden), BF16),
            jax.ShapeDtypeStruct((pairs, 1), F32),
        ],
        compiler_params=pltpu.CompilerParams(vmem_limit_bytes=48 * MIB),
        cost_estimate=pl.CostEstimate(
            flops=2 * slots * pairs * hidden, transcendentals=0,
            bytes_accessed=2 * hidden * (2 * pairs + slots),
        ),
        name="unpack",
    )(place, gates, h_flat, back_rows)


def line_slots(position):
    near = jnp.minimum(position, 3 - position)
    turned = (near, near + 1, near + 2, 3 - 3 * near)
    return [jnp.where(position < 2, slot, 3 - slot) for slot in turned]


def route_kernel(devices, top, here_ref, routing_ref, rank_ref, gate_ref):
    for side in range(2):
        mine = (here_ref[0] ^ side).astype(F32)
        marks, picked = [], []
        for source in range(devices):
            ids = routing_ref[source, :top, :]
            gates = routing_ref[source, top:, :]
            named = ids == mine
            marks.append(jnp.sum(jnp.where(named, 1.0, 0.0), axis=0, keepdims=True))
            picked.append(jnp.sum(jnp.where(named, gates, 0.0), axis=0, keepdims=True))
        mark = jnp.concatenate(marks, axis=0)
        rank = jnp.dot(mark.astype(BF16), upper(mark.shape[1]), preferred_element_type=F32)
        rank_ref[side] = jnp.where(mark > 0, rank, -1.0).astype(jnp.int32)
        gate_ref[side] = jnp.concatenate(picked, axis=0)


def route(here, routing, top):
    devices, _, tokens = routing.shape
    return pl.pallas_call(
        functools.partial(route_kernel, devices, top),
        in_specs=[pl.BlockSpec(memory_space=pltpu.SMEM), pl.BlockSpec(memory_space=pltpu.VMEM)],
        out_specs=[pl.BlockSpec(memory_space=pltpu.VMEM)] * 2,
        out_shape=[
            jax.ShapeDtypeStruct((2, devices, tokens), jnp.int32),
            jax.ShapeDtypeStruct((2, devices, tokens), F32),
        ],
        cost_estimate=pl.CostEstimate(flops=1 << 21, transcendentals=0, bytes_accessed=1 << 19),
        name="route",
    )(here, routing)


def chosen_rows(rank_ref, side, source, capacity):
    rank = rank_ref[side, pl.ds(source, 1), :]
    return lax.broadcasted_iota(jnp.int32, (capacity, rank.shape[1]), 0) == rank


def gate_column(gate_ref, chosen, side, source):
    return jnp.sum(jnp.where(chosen, gate_ref[side, pl.ds(source, 1), :], 0.0), axis=1, keepdims=True)


def one_hot(chosen):
    return jnp.where(chosen, 1.0, 0.0).astype(BF16)


def lane_sources(here, slots, lane):
    line, across = here // 4, (here // 2) % 2
    places = line_slots(line)
    return [places[slot] * 4 + (across ^ turn) * 2 + lane for slot in slots for turn in range(2)]


def back_kernel(capacity, rank_ref, gate_ref, cot_ref, weight_ref, z_ref, back_ref):
    each = cot_ref.shape[0]
    for j in range(each):
        source = pl.program_id(0) * each + j
        chosen = chosen_rows(rank_ref, 0, source, capacity)
        gate = gate_column(gate_ref, chosen, 0, source)
        rows = jnp.dot(one_hot(chosen), cot_ref[j], preferred_element_type=F32)
        z_ref[j * capacity:(j + 1) * capacity, :] = (rows * gate).astype(BF16)
    back = lax.dot_general(z_ref[...], weight_ref[...], (((1,), (1,)), ((), ())), preferred_element_type=F32)
    back_ref[...] = back.astype(BF16)


def backward_rows(rank, gate, cotangents, weight, capacity, each=4):
    devices, tokens, width = cotangents.shape
    hidden = weight.shape[0]
    rows = each * capacity
    return pl.pallas_call(
        functools.partial(back_kernel, capacity),
        grid=(devices // each,),
        in_specs=[
            pl.BlockSpec(rank.shape, lambda i: (0, 0, 0)),
            pl.BlockSpec(rank.shape, lambda i: (0, 0, 0)),
            pl.BlockSpec((each, tokens, width), lambda i: (i, 0, 0)),
            pl.BlockSpec((hidden, width), lambda i: (0, 0)),
        ],
        out_specs=[
            pl.BlockSpec((rows, width), lambda i: (i, 0)),
            pl.BlockSpec((rows, hidden), lambda i: (i, 0)),
        ],
        out_shape=[
            jax.ShapeDtypeStruct((devices * capacity, width), BF16),
            jax.ShapeDtypeStruct((devices * capacity, hidden), BF16),
        ],
        compiler_params=pltpu.CompilerParams(vmem_limit_bytes=48 * MIB),
        cost_estimate=pl.CostEstimate(
            flops=2 * devices * capacity * width * (hidden + tokens), transcendentals=0,
            bytes_accessed=2 * devices * (tokens * width + capacity * (width + hidden)) + 2 * width * hidden,
        ),
        name="backward_rows",
    )(rank, gate, cotangents, weight)


def forward_kernel(capacity, turn, here_ref, rank_ref, gate_ref, h_ref, weight_ref, out_ref):
    each = out_ref.shape[0]
    lane = (here_ref[0] % 2) ^ turn
    flat = h_ref[...].reshape(each * capacity, h_ref.shape[3])
    out = jnp.dot(flat, weight_ref[...], preferred_element_type=F32).astype(BF16).astype(F32)
    for j in range(each):
        source = (pl.program_id(0) * each + j) * 2 + lane
        gate = gate_column(gate_ref, chosen_rows(rank_ref, 0, source, capacity), 0, source)
        out_ref[j] = (out[j * capacity:(j + 1) * capacity, :] * gate).astype(BF16)


def forward_rows(here, rank, gate, rows_h, weight, turn, each=4):
    devices, capacity, hidden = rows_h.shape
    width = weight.shape[1]
    whole = pl.BlockSpec(rank.shape, lambda i, here: (0, 0, 0))
    return pl.pallas_call(
        functools.partial(forward_kernel, capacity, turn),
        grid_spec=pltpu.PrefetchScalarGridSpec(
            num_scalar_prefetch=1,
            grid=(devices // 2 // each,),
            in_specs=[
                whole,
                whole,
                pl.BlockSpec((each, 1, capacity, hidden), lambda i, here: (i, (here[0] % 2) ^ turn, 0, 0)),
                pl.BlockSpec((hidden, width), lambda i, here: (0, 0)),
            ],
            out_specs=pl.BlockSpec((each, capacity, width), lambda i, here: (i, 0, 0)),
        ),
        out_shape=jax.ShapeDtypeStruct((devices // 2, capacity, width), BF16),
        compiler_params=pltpu.CompilerParams(vmem_limit_bytes=40 * MIB),
        cost_estimate=pl.CostEstimate(
            flops=devices * capacity * width * hidden, transcendentals=0,
            bytes_accessed=devices * capacity * (width + hidden) + 2 * width * hidden,
        ),
        name="forward_rows",
    )(here, rank, gate, rows_h.reshape(devices // 2, 2, capacity, hidden), weight)


ORDER = (3, 2, 1, 0)


def sum_kernel(capacity, turn, here_ref, rank_ref, own_ref, other_ref, *part_refs):
    for step, slot in enumerate(ORDER):

        @pl.when(pl.program_id(0) == step)
        def _():
            source = lane_sources(here_ref[0], (slot,), here_ref[0] % 2)[turn]
            both = [one_hot(chosen_rows(rank_ref, side, source, capacity)) for side in range(2)]
            rows = jnp.concatenate([own_ref[0], other_ref[0]], axis=0)
            part = lax.dot_general(
                jnp.concatenate(both, axis=0), rows, (((0,), (0,)), ((), ())), preferred_element_type=F32
            )
            part_refs[step][...] = part.astype(BF16)


def summed(here, rank, own, other, turn):
    _, capacity, width = own.shape
    tokens = rank.shape[2]

    def block(i, here):
        place = jnp.int32(0)
        for step, slot in enumerate(ORDER):
            place = jnp.where(i == step, lane_sources(here[0], (slot,), 0)[turn] // 2, place)
        return (place, 0, 0)

    return pl.pallas_call(
        functools.partial(sum_kernel, capacity, turn),
        grid_spec=pltpu.PrefetchScalarGridSpec(
            num_scalar_prefetch=1,
            grid=(len(ORDER),),
            in_specs=[
                pl.BlockSpec(rank.shape, lambda i, here: (0, 0, 0)),
                pl.BlockSpec((1, capacity, width), block),
                pl.BlockSpec((1, capacity, width), block),
            ],
            out_specs=[pl.BlockSpec((tokens, width), lambda i, here: (0, 0))] * len(ORDER),
        ),
        out_shape=[jax.ShapeDtypeStruct((tokens, width), BF16)] * len(ORDER),
        compiler_params=pltpu.CompilerParams(vmem_limit_bytes=40 * MIB),
        cost_estimate=pl.CostEstimate(
            flops=16 * tokens * capacity * width, transcendentals=0,
            bytes_accessed=8 * width * (tokens + 2 * capacity),
        ),
        name="summed",
    )(here, rank, own, other)


def added(*values):
    total = values[0].astype(F32)
    for value in values[1:]:
        total = total + value.astype(F32)
    return total.astype(BF16)


def passed(pairs, value):
    return lax.ppermute(value, "expert", [(a * 4 + lane, b * 4 + lane) for a, b in pairs for lane in range(4)])


def swapped_with(value, bit):
    devices = lax.axis_size("expert")
    return lax.ppermute(value, "expert", [(i, i ^ bit) for i in range(devices)])


OUTER, INNER = ((0, 1), (3, 2)), ((1, 2), (2, 1))
ENDS, ENDS_SWAP = ((1, 0), (2, 3)), ((0, 3), (3, 0))


def dense_shards(h_rows, gates, expert_ids, cotangent, down_weight, swapped):
    devices = lax.axis_size("expert")
    here = lax.axis_index("expert").reshape(1)
    tokens, top, hidden = h_rows.shape
    capacity = min(tokens, 3 * tokens * top // (2 * devices))
    weight = down_weight[0]
    slot_ids = slots_of(expert_ids, swapped, devices)
    h_flat = h_rows.reshape(-1, hidden)

    routing = jnp.concatenate([slot_ids.T.astype(F32), gates.T], axis=0)
    routing = jnp.broadcast_to(routing, (devices,) + routing.shape)
    routing = lax.all_to_all(routing, "expert", split_axis=0, concat_axis=0, tiled=True)
    rank, gate = route(here, routing, top)

    cotangents = lax.all_gather(cotangent, "expert", axis=0, tiled=False)
    place, send_h = pack(slot_ids.reshape(1, -1), h_flat, devices, capacity)
    rows_h = lax.all_to_all(
        send_h.reshape(devices, capacity, hidden), "expert", split_axis=0, concat_axis=0, tiled=True
    )

    z_rows, back = backward_rows(rank, gate, cotangents, weight, capacity)
    back = back.reshape(devices, capacity, hidden)
    back_rows = lax.all_to_all(back, "expert", split_axis=0, concat_axis=0, tiled=True).reshape(-1, hidden)

    other = swapped_with(forward_rows(here, rank, gate, rows_h, weight, 1), 1)
    mine = forward_rows(here, rank, gate, rows_h, weight, 0)
    across = [swapped_with(part, 2) for part in summed(here, rank, mine, other, 1)]
    beside = summed(here, rank, mine, other, 0)
    far, mid, close, kept = zip(beside, across)
    outer1 = passed(OUTER, added(*far))
    mid = added(*mid, outer1)
    outer2, inner2 = passed(OUTER, mid), passed(INNER, mid)
    close = added(*close, outer2)
    outer3, inner3 = passed(OUTER, close), passed(INNER, close)
    ends3 = passed(ENDS, added(*far, inner2))
    mixed = added(*kept, outer3, inner3, ends3)

    grad_sum = lax.dot_general(
        rows_h.reshape(-1, hidden), z_rows, (((0,), (0,)), ((), ())),
        preferred_element_type=F32,
    )
    h_grad, gate_grad = unpack(place.reshape(-1, 1), gates.reshape(-1, 1), h_flat, back_rows)
    return (
        mixed,
        gate_grad.reshape(tokens, top),
        h_grad.reshape(tokens, top, hidden),
        grad_sum.astype(BF16)[None],
    )


def shards(h_rows, *rest):
    devices = lax.axis_size("expert")
    dense = devices == 16 and devices <= 2 * h_rows.shape[1]
    return (dense_shards if dense else sparse_shards)(h_rows, *rest)


def solution(mesh):
    in_specs = (
        P(("groups", "expert"), None, None),
        P(("groups", "expert"), None),
        P(("groups", "expert"), None),
        P(("groups", "expert"), None),
        P("expert", None, None),
        P(),
    )
    out_specs = (
        P(("groups", "expert"), None),
        P(("groups", "expert"), None),
        P(("groups", "expert"), None, None),
        P(("groups", "expert"), None, None),
    )
    return jax.shard_map(shards, mesh=mesh, in_specs=in_specs, out_specs=out_specs, check_vma=False)
```

```python
import functools

import jax
import jax.numpy as jnp
from jax import lax
from jax.experimental import pallas as pl
from jax.experimental.pallas import tpu as pltpu
from jax.sharding import PartitionSpec as P

F32 = jnp.float32
BF16 = jnp.bfloat16
MIB = 1 << 20


def slots_of(ids, swapped, devices):
    half_way = devices // 2
    table = jnp.arange(devices, dtype=jnp.int32)
    table = (table + half_way * swapped[table % half_way]) % devices
    return jnp.sum(jnp.where(ids[..., None] == jnp.arange(devices, dtype=jnp.int32), table, 0), axis=-1)


def place_rows(values, target, ranks, devices, capacity):
    buffer = jnp.zeros((devices, capacity, values.shape[-1]), values.dtype)
    return buffer.at[target, ranks].set(values)


def sparse_shards(h_rows, gates, expert_ids, cotangent, down_weight, swapped):
    devices = lax.axis_size("expert")
    tokens_here, top_count, hidden = h_rows.shape
    width = cotangent.shape[1]
    capacity = min(tokens_here, 3 * tokens_here * top_count // (2 * devices))
    experts = jnp.arange(devices, dtype=jnp.int32)
    weight = down_weight[0]
    flat_ids = slots_of(expert_ids.reshape(-1), swapped, devices)
    onehot = (flat_ids[:, None] == experts[None, :]).astype(jnp.int32)
    ranks = jnp.sum((jnp.cumsum(onehot, axis=0) - onehot) * onehot, axis=1)
    send_h = place_rows(h_rows.reshape(-1, hidden), flat_ids, ranks, devices, capacity)
    received = lax.all_to_all(send_h, "expert", split_axis=0, concat_axis=0, tiled=True)
    result = jnp.einsum("sch,hd->scd", received, weight, preferred_element_type=F32)
    results = result.astype(BF16)
    returned = lax.all_to_all(results, "expert", split_axis=0, concat_axis=0, tiled=True)
    out_rows = returned[flat_ids, ranks].reshape(tokens_here, top_count, width)
    mixed = jnp.einsum("tk,tkd->td", gates, out_rows.astype(F32)).astype(BF16)
    gate_grad = jnp.einsum("td,tkd->tk", cotangent, out_rows, preferred_element_type=F32)
    scaled = (gates[:, :, None] * cotangent[:, None, :].astype(F32)).astype(BF16)
    send_z = place_rows(scaled.reshape(-1, width), flat_ids, ranks, devices, capacity)
    recv_z = lax.all_to_all(send_z, "expert", split_axis=0, concat_axis=0, tiled=True)
    flat_z = recv_z.reshape(-1, width)
    flat_h = received.reshape(-1, hidden)
    grad_sum = lax.dot_general(flat_h, flat_z, (((0,), (0,)), ((), ())), preferred_element_type=F32)
    back = lax.dot_general(flat_z, weight, (((1,), (1,)), ((), ())), preferred_element_type=F32).astype(BF16)
    back_rows = lax.all_to_all(
        back.reshape(devices, capacity, hidden), "expert", split_axis=0, concat_axis=0, tiled=True
    )
    h_grad = back_rows[flat_ids, ranks].reshape(tokens_here, top_count, hidden)
    return (mixed, gate_grad, h_grad, grad_sum.astype(BF16)[None])


def upper(size):
    rows = lax.broadcasted_iota(jnp.int32, (size, size), 0)
    columns = lax.broadcasted_iota(jnp.int32, (size, size), 1)
    return (rows < columns).astype(F32).astype(BF16)


def pack_kernel(devices, capacity, ids_ref, h_ref, place_ref, sent_ref, place_scratch):
    pairs = ids_ref.shape[1]
    rows = sent_ref.shape[0]

    @pl.when(pl.program_id(0) == 0)
    def _():
        before = jnp.zeros((devices, 1), F32)
        for tile in range(pairs // 128):
            ids = ids_ref[:, tile * 128:(tile + 1) * 128]
            named = lax.broadcasted_iota(jnp.int32, (devices, 128), 0) == ids
            ones = jnp.where(named, 1.0, 0.0)
            rank = jnp.dot(ones.astype(BF16), upper(128), preferred_element_type=F32) + before
            before = before + jnp.sum(ones, axis=1, keepdims=True)
            rank = jnp.sum(jnp.where(named, rank, 0.0), axis=0, keepdims=True)
            place_scratch[:, tile * 128:(tile + 1) * 128] = ids * capacity + rank.astype(jnp.int32)
        place_ref[...] = place_scratch[...]

    first = pl.program_id(0) * rows
    wanted = lax.broadcasted_iota(jnp.int32, (rows, pairs), 0) + first
    chosen = jnp.where(wanted == place_scratch[...], 1.0, 0.0).astype(BF16)
    sent_ref[...] = jnp.dot(chosen, h_ref[...], preferred_element_type=F32).astype(BF16)


def pack(ids, h_flat, devices, capacity, steps=4):
    pairs, hidden = h_flat.shape
    rows = devices * capacity // steps
    return pl.pallas_call(
        functools.partial(pack_kernel, devices, capacity),
        grid=(steps,),
        in_specs=[
            pl.BlockSpec((1, pairs), lambda i: (0, 0)),
            pl.BlockSpec((pairs, hidden), lambda i: (0, 0)),
        ],
        out_specs=[
            pl.BlockSpec((1, pairs), lambda i: (0, 0)),
            pl.BlockSpec((rows, hidden), lambda i: (i, 0)),
        ],
        out_shape=[
            jax.ShapeDtypeStruct((1, pairs), jnp.int32),
            jax.ShapeDtypeStruct((devices * capacity, hidden), BF16),
        ],
        scratch_shapes=[pltpu.VMEM((1, pairs), jnp.int32)],
        compiler_params=pltpu.CompilerParams(vmem_limit_bytes=48 * MIB),
        cost_estimate=pl.CostEstimate(
            flops=2 * devices * capacity * pairs * hidden, transcendentals=0,
            bytes_accessed=2 * hidden * (pairs + devices * capacity),
        ),
        name="pack",
    )(ids, h_flat)


def unpack_kernel(slots, place_ref, gate_ref, h_ref, back_ref, grad_ref, gate_grad_ref):
    rows = place_ref.shape[0]
    chosen = lax.broadcasted_iota(jnp.int32, (rows, slots), 1) == place_ref[...]
    grad = jnp.dot(jnp.where(chosen, 1.0, 0.0).astype(BF16), back_ref[...], preferred_element_type=F32)
    grad_ref[...] = grad.astype(BF16)
    gate_grad_ref[...] = jnp.sum(grad * h_ref[...].astype(F32), axis=1, keepdims=True) / gate_ref[...]


def unpack(place, gates, h_flat, back_rows, steps=4):
    pairs, hidden = h_flat.shape
    slots = back_rows.shape[0]
    rows = pairs // steps
    return pl.pallas_call(
        functools.partial(unpack_kernel, slots),
        grid=(steps,),
        in_specs=[
            pl.BlockSpec((rows, 1), lambda i: (i, 0)),
            pl.BlockSpec((rows, 1), lambda i: (i, 0)),
            pl.BlockSpec((rows, hidden), lambda i: (i, 0)),
            pl.BlockSpec((slots, hidden), lambda i: (0, 0)),
        ],
        out_specs=[
            pl.BlockSpec((rows, hidden), lambda i: (i, 0)),
            pl.BlockSpec((rows, 1), lambda i: (i, 0)),
        ],
        out_shape=[
            jax.ShapeDtypeStruct((pairs, hidden), BF16),
            jax.ShapeDtypeStruct((pairs, 1), F32),
        ],
        compiler_params=pltpu.CompilerParams(vmem_limit_bytes=48 * MIB),
        cost_estimate=pl.CostEstimate(
            flops=2 * slots * pairs * hidden, transcendentals=0,
            bytes_accessed=2 * hidden * (2 * pairs + slots),
        ),
        name="unpack",
    )(place, gates, h_flat, back_rows)


def line_slots(position):
    near = jnp.minimum(position, 3 - position)
    turned = (near, near + 1, near + 2, 3 - 3 * near)
    return [jnp.where(position < 2, slot, 3 - slot) for slot in turned]


def route_kernel(devices, top, here_ref, routing_ref, rank_ref, gate_ref):
    for side in range(2):
        mine = (here_ref[0] ^ side).astype(F32)
        marks, picked = [], []
        for source in range(devices):
            ids = routing_ref[source, :top, :]
            gates = routing_ref[source, top:, :]
            named = ids == mine
            marks.append(jnp.sum(jnp.where(named, 1.0, 0.0), axis=0, keepdims=True))
            picked.append(jnp.sum(jnp.where(named, gates, 0.0), axis=0, keepdims=True))
        mark = jnp.concatenate(marks, axis=0)
        rank = jnp.dot(mark.astype(BF16), upper(mark.shape[1]), preferred_element_type=F32)
        rank_ref[side] = jnp.where(mark > 0, rank, -1.0).astype(jnp.int32)
        gate_ref[side] = jnp.concatenate(picked, axis=0)


def route(here, routing, top):
    devices, _, tokens = routing.shape
    return pl.pallas_call(
        functools.partial(route_kernel, devices, top),
        in_specs=[pl.BlockSpec(memory_space=pltpu.SMEM), pl.BlockSpec(memory_space=pltpu.VMEM)],
        out_specs=[pl.BlockSpec(memory_space=pltpu.VMEM)] * 2,
        out_shape=[
            jax.ShapeDtypeStruct((2, devices, tokens), jnp.int32),
            jax.ShapeDtypeStruct((2, devices, tokens), F32),
        ],
        cost_estimate=pl.CostEstimate(flops=1 << 21, transcendentals=0, bytes_accessed=1 << 19),
        name="route",
    )(here, routing)


def chosen_rows(rank_ref, side, source, capacity):
    rank = rank_ref[side, pl.ds(source, 1), :]
    return lax.broadcasted_iota(jnp.int32, (capacity, rank.shape[1]), 0) == rank


def gate_column(gate_ref, chosen, side, source):
    return jnp.sum(jnp.where(chosen, gate_ref[side, pl.ds(source, 1), :], 0.0), axis=1, keepdims=True)


def one_hot(chosen):
    return jnp.where(chosen, 1.0, 0.0).astype(BF16)


def lane_sources(here, slots, lane):
    line, across = here // 4, (here // 2) % 2
    places = line_slots(line)
    return [places[slot] * 4 + (across ^ turn) * 2 + lane for slot in slots for turn in range(2)]


def place_out(pieces, sem):
    copies = [pltpu.make_async_copy(source, target, sem.at[i]) for i, (source, target) in enumerate(pieces)]
    for copy in copies:
        copy.start()
    return copies


def scale_kernel(capacity, slots, held, here_ref, rank_ref, gate_ref, weight_ref, *refs):
    count = 2 * len(slots)
    blocks, refs = refs[:count], refs[count + held:]
    z_ref, back_ref, sibling_ref, z_scratch, back_scratch, z_sem, back_sem = refs
    sources = lane_sources(here_ref[0], slots, here_ref[0] % 2)
    for i, source in enumerate(sources):
        chosen = [chosen_rows(rank_ref, side, source, capacity) for side in range(2)]
        gates = [gate_column(gate_ref, chosen[side], side, source) for side in range(2)]
        both = jnp.concatenate([one_hot(chosen[0]), one_hot(chosen[1])], axis=0)
        rows = jnp.dot(both, blocks[i][...], preferred_element_type=F32)
        z_scratch[i] = (rows[:capacity] * gates[0]).astype(BF16)
        sibling_ref[i] = (rows[capacity:] * gates[1]).astype(BF16)
    copies = place_out([(z_scratch.at[i], z_ref.at[source]) for i, source in enumerate(sources)], z_sem)
    flat = z_scratch[...].reshape(count * capacity, z_scratch.shape[2])
    back = lax.dot_general(flat, weight_ref[...], (((1,), (1,)), ((), ())), preferred_element_type=F32)
    back_scratch[...] = back.astype(BF16).reshape(back_scratch.shape)
    copies += place_out([(back_scratch.at[i], back_ref.at[source]) for i, source in enumerate(sources)], back_sem)
    for copy in copies:
        copy.wait()


def scaled_rows(here, rank, gate, weight, blocks, slots, capacity, buffers):
    devices = rank.shape[1]
    hidden, width = weight.shape
    count = len(blocks)
    tokens = blocks[0].shape[0]
    vmem, anywhere = pl.BlockSpec(memory_space=pltpu.VMEM), pl.BlockSpec(memory_space=pl.ANY)
    return pl.pallas_call(
        functools.partial(scale_kernel, capacity, slots, len(buffers)),
        in_specs=[pl.BlockSpec(memory_space=pltpu.SMEM)] + [vmem] * (3 + count) + [anywhere] * len(buffers),
        out_specs=[anywhere, anywhere, vmem],
        out_shape=[
            jax.ShapeDtypeStruct((devices, capacity, width), BF16),
            jax.ShapeDtypeStruct((devices, capacity, hidden), BF16),
            jax.ShapeDtypeStruct((count, capacity, width), BF16),
        ],
        scratch_shapes=[
            pltpu.VMEM((count, capacity, width), BF16),
            pltpu.VMEM((count, capacity, hidden), BF16),
            pltpu.SemaphoreType.DMA((count,)),
            pltpu.SemaphoreType.DMA((count,)),
        ],
        input_output_aliases={4 + count + i: i for i in range(len(buffers))},
        compiler_params=pltpu.CompilerParams(vmem_limit_bytes=40 * MIB),
        cost_estimate=pl.CostEstimate(
            flops=2 * count * capacity * width * (hidden + 2 * tokens), transcendentals=0,
            bytes_accessed=2 * count * (tokens * width + capacity * (2 * width + hidden)) + 2 * width * hidden,
        ),
        name="scaled_rows",
    )(here, rank, gate, weight, *blocks, *buffers)


def sibling_kernel(capacity, slots, here_ref, weight_ref, rows_ref, _z, _back, z_ref, back_ref, back_scratch, z_sem, back_sem):
    count = 2 * len(slots)
    sources = lane_sources(here_ref[0], slots, 1 - here_ref[0] % 2)
    copies = place_out([(rows_ref.at[i], z_ref.at[source]) for i, source in enumerate(sources)], z_sem)
    flat = rows_ref[...].reshape(count * capacity, rows_ref.shape[2])
    back = lax.dot_general(flat, weight_ref[...], (((1,), (1,)), ((), ())), preferred_element_type=F32)
    back_scratch[...] = back.astype(BF16).reshape(back_scratch.shape)
    copies += place_out([(back_scratch.at[i], back_ref.at[source]) for i, source in enumerate(sources)], back_sem)
    for copy in copies:
        copy.wait()


def sibling_rows(here, weight, rows, slots, z_rows, back):
    count, capacity, width = rows.shape
    hidden = weight.shape[0]
    vmem, anywhere = pl.BlockSpec(memory_space=pltpu.VMEM), pl.BlockSpec(memory_space=pl.ANY)
    return pl.pallas_call(
        functools.partial(sibling_kernel, capacity, slots),
        in_specs=[pl.BlockSpec(memory_space=pltpu.SMEM), vmem, vmem, anywhere, anywhere],
        out_specs=[anywhere, anywhere],
        out_shape=[jax.ShapeDtypeStruct(z_rows.shape, BF16), jax.ShapeDtypeStruct(back.shape, BF16)],
        scratch_shapes=[
            pltpu.VMEM((count, capacity, hidden), BF16),
            pltpu.SemaphoreType.DMA((count,)),
            pltpu.SemaphoreType.DMA((count,)),
        ],
        input_output_aliases={3: 0, 4: 1},
        compiler_params=pltpu.CompilerParams(vmem_limit_bytes=40 * MIB),
        cost_estimate=pl.CostEstimate(
            flops=2 * count * capacity * width * hidden, transcendentals=0,
            bytes_accessed=2 * count * capacity * (2 * width + hidden) + 2 * width * hidden,
        ),
        name="sibling_rows",
    )(here, weight, rows, z_rows, back)


def forward_kernel(capacity, turn, here_ref, rank_ref, gate_ref, h_ref, weight_ref, out_ref):
    each = out_ref.shape[0]
    lane = (here_ref[0] % 2) ^ turn
    flat = h_ref[...].reshape(each * capacity, h_ref.shape[3])
    out = jnp.dot(flat, weight_ref[...], preferred_element_type=F32).astype(BF16).astype(F32)
    for j in range(each):
        source = (pl.program_id(0) * each + j) * 2 + lane
        gate = gate_column(gate_ref, chosen_rows(rank_ref, 0, source, capacity), 0, source)
        out_ref[j] = (out[j * capacity:(j + 1) * capacity, :] * gate).astype(BF16)


def forward_rows(here, rank, gate, rows_h, weight, turn, each=4):
    devices, capacity, hidden = rows_h.shape
    width = weight.shape[1]
    whole = pl.BlockSpec(rank.shape, lambda i, here: (0, 0, 0))
    return pl.pallas_call(
        functools.partial(forward_kernel, capacity, turn),
        grid_spec=pltpu.PrefetchScalarGridSpec(
            num_scalar_prefetch=1,
            grid=(devices // 2 // each,),
            in_specs=[
                whole,
                whole,
                pl.BlockSpec((each, 1, capacity, hidden), lambda i, here: (i, (here[0] % 2) ^ turn, 0, 0)),
                pl.BlockSpec((hidden, width), lambda i, here: (0, 0)),
            ],
            out_specs=pl.BlockSpec((each, capacity, width), lambda i, here: (i, 0, 0)),
        ),
        out_shape=jax.ShapeDtypeStruct((devices // 2, capacity, width), BF16),
        compiler_params=pltpu.CompilerParams(vmem_limit_bytes=40 * MIB),
        cost_estimate=pl.CostEstimate(
            flops=devices * capacity * width * hidden, transcendentals=0,
            bytes_accessed=devices * capacity * (width + hidden) + 2 * width * hidden,
        ),
        name="forward_rows",
    )(here, rank, gate, rows_h.reshape(devices // 2, 2, capacity, hidden), weight)


ORDER = (3, 2, 1, 0)


def sum_kernel(capacity, turn, here_ref, rank_ref, own_ref, other_ref, *part_refs):
    for step, slot in enumerate(ORDER):

        @pl.when(pl.program_id(0) == step)
        def _():
            source = lane_sources(here_ref[0], (slot,), here_ref[0] % 2)[turn]
            both = [one_hot(chosen_rows(rank_ref, side, source, capacity)) for side in range(2)]
            rows = jnp.concatenate([own_ref[0], other_ref[0]], axis=0)
            part = lax.dot_general(
                jnp.concatenate(both, axis=0), rows, (((0,), (0,)), ((), ())), preferred_element_type=F32
            )
            part_refs[step][...] = part.astype(BF16)


def summed(here, rank, own, other, turn):
    _, capacity, width = own.shape
    tokens = rank.shape[2]

    def block(i, here):
        place = jnp.int32(0)
        for step, slot in enumerate(ORDER):
            place = jnp.where(i == step, lane_sources(here[0], (slot,), 0)[turn] // 2, place)
        return (place, 0, 0)

    return pl.pallas_call(
        functools.partial(sum_kernel, capacity, turn),
        grid_spec=pltpu.PrefetchScalarGridSpec(
            num_scalar_prefetch=1,
            grid=(len(ORDER),),
            in_specs=[
                pl.BlockSpec(rank.shape, lambda i, here: (0, 0, 0)),
                pl.BlockSpec((1, capacity, width), block),
                pl.BlockSpec((1, capacity, width), block),
            ],
            out_specs=[pl.BlockSpec((tokens, width), lambda i, here: (0, 0))] * len(ORDER),
        ),
        out_shape=[jax.ShapeDtypeStruct((tokens, width), BF16)] * len(ORDER),
        compiler_params=pltpu.CompilerParams(vmem_limit_bytes=40 * MIB),
        cost_estimate=pl.CostEstimate(
            flops=16 * tokens * capacity * width, transcendentals=0,
            bytes_accessed=8 * width * (tokens + 2 * capacity),
        ),
        name="summed",
    )(here, rank, own, other)


def added(*values):
    total = values[0].astype(F32)
    for value in values[1:]:
        total = total + value.astype(F32)
    return total.astype(BF16)


def passed(pairs, value):
    return lax.ppermute(value, "expert", [(a * 4 + lane, b * 4 + lane) for a, b in pairs for lane in range(4)])


def swapped_with(value, bit):
    devices = lax.axis_size("expert")
    return lax.ppermute(value, "expert", [(i, i ^ bit) for i in range(devices)])


OUTER, INNER = ((0, 1), (3, 2)), ((1, 2), (2, 1))
ENDS, ENDS_SWAP = ((1, 0), (2, 3)), ((0, 3), (3, 0))


def dense_shards(h_rows, gates, expert_ids, cotangent, down_weight, swapped):
    devices = lax.axis_size("expert")
    here = lax.axis_index("expert").reshape(1)
    tokens, top, hidden = h_rows.shape
    capacity = min(tokens, 3 * tokens * top // (2 * devices))
    weight = down_weight[0]
    slot_ids = slots_of(expert_ids, swapped, devices)
    h_flat = h_rows.reshape(-1, hidden)

    routing = jnp.concatenate([slot_ids.T.astype(F32), gates.T], axis=0)
    routing = jnp.broadcast_to(routing, (devices,) + routing.shape)
    routing = lax.all_to_all(routing, "expert", split_axis=0, concat_axis=0, tiled=True)
    rank, gate = route(here, routing, top)

    own = cotangent
    from_end, from_inner, from_near_end = passed(OUTER, own), passed(INNER, own), passed(ENDS, own)
    from_far_end = passed(ENDS_SWAP, own)
    own_y = swapped_with(own, 2)
    from_end, from_inner, from_near_end, from_far_end, own_y = lax.optimization_barrier(
        (from_end, from_inner, from_near_end, from_far_end, own_y)
    )
    near, last = added(from_inner, from_near_end), added(from_end, from_far_end)
    middle_inner, middle_end = passed(INNER, from_end), passed(ENDS, from_inner)
    near_y, last_y = swapped_with(near, 2), swapped_with(last, 2)
    middle = added(middle_inner, middle_end)
    middle_y = swapped_with(middle, 2)

    place, send_h = pack(slot_ids.reshape(1, -1), h_flat, devices, capacity)
    send_h, middle = lax.optimization_barrier((send_h, middle))
    rows_h = lax.all_to_all(
        send_h.reshape(devices, capacity, hidden), "expert", split_axis=0, concat_axis=0, tiled=True
    )

    z_rows, back, sibling = scaled_rows(here, rank, gate, weight, [own, own_y, near, near_y], (0, 1), capacity, [])
    sibling = swapped_with(sibling, 1)
    z_rows, back, sibling_last = scaled_rows(
        here, rank, gate, weight, [middle, middle_y, last, last_y], (2, 3), capacity, [z_rows, back]
    )
    sibling_last = swapped_with(sibling_last, 1)
    z_rows, back = sibling_rows(here, weight, sibling, (0, 1), z_rows, back)
    z_rows, back = sibling_rows(here, weight, sibling_last, (2, 3), z_rows, back)
    back_rows = lax.all_to_all(back, "expert", split_axis=0, concat_axis=0, tiled=True).reshape(-1, hidden)

    rows_h, _ = lax.optimization_barrier((rows_h, back))
    other = swapped_with(forward_rows(here, rank, gate, rows_h, weight, 1), 1)
    mine = forward_rows(here, rank, gate, rows_h, weight, 0)
    across = [swapped_with(part, 2) for part in summed(here, rank, mine, other, 1)]
    beside = summed(here, rank, mine, other, 0)
    far, mid, close, kept = zip(beside, across)
    far, mid, close = added(*far), added(*mid), added(*close)
    ends = passed(ENDS_SWAP, far)
    mid_outer, mid_inner = passed(OUTER, mid), passed(INNER, mid)
    close_outer = passed(OUTER, close)
    close_inner = passed(INNER, added(close, mid_outer))
    far_ends = passed(ENDS, added(far, mid_inner))
    mixed = added(*kept, ends, close_outer, close_inner, far_ends)

    grad_sum = lax.dot_general(flat_h, flat_z, (((0,), (0,)), ((), ())), preferred_element_type=F32)
    back = lax.dot_general(flat_z, weight, (((1,), (1,)), ((), ())), preferred_element_type=F32).astype(BF16)
    back_rows = lax.all_to_all(
        back.reshape(devices, capacity, hidden), "expert", split_axis=0, concat_axis=0, tiled=True
    )
    h_grad = back_rows[flat_ids, ranks].reshape(tokens_here, top_count, hidden)
    return (mixed, gate_grad, h_grad, grad_sum.astype(BF16)[None])


def upper(size):
    rows = lax.broadcasted_iota(jnp.int32, (size, size), 0)
    columns = lax.broadcasted_iota(jnp.int32, (size, size), 1)
    return (rows < columns).astype(F32).astype(BF16)


def pack_kernel(devices, capacity, ids_ref, h_ref, place_ref, sent_ref, place_scratch):
    pairs = ids_ref.shape[1]
    rows = sent_ref.shape[0]

    @pl.when(pl.program_id(0) == 0)
    def _():
        before = jnp.zeros((devices, 1), F32)
        for tile in range(pairs // 128):
            ids = ids_ref[:, tile * 128:(tile + 1) * 128]
            named = lax.broadcasted_iota(jnp.int32, (devices, 128), 0) == ids
            ones = jnp.where(named, 1.0, 0.0)
            rank = jnp.dot(ones.astype(BF16), upper(128), preferred_element_type=F32) + before
            before = before + jnp.sum(ones, axis=1, keepdims=True)
            rank = jnp.sum(jnp.where(named, rank, 0.0), axis=0, keepdims=True)
            place_scratch[:, tile * 128:(tile + 1) * 128] = ids * capacity + rank.astype(jnp.int32)
        place_ref[...] = place_scratch[...]

    first = pl.program_id(0) * rows
    wanted = lax.broadcasted_iota(jnp.int32, (rows, pairs), 0) + first
    chosen = jnp.where(wanted == place_scratch[...], 1.0, 0.0).astype(BF16)
    sent_ref[...] = jnp.dot(chosen, h_ref[...], preferred_element_type=F32).astype(BF16)


def pack(ids, h_flat, devices, capacity, steps=4):
    pairs, hidden = h_flat.shape
    rows = devices * capacity // steps
    return pl.pallas_call(
        functools.partial(pack_kernel, devices, capacity),
        grid=(steps,),
        in_specs=[
            pl.BlockSpec((1, pairs), lambda i: (0, 0)),
            pl.BlockSpec((pairs, hidden), lambda i: (0, 0)),
        ],
        out_specs=[
            pl.BlockSpec((1, pairs), lambda i: (0, 0)),
            pl.BlockSpec((rows, hidden), lambda i: (i, 0)),
        ],
        out_shape=[
            jax.ShapeDtypeStruct((1, pairs), jnp.int32),
            jax.ShapeDtypeStruct((devices * capacity, hidden), BF16),
        ],
        scratch_shapes=[pltpu.VMEM((1, pairs), jnp.int32)],
        compiler_params=pltpu.CompilerParams(vmem_limit_bytes=48 * MIB),
        cost_estimate=pl.CostEstimate(
            flops=2 * devices * capacity * pairs * hidden, transcendentals=0,
            bytes_accessed=2 * hidden * (pairs + devices * capacity),
        ),
        name="pack",
    )(ids, h_flat)


def unpack_kernel(slots, place_ref, gate_ref, h_ref, back_ref, grad_ref, gate_grad_ref):
    rows = place_ref.shape[0]
    chosen = lax.broadcasted_iota(jnp.int32, (rows, slots), 1) == place_ref[...]
    grad = jnp.dot(jnp.where(chosen, 1.0, 0.0).astype(BF16), back_ref[...], preferred_element_type=F32)
    grad_ref[...] = grad.astype(BF16)
    gate_grad_ref[...] = jnp.sum(grad * h_ref[...].astype(F32), axis=1, keepdims=True) / gate_ref[...]


def unpack(place, gates, h_flat, back_rows, steps=4):
    pairs, hidden = h_flat.shape
    slots = back_rows.shape[0]
    rows = pairs // steps
    return pl.pallas_call(
        functools.partial(unpack_kernel, slots),
        grid=(steps,),
        in_specs=[
            pl.BlockSpec((rows, 1), lambda i: (i, 0)),
            pl.BlockSpec((rows, 1), lambda i: (i, 0)),
            pl.BlockSpec((rows, hidden), lambda i: (i, 0)),
            pl.BlockSpec((slots, hidden), lambda i: (0, 0)),
        ],
        out_specs=[
            pl.BlockSpec((rows, hidden), lambda i: (i, 0)),
            pl.BlockSpec((rows, 1), lambda i: (i, 0)),
        ],
        out_shape=[
            jax.ShapeDtypeStruct((pairs, hidden), BF16),
            jax.ShapeDtypeStruct((pairs, 1), F32),
        ],
        compiler_params=pltpu.CompilerParams(vmem_limit_bytes=48 * MIB),
        cost_estimate=pl.CostEstimate(
            flops=2 * slots * pairs * hidden, transcendentals=0,
            bytes_accessed=2 * hidden * (2 * pairs + slots),
        ),
        name="unpack",
    )(place, gates, h_flat, back_rows)


def line_slots(position):
    near = jnp.minimum(position, 3 - position)
    turned = (near, near + 1, near + 2, 3 - 3 * near)
    return [jnp.where(position < 2, slot, 3 - slot) for slot in turned]


def route_kernel(devices, top, here_ref, routing_ref, rank_ref, gate_ref):
    for side in range(2):
        mine = (here_ref[0] ^ side).astype(F32)
        marks, picked = [], []
        for source in range(devices):
            ids = routing_ref[source, :top, :]
            gates = routing_ref[source, top:, :]
            named = ids == mine
            marks.append(jnp.sum(jnp.where(named, 1.0, 0.0), axis=0, keepdims=True))
            picked.append(jnp.sum(jnp.where(named, gates, 0.0), axis=0, keepdims=True))
        mark = jnp.concatenate(marks, axis=0)
        rank = jnp.dot(mark.astype(BF16), upper(mark.shape[1]), preferred_element_type=F32)
        rank_ref[side] = jnp.where(mark > 0, rank, -1.0).astype(jnp.int32)
        gate_ref[side] = jnp.concatenate(picked, axis=0)


def route(here, routing, top):
    devices, _, tokens = routing.shape
    return pl.pallas_call(
        functools.partial(route_kernel, devices, top),
        in_specs=[pl.BlockSpec(memory_space=pltpu.SMEM), pl.BlockSpec(memory_space=pltpu.VMEM)],
        out_specs=[pl.BlockSpec(memory_space=pltpu.VMEM)] * 2,
        out_shape=[
            jax.ShapeDtypeStruct((2, devices, tokens), jnp.int32),
            jax.ShapeDtypeStruct((2, devices, tokens), F32),
        ],
        cost_estimate=pl.CostEstimate(flops=1 << 21, transcendentals=0, bytes_accessed=1 << 19),
        name="route",
    )(here, routing)


def chosen_rows(rank_ref, side, source, capacity):
    rank = rank_ref[side, pl.ds(source, 1), :]
    return lax.broadcasted_iota(jnp.int32, (capacity, rank.shape[1]), 0) == rank


def gate_column(gate_ref, chosen, side, source):
    return jnp.sum(jnp.where(chosen, gate_ref[side, pl.ds(source, 1), :], 0.0), axis=1, keepdims=True)


def one_hot(chosen):
    return jnp.where(chosen, 1.0, 0.0).astype(BF16)


def lane_sources(here, slots, lane):
    line, across = here // 4, (here // 2) % 2
    places = line_slots(line)
    return [places[slot] * 4 + (across ^ turn) * 2 + lane for slot in slots for turn in range(2)]


def place_out(pieces, sem):
    copies = [pltpu.make_async_copy(source, target, sem.at[i]) for i, (source, target) in enumerate(pieces)]
    for copy in copies:
        copy.start()
    return copies


def scale_kernel(capacity, slots, held, here_ref, rank_ref, gate_ref, weight_ref, *refs):
    count = 2 * len(slots)
    blocks, refs = refs[:count], refs[count + held:]
    z_ref, back_ref, sibling_ref, z_scratch, back_scratch, z_sem, back_sem = refs
    sources = lane_sources(here_ref[0], slots, here_ref[0] % 2)
    for i, source in enumerate(sources):
        chosen = [chosen_rows(rank_ref, side, source, capacity) for side in range(2)]
        gates = [gate_column(gate_ref, chosen[side], side, source) for side in range(2)]
        both = jnp.concatenate([one_hot(chosen[0]), one_hot(chosen[1])], axis=0)
        rows = jnp.dot(both, blocks[i][...], preferred_element_type=F32)
        z_scratch[i] = (rows[:capacity] * gates[0]).astype(BF16)
        sibling_ref[i] = (rows[capacity:] * gates[1]).astype(BF16)
    copies = place_out([(z_scratch.at[i], z_ref.at[source]) for i, source in enumerate(sources)], z_sem)
    flat = z_scratch[...].reshape(count * capacity, z_scratch.shape[2])
    back = lax.dot_general(flat, weight_ref[...], (((1,), (1,)), ((), ())), preferred_element_type=F32)
    back_scratch[...] = back.astype(BF16).reshape(back_scratch.shape)
    copies += place_out([(back_scratch.at[i], back_ref.at[source]) for i, source in enumerate(sources)], back_sem)
    for copy in copies:
        copy.wait()


def scaled_rows(here, rank, gate, weight, blocks, slots, capacity, buffers):
    devices = rank.shape[1]
    hidden, width = weight.shape
    count = len(blocks)
    tokens = blocks[0].shape[0]
    vmem, anywhere = pl.BlockSpec(memory_space=pltpu.VMEM), pl.BlockSpec(memory_space=pl.ANY)
    return pl.pallas_call(
        functools.partial(scale_kernel, capacity, slots, len(buffers)),
        in_specs=[pl.BlockSpec(memory_space=pltpu.SMEM)] + [vmem] * (3 + count) + [anywhere] * len(buffers),
        out_specs=[anywhere, anywhere, vmem],
        out_shape=[
            jax.ShapeDtypeStruct((devices, capacity, width), BF16),
            jax.ShapeDtypeStruct((devices, capacity, hidden), BF16),
            jax.ShapeDtypeStruct((count, capacity, width), BF16),
        ],
        scratch_shapes=[
            pltpu.VMEM((count, capacity, width), BF16),
            pltpu.VMEM((count, capacity, hidden), BF16),
            pltpu.SemaphoreType.DMA((count,)),
            pltpu.SemaphoreType.DMA((count,)),
        ],
        input_output_aliases={4 + count + i: i for i in range(len(buffers))},
        compiler_params=pltpu.CompilerParams(vmem_limit_bytes=40 * MIB),
        cost_estimate=pl.CostEstimate(
            flops=2 * count * capacity * width * (hidden + 2 * tokens), transcendentals=0,
            bytes_accessed=2 * count * (tokens * width + capacity * (2 * width + hidden)) + 2 * width * hidden,
        ),
        name="scaled_rows",
    )(here, rank, gate, weight, *blocks, *buffers)


def sibling_kernel(capacity, slots, here_ref, weight_ref, rows_ref, _z, _back, z_ref, back_ref, back_scratch, z_sem, back_sem):
    count = 2 * len(slots)
    sources = lane_sources(here_ref[0], slots, 1 - here_ref[0] % 2)
    copies = place_out([(rows_ref.at[i], z_ref.at[source]) for i, source in enumerate(sources)], z_sem)
    flat = rows_ref[...].reshape(count * capacity, rows_ref.shape[2])
    back = lax.dot_general(flat, weight_ref[...], (((1,), (1,)), ((), ())), preferred_element_type=F32)
    back_scratch[...] = back.astype(BF16).reshape(back_scratch.shape)
    copies += place_out([(back_scratch.at[i], back_ref.at[source]) for i, source in enumerate(sources)], back_sem)
    for copy in copies:
        copy.wait()


def sibling_rows(here, weight, rows, slots, z_rows, back):
    count, capacity, width = rows.shape
    hidden = weight.shape[0]
    vmem, anywhere = pl.BlockSpec(memory_space=pltpu.VMEM), pl.BlockSpec(memory_space=pl.ANY)
    return pl.pallas_call(
        functools.partial(sibling_kernel, capacity, slots),
        in_specs=[pl.BlockSpec(memory_space=pltpu.SMEM), vmem, vmem, anywhere, anywhere],
        out_specs=[anywhere, anywhere],
        out_shape=[jax.ShapeDtypeStruct(z_rows.shape, BF16), jax.ShapeDtypeStruct(back.shape, BF16)],
        scratch_shapes=[
            pltpu.VMEM((count, capacity, hidden), BF16),
            pltpu.SemaphoreType.DMA((count,)),
            pltpu.SemaphoreType.DMA((count,)),
        ],
        input_output_aliases={3: 0, 4: 1},
        compiler_params=pltpu.CompilerParams(vmem_limit_bytes=40 * MIB),
        cost_estimate=pl.CostEstimate(
            flops=2 * count * capacity * width * hidden, transcendentals=0,
            bytes_accessed=2 * count * capacity * (2 * width + hidden) + 2 * width * hidden,
        ),
        name="sibling_rows",
    )(here, weight, rows, z_rows, back)


def forward_kernel(capacity, turn, here_ref, rank_ref, gate_ref, h_ref, weight_ref, out_ref):
    each = out_ref.shape[0]
    lane = (here_ref[0] % 2) ^ turn
    flat = h_ref[...].reshape(each * capacity, h_ref.shape[3])
    out = jnp.dot(flat, weight_ref[...], preferred_element_type=F32).astype(BF16).astype(F32)
    for j in range(each):
        source = (pl.program_id(0) * each + j) * 2 + lane
        gate = gate_column(gate_ref, chosen_rows(rank_ref, 0, source, capacity), 0, source)
        out_ref[j] = (out[j * capacity:(j + 1) * capacity, :] * gate).astype(BF16)


def forward_rows(here, rank, gate, rows_h, weight, turn, each=4):
    devices, capacity, hidden = rows_h.shape
    width = weight.shape[1]
    whole = pl.BlockSpec(rank.shape, lambda i, here: (0, 0, 0))
    return pl.pallas_call(
        functools.partial(forward_kernel, capacity, turn),
        grid_spec=pltpu.PrefetchScalarGridSpec(
            num_scalar_prefetch=1,
            grid=(devices // 2 // each,),
            in_specs=[
                whole,
                whole,
                pl.BlockSpec((each, 1, capacity, hidden), lambda i, here: (i, (here[0] % 2) ^ turn, 0, 0)),
                pl.BlockSpec((hidden, width), lambda i, here: (0, 0)),
            ],
            out_specs=pl.BlockSpec((each, capacity, width), lambda i, here: (i, 0, 0)),
        ),
        out_shape=jax.ShapeDtypeStruct((devices // 2, capacity, width), BF16),
        compiler_params=pltpu.CompilerParams(vmem_limit_bytes=40 * MIB),
        cost_estimate=pl.CostEstimate(
            flops=devices * capacity * width * hidden, transcendentals=0,
            bytes_accessed=devices * capacity * (width + hidden) + 2 * width * hidden,
        ),
        name="forward_rows",
    )(here, rank, gate, rows_h.reshape(devices // 2, 2, capacity, hidden), weight)


ORDER = (3, 2, 1, 0)


def sum_kernel(capacity, turn, here_ref, rank_ref, own_ref, other_ref, *part_refs):
    for step, slot in enumerate(ORDER):

        @pl.when(pl.program_id(0) == step)
        def _():
            source = lane_sources(here_ref[0], (slot,), here_ref[0] % 2)[turn]
            both = [one_hot(chosen_rows(rank_ref, side, source, capacity)) for side in range(2)]
            rows = jnp.concatenate([own_ref[0], other_ref[0]], axis=0)
            part = lax.dot_general(
                jnp.concatenate(both, axis=0), rows, (((0,), (0,)), ((), ())), preferred_element_type=F32
            )
            part_refs[step][...] = part.astype(BF16)


def summed(here, rank, own, other, turn):
    _, capacity, width = own.shape
    tokens = rank.shape[2]

    def block(i, here):
        place = jnp.int32(0)
        for step, slot in enumerate(ORDER):
            place = jnp.where(i == step, lane_sources(here[0], (slot,), 0)[turn] // 2, place)
        return (place, 0, 0)

    return pl.pallas_call(
        functools.partial(sum_kernel, capacity, turn),
        grid_spec=pltpu.PrefetchScalarGridSpec(
            num_scalar_prefetch=1,
            grid=(len(ORDER),),
            in_specs=[
                pl.BlockSpec(rank.shape, lambda i, here: (0, 0, 0)),
                pl.BlockSpec((1, capacity, width), block),
                pl.BlockSpec((1, capacity, width), block),
            ],
            out_specs=[pl.BlockSpec((tokens, width), lambda i, here: (0, 0))] * len(ORDER),
        ),
        out_shape=[jax.ShapeDtypeStruct((tokens, width), BF16)] * len(ORDER),
        compiler_params=pltpu.CompilerParams(vmem_limit_bytes=40 * MIB),
        cost_estimate=pl.CostEstimate(
            flops=16 * tokens * capacity * width, transcendentals=0,
            bytes_accessed=8 * width * (tokens + 2 * capacity),
        ),
        name="summed",
    )(here, rank, own, other)


def added(*values):
    total = values[0].astype(F32)
    for value in values[1:]:
        total = total + value.astype(F32)
    return total.astype(BF16)


def passed(pairs, value):
    return lax.ppermute(value, "expert", [(a * 4 + lane, b * 4 + lane) for a, b in pairs for lane in range(4)])


def swapped_with(value, bit):
    devices = lax.axis_size("expert")
    return lax.ppermute(value, "expert", [(i, i ^ bit) for i in range(devices)])


OUTER, INNER = ((0, 1), (3, 2)), ((1, 2), (2, 1))
ENDS, ENDS_SWAP = ((1, 0), (2, 3)), ((0, 3), (3, 0))


def dense_shards(h_rows, gates, expert_ids, cotangent, down_weight, swapped):
    devices = lax.axis_size("expert")
    here = lax.axis_index("expert").reshape(1)
    tokens, top, hidden = h_rows.shape
    capacity = min(tokens, 3 * tokens * top // (2 * devices))
    weight = down_weight[0]
    slot_ids = slots_of(expert_ids, swapped, devices)
    h_flat = h_rows.reshape(-1, hidden)

    routing = jnp.concatenate([slot_ids.T.astype(F32), gates.T], axis=0)
    routing = jnp.broadcast_to(routing, (devices,) + routing.shape)
    routing = lax.all_to_all(routing, "expert", split_axis=0, concat_axis=0, tiled=True)
    rank, gate = route(here, routing, top)

    own = cotangent
    from_end, from_inner, from_near_end = passed(OUTER, own), passed(INNER, own), passed(ENDS, own)
    from_far_end = passed(ENDS_SWAP, own)
    own_y = swapped_with(own, 2)
    from_end, from_inner, from_near_end, from_far_end, own_y = lax.optimization_barrier(
        (from_end, from_inner, from_near_end, from_far_end, own_y)
    )
    near, last = added(from_inner, from_near_end), added(from_end, from_far_end)
    middle_inner, middle_end = passed(INNER, from_end), passed(ENDS, from_inner)
    near_y, last_y = swapped_with(near, 2), swapped_with(last, 2)
    middle = added(middle_inner, middle_end)
    middle_y = swapped_with(middle, 2)

    place, send_h = pack(slot_ids.reshape(1, -1), h_flat, devices, capacity)
    send_h, middle = lax.optimization_barrier((send_h, middle))
    rows_h = lax.all_to_all(
        send_h.reshape(devices, capacity, hidden), "expert", split_axis=0, concat_axis=0, tiled=True
    )

    z_rows, back, sibling = scaled_rows(here, rank, gate, weight, [own, own_y, near, near_y], (0, 1), capacity, [])
    sibling = swapped_with(sibling, 1)
    z_rows, back, sibling_last = scaled_rows(
        here, rank, gate, weight, [middle, middle_y, last, last_y], (2, 3), capacity, [z_rows, back]
    )
    sibling_last = swapped_with(sibling_last, 1)
    z_rows, back = sibling_rows(here, weight, sibling, (0, 1), z_rows, back)
    z_rows, back = sibling_rows(here, weight, sibling_last, (2, 3), z_rows, back)
    back_rows = lax.all_to_all(back, "expert", split_axis=0, concat_axis=0, tiled=True).reshape(-1, hidden)

    rows_h, _ = lax.optimization_barrier((rows_h, back))
    other = swapped_with(forward_rows(here, rank, gate, rows_h, weight, 1), 1)
    mine = forward_rows(here, rank, gate, rows_h, weight, 0)
    across = [swapped_with(part, 2) for part in summed(here, rank, mine, other, 1)]
    beside = summed(here, rank, mine, other, 0)
    far, mid, close, kept = zip(beside, across)
    outer1 = passed(OUTER, added(*far))
    mid = added(*mid, outer1)
    outer2, inner2 = passed(OUTER, mid), passed(INNER, mid)
    close = added(*close, outer2)
    outer3, inner3 = passed(OUTER, close), passed(INNER, close)
    ends3 = passed(ENDS, added(*far, inner2))
    mixed = added(*kept, outer3, inner3, ends3)

    grad_sum = lax.dot_general(
        rows_h.reshape(-1, hidden), z_rows.reshape(devices * capacity, -1), (((0,), (0,)), ((), ())),
        preferred_element_type=F32,
    )
    h_grad, gate_grad = unpack(place.reshape(-1, 1), gates.reshape(-1, 1), h_flat, back_rows)
    return (
        mixed,
        gate_grad.reshape(tokens, top),
        h_grad.reshape(tokens, top, hidden),
        grad_sum.astype(BF16)[None],
    )


def shards(h_rows, *rest):
    devices = lax.axis_size("expert")
    dense = devices == 16 and devices <= 2 * h_rows.shape[1]
    return (dense_shards if dense else sparse_shards)(h_rows, *rest)


def solution(mesh):
    in_specs = (
        P(("groups", "expert"), None, None),
        P(("groups", "expert"), None),
        P(("groups", "expert"), None),
        P(("groups", "expert"), None),
        P("expert", None, None),
        P(),
    )
    out_specs = (
        P(("groups", "expert"), None),
        P(("groups", "expert"), None),
        P(("groups", "expert"), None, None),
        P(("groups", "expert"), None, None),
    )
    return jax.shard_map(shards, mesh=mesh, in_specs=in_specs, out_specs=out_specs, check_vma=False)
```

```python
import functools

import jax
import jax.numpy as jnp
from jax import lax
from jax.experimental import pallas as pl
from jax.experimental.pallas import tpu as pltpu
from jax.sharding import PartitionSpec as P

F32 = jnp.float32
BF16 = jnp.bfloat16
MIB = 1 << 20


def slots_of(ids, swapped, devices):
    half_way = devices // 2
    table = jnp.arange(devices, dtype=jnp.int32)
    table = (table + half_way * swapped[table % half_way]) % devices
    return jnp.sum(jnp.where(ids[..., None] == jnp.arange(devices, dtype=jnp.int32), table, 0), axis=-1)


def place_rows(values, target, ranks, devices, capacity):
    buffer = jnp.zeros((devices, capacity, values.shape[-1]), values.dtype)
    return buffer.at[target, ranks].set(values)


def sparse_shards(h_rows, gates, expert_ids, cotangent, down_weight, swapped):
    devices = lax.axis_size("expert")
    tokens_here, top_count, hidden = h_rows.shape
    width = cotangent.shape[1]
    capacity = min(tokens_here, 3 * tokens_here * top_count // (2 * devices))
    experts = jnp.arange(devices, dtype=jnp.int32)
    weight = down_weight[0]
    flat_ids = slots_of(expert_ids.reshape(-1), swapped, devices)
    onehot = (flat_ids[:, None] == experts[None, :]).astype(jnp.int32)
    ranks = jnp.sum((jnp.cumsum(onehot, axis=0) - onehot) * onehot, axis=1)
    send_h = place_rows(h_rows.reshape(-1, hidden), flat_ids, ranks, devices, capacity)
    received = lax.all_to_all(send_h, "expert", split_axis=0, concat_axis=0, tiled=True)
    result = jnp.einsum("sch,hd->scd", received, weight, preferred_element_type=F32)
    results = result.astype(BF16)
    returned = lax.all_to_all(results, "expert", split_axis=0, concat_axis=0, tiled=True)
    out_rows = returned[flat_ids, ranks].reshape(tokens_here, top_count, width)
    mixed = jnp.einsum("tk,tkd->td", gates, out_rows.astype(F32)).astype(BF16)
    gate_grad = jnp.einsum("td,tkd->tk", cotangent, out_rows, preferred_element_type=F32)
    scaled = (gates[:, :, None] * cotangent[:, None, :].astype(F32)).astype(BF16)
    send_z = place_rows(scaled.reshape(-1, width), flat_ids, ranks, devices, capacity)
    recv_z = lax.all_to_all(send_z, "expert", split_axis=0, concat_axis=0, tiled=True)
    flat_z = recv_z.reshape(-1, width)
    flat_h = received.reshape(-1, hidden)
    grad_sum = lax.dot_general(flat_h, flat_z, (((0,), (0,)), ((), ())), preferred_element_type=F32)
    back = lax.dot_general(flat_z, weight, (((1,), (1,)), ((), ())), preferred_element_type=F32).astype(BF16)
    back_rows = lax.all_to_all(
        back.reshape(devices, capacity, hidden), "expert", split_axis=0, concat_axis=0, tiled=True
    )
    h_grad = back_rows[flat_ids, ranks].reshape(tokens_here, top_count, hidden)
    return (mixed, gate_grad, h_grad, grad_sum.astype(BF16)[None])


def upper(size):
    rows = lax.broadcasted_iota(jnp.int32, (size, size), 0)
    columns = lax.broadcasted_iota(jnp.int32, (size, size), 1)
    return (rows < columns).astype(F32).astype(BF16)


def pack_kernel(devices, capacity, ids_ref, h_ref, place_ref, sent_ref, place_scratch):
    pairs = ids_ref.shape[1]
    rows = sent_ref.shape[0]

    @pl.when(pl.program_id(0) == 0)
    def _():
        before = jnp.zeros((devices, 1), F32)
        for tile in range(pairs // 128):
            ids = ids_ref[:, tile * 128:(tile + 1) * 128]
            named = lax.broadcasted_iota(jnp.int32, (devices, 128), 0) == ids
            ones = jnp.where(named, 1.0, 0.0)
            rank = jnp.dot(ones.astype(BF16), upper(128), preferred_element_type=F32) + before
            before = before + jnp.sum(ones, axis=1, keepdims=True)
            rank = jnp.sum(jnp.where(named, rank, 0.0), axis=0, keepdims=True)
            place_scratch[:, tile * 128:(tile + 1) * 128] = ids * capacity + rank.astype(jnp.int32)
        place_ref[...] = place_scratch[...]

    first = pl.program_id(0) * rows
    wanted = lax.broadcasted_iota(jnp.int32, (rows, pairs), 0) + first
    chosen = jnp.where(wanted == place_scratch[...], 1.0, 0.0).astype(BF16)
    sent_ref[...] = jnp.dot(chosen, h_ref[...], preferred_element_type=F32).astype(BF16)


def pack(ids, h_flat, devices, capacity, steps=4):
    pairs, hidden = h_flat.shape
    rows = devices * capacity // steps
    return pl.pallas_call(
        functools.partial(pack_kernel, devices, capacity),
        grid=(steps,),
        in_specs=[
            pl.BlockSpec((1, pairs), lambda i: (0, 0)),
            pl.BlockSpec((pairs, hidden), lambda i: (0, 0)),
        ],
        out_specs=[
            pl.BlockSpec((1, pairs), lambda i: (0, 0)),
            pl.BlockSpec((rows, hidden), lambda i: (i, 0)),
        ],
        out_shape=[
            jax.ShapeDtypeStruct((1, pairs), jnp.int32),
            jax.ShapeDtypeStruct((devices * capacity, hidden), BF16),
        ],
        scratch_shapes=[pltpu.VMEM((1, pairs), jnp.int32)],
        compiler_params=pltpu.CompilerParams(vmem_limit_bytes=48 * MIB),
        cost_estimate=pl.CostEstimate(
            flops=2 * devices * capacity * pairs * hidden, transcendentals=0,
            bytes_accessed=2 * hidden * (pairs + devices * capacity),
        ),
        name="pack",
    )(ids, h_flat)


def unpack_kernel(slots, place_ref, gate_ref, h_ref, back_ref, grad_ref, gate_grad_ref):
    rows = place_ref.shape[0]
    chosen = lax.broadcasted_iota(jnp.int32, (rows, slots), 1) == place_ref[...]
    grad = jnp.dot(jnp.where(chosen, 1.0, 0.0).astype(BF16), back_ref[...], preferred_element_type=F32)
    grad_ref[...] = grad.astype(BF16)
    gate_grad_ref[...] = jnp.sum(grad * h_ref[...].astype(F32), axis=1, keepdims=True) / gate_ref[...]


def unpack(place, gates, h_flat, back_rows, steps=4):
    pairs, hidden = h_flat.shape
    slots = back_rows.shape[0]
    rows = pairs // steps
    return pl.pallas_call(
        functools.partial(unpack_kernel, slots),
        grid=(steps,),
        in_specs=[
            pl.BlockSpec((rows, 1), lambda i: (i, 0)),
            pl.BlockSpec((rows, 1), lambda i: (i, 0)),
            pl.BlockSpec((rows, hidden), lambda i: (i, 0)),
            pl.BlockSpec((slots, hidden), lambda i: (0, 0)),
        ],
        out_specs=[
            pl.BlockSpec((rows, hidden), lambda i: (i, 0)),
            pl.BlockSpec((rows, 1), lambda i: (i, 0)),
        ],
        out_shape=[
            jax.ShapeDtypeStruct((pairs, hidden), BF16),
            jax.ShapeDtypeStruct((pairs, 1), F32),
        ],
        compiler_params=pltpu.CompilerParams(vmem_limit_bytes=48 * MIB),
        cost_estimate=pl.CostEstimate(
            flops=2 * slots * pairs * hidden, transcendentals=0,
            bytes_accessed=2 * hidden * (2 * pairs + slots),
        ),
        name="unpack",
    )(place, gates, h_flat, back_rows)


def line_slots(position):
    near = jnp.minimum(position, 3 - position)
    turned = (near, near + 1, near + 2, 3 - 3 * near)
    return [jnp.where(position < 2, slot, 3 - slot) for slot in turned]


def route_kernel(devices, top, here_ref, routing_ref, rank_ref, gate_ref):
    for side in range(2):
        mine = (here_ref[0] ^ side).astype(F32)
        marks, picked = [], []
        for source in range(devices):
            ids = routing_ref[source, :top, :]
            gates = routing_ref[source, top:, :]
            named = ids == mine
            marks.append(jnp.sum(jnp.where(named, 1.0, 0.0), axis=0, keepdims=True))
            picked.append(jnp.sum(jnp.where(named, gates, 0.0), axis=0, keepdims=True))
        mark = jnp.concatenate(marks, axis=0)
        rank = jnp.dot(mark.astype(BF16), upper(mark.shape[1]), preferred_element_type=F32)
        rank_ref[side] = jnp.where(mark > 0, rank, -1.0).astype(jnp.int32)
        gate_ref[side] = jnp.concatenate(picked, axis=0)


def route(here, routing, top):
    devices, _, tokens = routing.shape
    return pl.pallas_call(
        functools.partial(route_kernel, devices, top),
        in_specs=[pl.BlockSpec(memory_space=pltpu.SMEM), pl.BlockSpec(memory_space=pltpu.VMEM)],
        out_specs=[pl.BlockSpec(memory_space=pltpu.VMEM)] * 2,
        out_shape=[
            jax.ShapeDtypeStruct((2, devices, tokens), jnp.int32),
            jax.ShapeDtypeStruct((2, devices, tokens), F32),
        ],
        cost_estimate=pl.CostEstimate(flops=1 << 21, transcendentals=0, bytes_accessed=1 << 19),
        name="route",
    )(here, routing)


def chosen_rows(rank_ref, side, source, capacity):
    rank = rank_ref[side, pl.ds(source, 1), :]
    return lax.broadcasted_iota(jnp.int32, (capacity, rank.shape[1]), 0) == rank


def gate_column(gate_ref, chosen, side, source):
    return jnp.sum(jnp.where(chosen, gate_ref[side, pl.ds(source, 1), :], 0.0), axis=1, keepdims=True)


def one_hot(chosen):
    return jnp.where(chosen, 1.0, 0.0).astype(BF16)


def lane_sources(here, slots, lane):
    line, across = here // 4, (here // 2) % 2
    places = line_slots(line)
    return [places[slot] * 4 + (across ^ turn) * 2 + lane for slot in slots for turn in range(2)]


def place_out(pieces, sem):
    copies = [pltpu.make_async_copy(source, target, sem.at[i]) for i, (source, target) in enumerate(pieces)]
    for copy in copies:
        copy.start()
    return copies


def scale_kernel(capacity, slots, held, here_ref, rank_ref, gate_ref, weight_ref, *refs):
    count = 2 * len(slots)
    blocks, refs = refs[:count], refs[count + held:]
    z_ref, back_ref, sibling_ref, z_scratch, back_scratch, z_sem, back_sem = refs
    sources = lane_sources(here_ref[0], slots, here_ref[0] % 2)
    for i, source in enumerate(sources):
        chosen = [chosen_rows(rank_ref, side, source, capacity) for side in range(2)]
        gates = [gate_column(gate_ref, chosen[side], side, source) for side in range(2)]
        both = jnp.concatenate([one_hot(chosen[0]), one_hot(chosen[1])], axis=0)
        rows = jnp.dot(both, blocks[i][...], preferred_element_type=F32)
        z_scratch[i] = (rows[:capacity] * gates[0]).astype(BF16)
        sibling_ref[i] = (rows[capacity:] * gates[1]).astype(BF16)
    copies = place_out([(z_scratch.at[i], z_ref.at[source]) for i, source in enumerate(sources)], z_sem)
    flat = z_scratch[...].reshape(count * capacity, z_scratch.shape[2])
    back = lax.dot_general(flat, weight_ref[...], (((1,), (1,)), ((), ())), preferred_element_type=F32)
    back_scratch[...] = back.astype(BF16).reshape(back_scratch.shape)
    copies += place_out([(back_scratch.at[i], back_ref.at[source]) for i, source in enumerate(sources)], back_sem)
    for copy in copies:
        copy.wait()


def scaled_rows(here, rank, gate, weight, blocks, slots, capacity, buffers):
    devices = rank.shape[1]
    hidden, width = weight.shape
    count = len(blocks)
    tokens = blocks[0].shape[0]
    vmem, anywhere = pl.BlockSpec(memory_space=pltpu.VMEM), pl.BlockSpec(memory_space=pl.ANY)
    return pl.pallas_call(
        functools.partial(scale_kernel, capacity, slots, len(buffers)),
        in_specs=[pl.BlockSpec(memory_space=pltpu.SMEM)] + [vmem] * (3 + count) + [anywhere] * len(buffers),
        out_specs=[anywhere, anywhere, vmem],
        out_shape=[
            jax.ShapeDtypeStruct((devices, capacity, width), BF16),
            jax.ShapeDtypeStruct((devices, capacity, hidden), BF16),
            jax.ShapeDtypeStruct((count, capacity, width), BF16),
        ],
        scratch_shapes=[
            pltpu.VMEM((count, capacity, width), BF16),
            pltpu.VMEM((count, capacity, hidden), BF16),
            pltpu.SemaphoreType.DMA((count,)),
            pltpu.SemaphoreType.DMA((count,)),
        ],
        input_output_aliases={4 + count + i: i for i in range(len(buffers))},
        compiler_params=pltpu.CompilerParams(vmem_limit_bytes=40 * MIB),
        cost_estimate=pl.CostEstimate(
            flops=2 * count * capacity * width * (hidden + 2 * tokens), transcendentals=0,
            bytes_accessed=2 * count * (tokens * width + capacity * (2 * width + hidden)) + 2 * width * hidden,
        ),
        name="scaled_rows",
    )(here, rank, gate, weight, *blocks, *buffers)


def sibling_kernel(capacity, slots, here_ref, weight_ref, rows_ref, _z, _back, z_ref, back_ref, back_scratch, z_sem, back_sem):
    count = 2 * len(slots)
    sources = lane_sources(here_ref[0], slots, 1 - here_ref[0] % 2)
    copies = place_out([(rows_ref.at[i], z_ref.at[source]) for i, source in enumerate(sources)], z_sem)
    flat = rows_ref[...].reshape(count * capacity, rows_ref.shape[2])
    back = lax.dot_general(flat, weight_ref[...], (((1,), (1,)), ((), ())), preferred_element_type=F32)
    back_scratch[...] = back.astype(BF16).reshape(back_scratch.shape)
    copies += place_out([(back_scratch.at[i], back_ref.at[source]) for i, source in enumerate(sources)], back_sem)
    for copy in copies:
        copy.wait()


def sibling_rows(here, weight, rows, slots, z_rows, back):
    count, capacity, width = rows.shape
    hidden = weight.shape[0]
    vmem, anywhere = pl.BlockSpec(memory_space=pltpu.VMEM), pl.BlockSpec(memory_space=pl.ANY)
    return pl.pallas_call(
        functools.partial(sibling_kernel, capacity, slots),
        in_specs=[pl.BlockSpec(memory_space=pltpu.SMEM), vmem, vmem, anywhere, anywhere],
        out_specs=[anywhere, anywhere],
        out_shape=[jax.ShapeDtypeStruct(z_rows.shape, BF16), jax.ShapeDtypeStruct(back.shape, BF16)],
        scratch_shapes=[
            pltpu.VMEM((count, capacity, hidden), BF16),
            pltpu.SemaphoreType.DMA((count,)),
            pltpu.SemaphoreType.DMA((count,)),
        ],
        input_output_aliases={3: 0, 4: 1},
        compiler_params=pltpu.CompilerParams(vmem_limit_bytes=40 * MIB),
        cost_estimate=pl.CostEstimate(
            flops=2 * count * capacity * width * hidden, transcendentals=0,
            bytes_accessed=2 * count * capacity * (2 * width + hidden) + 2 * width * hidden,
        ),
        name="sibling_rows",
    )(here, weight, rows, z_rows, back)


def forward_kernel(capacity, turn, here_ref, rank_ref, gate_ref, h_ref, weight_ref, out_ref):
    each = out_ref.shape[0]
    lane = (here_ref[0] % 2) ^ turn
    flat = h_ref[...].reshape(each * capacity, h_ref.shape[3])
    out = jnp.dot(flat, weight_ref[...], preferred_element_type=F32).astype(BF16).astype(F32)
    for j in range(each):
        source = (pl.program_id(0) * each + j) * 2 + lane
        gate = gate_column(gate_ref, chosen_rows(rank_ref, 0, source, capacity), 0, source)
        out_ref[j] = (out[j * capacity:(j + 1) * capacity, :] * gate).astype(BF16)


def forward_rows(here, rank, gate, rows_h, weight, turn, each=4):
    devices, capacity, hidden = rows_h.shape
    width = weight.shape[1]
    whole = pl.BlockSpec(rank.shape, lambda i, here: (0, 0, 0))
    return pl.pallas_call(
        functools.partial(forward_kernel, capacity, turn),
        grid_spec=pltpu.PrefetchScalarGridSpec(
            num_scalar_prefetch=1,
            grid=(devices // 2 // each,),
            in_specs=[
                whole,
                whole,
                pl.BlockSpec((each, 1, capacity, hidden), lambda i, here: (i, (here[0] % 2) ^ turn, 0, 0)),
                pl.BlockSpec((hidden, width), lambda i, here: (0, 0)),
            ],
            out_specs=pl.BlockSpec((each, capacity, width), lambda i, here: (i, 0, 0)),
        ),
        out_shape=jax.ShapeDtypeStruct((devices // 2, capacity, width), BF16),
        compiler_params=pltpu.CompilerParams(vmem_limit_bytes=40 * MIB),
        cost_estimate=pl.CostEstimate(
            flops=devices * capacity * width * hidden, transcendentals=0,
            bytes_accessed=devices * capacity * (width + hidden) + 2 * width * hidden,
        ),
        name="forward_rows",
    )(here, rank, gate, rows_h.reshape(devices // 2, 2, capacity, hidden), weight)


ORDER = (3, 2, 1, 0)


def sum_kernel(capacity, turn, here_ref, rank_ref, own_ref, other_ref, *part_refs):
    for step, slot in enumerate(ORDER):

        @pl.when(pl.program_id(0) == step)
        def _():
            source = lane_sources(here_ref[0], (slot,), here_ref[0] % 2)[turn]
            both = [one_hot(chosen_rows(rank_ref, side, source, capacity)) for side in range(2)]
            rows = jnp.concatenate([own_ref[0], other_ref[0]], axis=0)
            part = lax.dot_general(
                jnp.concatenate(both, axis=0), rows, (((0,), (0,)), ((), ())), preferred_element_type=F32
            )
            part_refs[step][...] = part.astype(BF16)


def summed(here, rank, own, other, turn):
    _, capacity, width = own.shape
    tokens = rank.shape[2]

    def block(i, here):
        place = jnp.int32(0)
        for step, slot in enumerate(ORDER):
            place = jnp.where(i == step, lane_sources(here[0], (slot,), 0)[turn] // 2, place)
        return (place, 0, 0)

    return pl.pallas_call(
        functools.partial(sum_kernel, capacity, turn),
        grid_spec=pltpu.PrefetchScalarGridSpec(
            num_scalar_prefetch=1,
            grid=(len(ORDER),),
            in_specs=[
                pl.BlockSpec(rank.shape, lambda i, here: (0, 0, 0)),
                pl.BlockSpec((1, capacity, width), block),
                pl.BlockSpec((1, capacity, width), block),
            ],
            out_specs=[pl.BlockSpec((tokens, width), lambda i, here: (0, 0))] * len(ORDER),
        ),
        out_shape=[jax.ShapeDtypeStruct((tokens, width), BF16)] * len(ORDER),
        compiler_params=pltpu.CompilerParams(vmem_limit_bytes=40 * MIB),
        cost_estimate=pl.CostEstimate(
            flops=16 * tokens * capacity * width, transcendentals=0,
            bytes_accessed=8 * width * (tokens + 2 * capacity),
        ),
        name="summed",
    )(here, rank, own, other)


def added(*values):
    total = values[0].astype(F32)
    for value in values[1:]:
        total = total + value.astype(F32)
    return total.astype(BF16)


def passed(pairs, value):
    return lax.ppermute(value, "expert", [(a * 4 + lane, b * 4 + lane) for a, b in pairs for lane in range(4)])


def swapped_with(value, bit):
    devices = lax.axis_size("expert")
    return lax.ppermute(value, "expert", [(i, i ^ bit) for i in range(devices)])


OUTER, INNER = ((0, 1), (3, 2)), ((1, 2), (2, 1))
ENDS, ENDS_SWAP = ((1, 0), (2, 3)), ((0, 3), (3, 0))


def gate_kernel(*refs):
    pass


def after(values, *waited):
    count = len(values)
    anywhere = pl.BlockSpec(memory_space=pl.ANY)
    return pl.pallas_call(
        gate_kernel,
        in_specs=[anywhere] * (count + len(waited)),
        out_specs=[anywhere] * count,
        out_shape=[jax.ShapeDtypeStruct(value.shape, value.dtype) for value in values],
        input_output_aliases={i: i for i in range(count)},
        cost_estimate=pl.CostEstimate(flops=0, transcendentals=0, bytes_accessed=0),
        name="after",
    )(*values, *waited)


def dense_shards(h_rows, gates, expert_ids, cotangent, down_weight, swapped):
    devices = lax.axis_size("expert")
    here = lax.axis_index("expert").reshape(1)
    tokens, top, hidden = h_rows.shape
    capacity = min(tokens, 3 * tokens * top // (2 * devices))
    weight = down_weight[0]
    slot_ids = slots_of(expert_ids, swapped, devices)
    h_flat = h_rows.reshape(-1, hidden)

    own = cotangent
    from_end, from_inner, from_near_end = passed(OUTER, own), passed(INNER, own), passed(ENDS, own)
    from_far_end = passed(ENDS_SWAP, own)
    own_y = swapped_with(own, 2)
    routing = jnp.concatenate([slot_ids.T.astype(F32), gates.T], axis=0)
    routing = jnp.broadcast_to(routing, (devices,) + routing.shape)
    routing = lax.all_to_all(routing, "expert", split_axis=0, concat_axis=0, tiled=True)
    place, send_h = pack(slot_ids.reshape(1, -1), h_flat, devices, capacity)
    rank, gate = route(here, routing, top)
    near, last = added(from_inner, from_near_end), added(from_end, from_far_end)
    from_end, from_inner = after((from_end, from_inner), send_h, rank, own_y)
    middle_inner, middle_end = passed(INNER, from_end), passed(ENDS, from_inner)
    near_y = swapped_with(near, 2)
    middle = added(middle_inner, middle_end)
    send_h, = after((send_h,), middle, near_y)
    rows_h = lax.all_to_all(
        send_h.reshape(devices, capacity, hidden), "expert", split_axis=0, concat_axis=0, tiled=True
    )
    last_y = swapped_with(last, 2)
    middle_y = swapped_with(middle, 2)

    z_rows, back, sibling = scaled_rows(here, rank, gate, weight, [own, own_y, near, near_y], (0, 1), capacity, [])
    sibling = swapped_with(sibling, 1)
    z_rows, back, sibling_last = scaled_rows(
        here, rank, gate, weight, [middle, middle_y, last, last_y], (2, 3), capacity, [z_rows, back]
    )
    sibling_last = swapped_with(sibling_last, 1)
    z_rows, back = sibling_rows(here, weight, sibling, (0, 1), z_rows, back)
    z_rows, back = sibling_rows(here, weight, sibling_last, (2, 3), z_rows, back)
    back_rows = lax.all_to_all(back, "expert", split_axis=0, concat_axis=0, tiled=True).reshape(-1, hidden)

    rows_h, = after((rows_h,), last_y, middle_y, sibling)
    other = swapped_with(forward_rows(here, rank, gate, rows_h, weight, 1), 1)
    mine = forward_rows(here, rank, gate, rows_h, weight, 0)
    across = [swapped_with(part, 2) for part in summed(here, rank, mine, other, 1)]
    beside = summed(here, rank, mine, other, 0)
    far, mid, close, kept = zip(beside, across)
    far, mid, close = added(*far), added(*mid), added(*close)
    ends = passed(ENDS_SWAP, far)
    mid_outer, mid_inner = passed(OUTER, mid), passed(INNER, mid)
    close_outer = passed(OUTER, close)
    close_inner = passed(INNER, added(close, mid_outer))
    far_ends = passed(ENDS, added(far, mid_inner))
    mixed = added(*kept, ends, close_outer, close_inner, far_ends)

    grad_sum = lax.dot_general(
        rows_h.reshape(-1, hidden), z_rows.reshape(devices * capacity, -1), (((0,), (0,)), ((), ())),
        preferred_element_type=F32,
    )
    h_grad, gate_grad = unpack(place.reshape(-1, 1), gates.reshape(-1, 1), h_flat, back_rows)
    return (
        mixed,
        gate_grad.reshape(tokens, top),
        h_grad.reshape(tokens, top, hidden),
        grad_sum.astype(BF16)[None],
    )


def shards(h_rows, *rest):
    devices = lax.axis_size("expert")
    dense = devices == 16 and devices <= 2 * h_rows.shape[1]
    return (dense_shards if dense else sparse_shards)(h_rows, *rest)


def solution(mesh):
    in_specs = (
        P(("groups", "expert"), None, None),
        P(("groups", "expert"), None),
        P(("groups", "expert"), None),
        P(("groups", "expert"), None),
        P("expert", None, None),
        P(),
    )
    out_specs = (
        P(("groups", "expert"), None),
        P(("groups", "expert"), None),
        P(("groups", "expert"), None, None),
        P(("groups", "expert"), None, None),
    )
    return jax.shard_map(shards, mesh=mesh, in_specs=in_specs, out_specs=out_specs, check_vma=False)
```

```python
import functools

import jax
import jax.numpy as jnp
from jax import lax
from jax.experimental import pallas as pl
from jax.experimental.pallas import tpu as pltpu
from jax.sharding import PartitionSpec as P

F32 = jnp.float32
BF16 = jnp.bfloat16
MIB = 1 << 20


def slots_of(ids, swapped, devices):
    half_way = devices // 2
    table = jnp.arange(devices, dtype=jnp.int32)
    table = (table + half_way * swapped[table % half_way]) % devices
    return jnp.sum(jnp.where(ids[..., None] == jnp.arange(devices, dtype=jnp.int32), table, 0), axis=-1)


def place_rows(values, target, ranks, devices, capacity):
    buffer = jnp.zeros((devices, capacity, values.shape[-1]), values.dtype)
    return buffer.at[target, ranks].set(values)


def sparse_shards(h_rows, gates, expert_ids, cotangent, down_weight, swapped):
    devices = lax.axis_size("expert")
    tokens_here, top_count, hidden = h_rows.shape
    width = cotangent.shape[1]
    capacity = min(tokens_here, 3 * tokens_here * top_count // (2 * devices))
    experts = jnp.arange(devices, dtype=jnp.int32)
    weight = down_weight[0]
    flat_ids = slots_of(expert_ids.reshape(-1), swapped, devices)
    onehot = (flat_ids[:, None] == experts[None, :]).astype(jnp.int32)
    ranks = jnp.sum((jnp.cumsum(onehot, axis=0) - onehot) * onehot, axis=1)
    send_h = place_rows(h_rows.reshape(-1, hidden), flat_ids, ranks, devices, capacity)
    received = lax.all_to_all(send_h, "expert", split_axis=0, concat_axis=0, tiled=True)
    result = jnp.einsum("sch,hd->scd", received, weight, preferred_element_type=F32)
    results = result.astype(BF16)
    returned = lax.all_to_all(results, "expert", split_axis=0, concat_axis=0, tiled=True)
    out_rows = returned[flat_ids, ranks].reshape(tokens_here, top_count, width)
    mixed = jnp.einsum("tk,tkd->td", gates, out_rows.astype(F32)).astype(BF16)
    gate_grad = jnp.einsum("td,tkd->tk", cotangent, out_rows, preferred_element_type=F32)
    scaled = (gates[:, :, None] * cotangent[:, None, :].astype(F32)).astype(BF16)
    send_z = place_rows(scaled.reshape(-1, width), flat_ids, ranks, devices, capacity)
    recv_z = lax.all_to_all(send_z, "expert", split_axis=0, concat_axis=0, tiled=True)
    flat_z = recv_z.reshape(-1, width)
    flat_h = received.reshape(-1, hidden)
    grad_sum = lax.dot_general(flat_h, flat_z, (((0,), (0,)), ((), ())), preferred_element_type=F32)
    back = lax.dot_general(flat_z, weight, (((1,), (1,)), ((), ())), preferred_element_type=F32).astype(BF16)
    back_rows = lax.all_to_all(
        back.reshape(devices, capacity, hidden), "expert", split_axis=0, concat_axis=0, tiled=True
    )
    h_grad = back_rows[flat_ids, ranks].reshape(tokens_here, top_count, hidden)
    return (mixed, gate_grad, h_grad, grad_sum.astype(BF16)[None])


def upper(size):
    rows = lax.broadcasted_iota(jnp.int32, (size, size), 0)
    columns = lax.broadcasted_iota(jnp.int32, (size, size), 1)
    return (rows < columns).astype(F32).astype(BF16)


def pack_kernel(devices, capacity, ids_ref, h_ref, place_ref, sent_ref, place_scratch):
    pairs = ids_ref.shape[1]
    rows = sent_ref.shape[0]

    @pl.when(pl.program_id(0) == 0)
    def _():
        before = jnp.zeros((devices, 1), F32)
        for tile in range(pairs // 128):
            ids = ids_ref[:, tile * 128:(tile + 1) * 128]
            named = lax.broadcasted_iota(jnp.int32, (devices, 128), 0) == ids
            ones = jnp.where(named, 1.0, 0.0)
            rank = jnp.dot(ones.astype(BF16), upper(128), preferred_element_type=F32) + before
            before = before + jnp.sum(ones, axis=1, keepdims=True)
            rank = jnp.sum(jnp.where(named, rank, 0.0), axis=0, keepdims=True)
            place_scratch[:, tile * 128:(tile + 1) * 128] = ids * capacity + rank.astype(jnp.int32)
        place_ref[...] = place_scratch[...]

    first = pl.program_id(0) * rows
    wanted = lax.broadcasted_iota(jnp.int32, (rows, pairs), 0) + first
    chosen = jnp.where(wanted == place_scratch[...], 1.0, 0.0).astype(BF16)
    sent_ref[...] = jnp.dot(chosen, h_ref[...], preferred_element_type=F32).astype(BF16)


def pack(ids, h_flat, devices, capacity, steps=4):
    pairs, hidden = h_flat.shape
    rows = devices * capacity // steps
    return pl.pallas_call(
        functools.partial(pack_kernel, devices, capacity),
        grid=(steps,),
        in_specs=[
            pl.BlockSpec((1, pairs), lambda i: (0, 0)),
            pl.BlockSpec((pairs, hidden), lambda i: (0, 0)),
        ],
        out_specs=[
            pl.BlockSpec((1, pairs), lambda i: (0, 0)),
            pl.BlockSpec((rows, hidden), lambda i: (i, 0)),
        ],
        out_shape=[
            jax.ShapeDtypeStruct((1, pairs), jnp.int32),
            jax.ShapeDtypeStruct((devices * capacity, hidden), BF16),
        ],
        scratch_shapes=[pltpu.VMEM((1, pairs), jnp.int32)],
        compiler_params=pltpu.CompilerParams(vmem_limit_bytes=60 * MIB),
        cost_estimate=pl.CostEstimate(
            flops=2 * devices * capacity * pairs * hidden, transcendentals=0,
            bytes_accessed=2 * hidden * (pairs + devices * capacity),
        ),
        name="pack",
    )(ids, h_flat)


def unpack_kernel(slots, place_ref, gate_ref, h_ref, back_ref, grad_ref, gate_grad_ref):
    rows = place_ref.shape[0]
    chosen = lax.broadcasted_iota(jnp.int32, (rows, slots), 1) == place_ref[...]
    grad = jnp.dot(jnp.where(chosen, 1.0, 0.0).astype(BF16), back_ref[...], preferred_element_type=F32)
    grad_ref[...] = grad.astype(BF16)
    gate_grad_ref[...] = jnp.sum(grad * h_ref[...].astype(F32), axis=1, keepdims=True) / gate_ref[...]


def unpack(place, gates, h_flat, back_rows, steps=4):
    pairs, hidden = h_flat.shape
    slots = back_rows.shape[0]
    rows = pairs // steps
    return pl.pallas_call(
        functools.partial(unpack_kernel, slots),
        grid=(steps,),
        in_specs=[
            pl.BlockSpec((rows, 1), lambda i: (i, 0)),
            pl.BlockSpec((rows, 1), lambda i: (i, 0)),
            pl.BlockSpec((rows, hidden), lambda i: (i, 0)),
            pl.BlockSpec((slots, hidden), lambda i: (0, 0)),
        ],
        out_specs=[
            pl.BlockSpec((rows, hidden), lambda i: (i, 0)),
            pl.BlockSpec((rows, 1), lambda i: (i, 0)),
        ],
        out_shape=[
            jax.ShapeDtypeStruct((pairs, hidden), BF16),
            jax.ShapeDtypeStruct((pairs, 1), F32),
        ],
        compiler_params=pltpu.CompilerParams(vmem_limit_bytes=60 * MIB),
        cost_estimate=pl.CostEstimate(
            flops=2 * slots * pairs * hidden, transcendentals=0,
            bytes_accessed=2 * hidden * (2 * pairs + slots),
        ),
        name="unpack",
    )(place, gates, h_flat, back_rows)


def line_slots(position):
    near = jnp.minimum(position, 3 - position)
    turned = (near, near + 1, near + 2, 3 - 3 * near)
    return [jnp.where(position < 2, slot, 3 - slot) for slot in turned]


def route_kernel(devices, top, here_ref, routing_ref, rank_ref, gate_ref):
    for side in range(2):
        mine = (here_ref[0] ^ side).astype(F32)
        marks, picked = [], []
        for source in range(devices):
            ids = routing_ref[source, :top, :]
            gates = routing_ref[source, top:, :]
            named = ids == mine
            marks.append(jnp.sum(jnp.where(named, 1.0, 0.0), axis=0, keepdims=True))
            picked.append(jnp.sum(jnp.where(named, gates, 0.0), axis=0, keepdims=True))
        mark = jnp.concatenate(marks, axis=0)
        rank = jnp.dot(mark.astype(BF16), upper(mark.shape[1]), preferred_element_type=F32)
        rank_ref[side] = jnp.where(mark > 0, rank, -1.0).astype(jnp.int32)
        gate_ref[side] = jnp.concatenate(picked, axis=0)


def route(here, routing, top):
    devices, _, tokens = routing.shape
    return pl.pallas_call(
        functools.partial(route_kernel, devices, top),
        in_specs=[pl.BlockSpec(memory_space=pltpu.SMEM), pl.BlockSpec(memory_space=pltpu.VMEM)],
        out_specs=[pl.BlockSpec(memory_space=pltpu.VMEM)] * 2,
        out_shape=[
            jax.ShapeDtypeStruct((2, devices, tokens), jnp.int32),
            jax.ShapeDtypeStruct((2, devices, tokens), F32),
        ],
        cost_estimate=pl.CostEstimate(flops=1 << 21, transcendentals=0, bytes_accessed=1 << 19),
        name="route",
    )(here, routing)


def chosen_rows(rank_ref, side, source, capacity):
    rank = rank_ref[side, pl.ds(source, 1), :]
    return lax.broadcasted_iota(jnp.int32, (capacity, rank.shape[1]), 0) == rank


def gate_column(gate_ref, chosen, side, source):
    return jnp.sum(jnp.where(chosen, gate_ref[side, pl.ds(source, 1), :], 0.0), axis=1, keepdims=True)


def one_hot(chosen):
    return jnp.where(chosen, 1.0, 0.0).astype(BF16)


def lane_sources(here, slots, lane):
    line, across = here // 4, (here // 2) % 2
    places = line_slots(line)
    return [places[slot] * 4 + (across ^ turn) * 2 + lane for slot in slots for turn in range(2)]


def place_out(pieces, sem):
    copies = [pltpu.make_async_copy(source, target, sem.at[i]) for i, (source, target) in enumerate(pieces)]
    for copy in copies:
        copy.start()
    return copies


def scale_kernel(capacity, slots, held, here_ref, rank_ref, gate_ref, weight_ref, *refs):
    count = 2 * len(slots)
    blocks, refs = refs[:count], refs[count + held:]
    z_ref, back_ref, sibling_ref, z_scratch, back_scratch, z_sem, back_sem = refs
    sources = lane_sources(here_ref[0], slots, here_ref[0] % 2)
    for i, source in enumerate(sources):
        chosen = [chosen_rows(rank_ref, side, source, capacity) for side in range(2)]
        gates = [gate_column(gate_ref, chosen[side], side, source) for side in range(2)]
        both = jnp.concatenate([one_hot(chosen[0]), one_hot(chosen[1])], axis=0)
        rows = jnp.dot(both, blocks[i][...], preferred_element_type=F32)
        z_scratch[i] = (rows[:capacity] * gates[0]).astype(BF16)
        sibling_ref[i] = (rows[capacity:] * gates[1]).astype(BF16)
    copies = place_out([(z_scratch.at[i], z_ref.at[source]) for i, source in enumerate(sources)], z_sem)
    flat = z_scratch[...].reshape(count * capacity, z_scratch.shape[2])
    back = lax.dot_general(flat, weight_ref[...], (((1,), (1,)), ((), ())), preferred_element_type=F32)
    back_scratch[...] = back.astype(BF16).reshape(back_scratch.shape)
    copies += place_out([(back_scratch.at[i], back_ref.at[source]) for i, source in enumerate(sources)], back_sem)
    for copy in copies:
        copy.wait()


def scaled_rows(here, rank, gate, weight, blocks, slots, capacity, buffers):
    devices = rank.shape[1]
    hidden, width = weight.shape
    count = len(blocks)
    tokens = blocks[0].shape[0]
    vmem, anywhere = pl.BlockSpec(memory_space=pltpu.VMEM), pl.BlockSpec(memory_space=pltpu.HBM)
    return pl.pallas_call(
        functools.partial(scale_kernel, capacity, slots, len(buffers)),
        in_specs=[pl.BlockSpec(memory_space=pltpu.SMEM)] + [vmem] * (3 + count) + [anywhere] * len(buffers),
        out_specs=[anywhere, anywhere, vmem],
        out_shape=[
            jax.ShapeDtypeStruct((devices, capacity, width), BF16),
            jax.ShapeDtypeStruct((devices, capacity, hidden), BF16),
            jax.ShapeDtypeStruct((count, capacity, width), BF16),
        ],
        scratch_shapes=[
            pltpu.VMEM((count, capacity, width), BF16),
            pltpu.VMEM((count, capacity, hidden), BF16),
            pltpu.SemaphoreType.DMA((count,)),
            pltpu.SemaphoreType.DMA((count,)),
        ],
        input_output_aliases={4 + count + i: i for i in range(len(buffers))},
        compiler_params=pltpu.CompilerParams(vmem_limit_bytes=60 * MIB),
        cost_estimate=pl.CostEstimate(
            flops=2 * count * capacity * width * (hidden + 2 * tokens), transcendentals=0,
            bytes_accessed=2 * count * (tokens * width + capacity * (2 * width + hidden)) + 2 * width * hidden,
        ),
        name="scaled_rows",
    )(here, rank, gate, weight, *blocks, *buffers)


def sibling_kernel(capacity, slots, here_ref, weight_ref, rows_ref, _z, _back, z_ref, back_ref, token_ref, back_scratch, z_sem, back_sem):
    count = 2 * len(slots)
    sources = lane_sources(here_ref[0], slots, 1 - here_ref[0] % 2)
    copies = place_out([(rows_ref.at[i], z_ref.at[source]) for i, source in enumerate(sources)], z_sem)
    flat = rows_ref[...].reshape(count * capacity, rows_ref.shape[2])
    back = lax.dot_general(flat, weight_ref[...], (((1,), (1,)), ((), ())), preferred_element_type=F32)
    back_scratch[...] = back.astype(BF16).reshape(back_scratch.shape)
    copies += place_out([(back_scratch.at[i], back_ref.at[source]) for i, source in enumerate(sources)], back_sem)
    token_ref[...] = jnp.zeros_like(token_ref)
    for copy in copies:
        copy.wait()


def sibling_rows(here, weight, rows, slots, z_rows, back):
    count, capacity, width = rows.shape
    hidden = weight.shape[0]
    vmem, anywhere = pl.BlockSpec(memory_space=pltpu.VMEM), pl.BlockSpec(memory_space=pltpu.HBM)
    return pl.pallas_call(
        functools.partial(sibling_kernel, capacity, slots),
        in_specs=[pl.BlockSpec(memory_space=pltpu.SMEM), vmem, vmem, anywhere, anywhere],
        out_specs=[anywhere, anywhere, vmem],
        out_shape=[
            jax.ShapeDtypeStruct(z_rows.shape, BF16),
            jax.ShapeDtypeStruct(back.shape, BF16),
            jax.ShapeDtypeStruct((8, 128), F32),
        ],
        scratch_shapes=[
            pltpu.VMEM((count, capacity, hidden), BF16),
            pltpu.SemaphoreType.DMA((count,)),
            pltpu.SemaphoreType.DMA((count,)),
        ],
        input_output_aliases={3: 0, 4: 1},
        compiler_params=pltpu.CompilerParams(vmem_limit_bytes=60 * MIB),
        cost_estimate=pl.CostEstimate(
            flops=2 * count * capacity * width * hidden, transcendentals=0,
            bytes_accessed=2 * count * capacity * (2 * width + hidden) + 2 * width * hidden,
        ),
        name="sibling_rows",
    )(here, weight, rows, z_rows, back)


def forward_kernel(capacity, turn, here_ref, rank_ref, gate_ref, h_ref, weight_ref, out_ref):
    each = out_ref.shape[0]
    lane = (here_ref[0] % 2) ^ turn
    flat = h_ref[...].reshape(each * capacity, h_ref.shape[3])
    out = jnp.dot(flat, weight_ref[...], preferred_element_type=F32).astype(BF16).astype(F32)
    for j in range(each):
        source = (pl.program_id(0) * each + j) * 2 + lane
        gate = gate_column(gate_ref, chosen_rows(rank_ref, 0, source, capacity), 0, source)
        out_ref[j] = (out[j * capacity:(j + 1) * capacity, :] * gate).astype(BF16)


def forward_rows(here, rank, gate, rows_h, weight, turn, each=4):
    devices, capacity, hidden = rows_h.shape
    width = weight.shape[1]
    whole = pl.BlockSpec(rank.shape, lambda i, here: (0, 0, 0))
    return pl.pallas_call(
        functools.partial(forward_kernel, capacity, turn),
        grid_spec=pltpu.PrefetchScalarGridSpec(
            num_scalar_prefetch=1,
            grid=(devices // 2 // each,),
            in_specs=[
                whole,
                whole,
                pl.BlockSpec((each, 1, capacity, hidden), lambda i, here: (i, (here[0] % 2) ^ turn, 0, 0)),
                pl.BlockSpec((hidden, width), lambda i, here: (0, 0)),
            ],
            out_specs=pl.BlockSpec((each, capacity, width), lambda i, here: (i, 0, 0)),
        ),
        out_shape=jax.ShapeDtypeStruct((devices // 2, capacity, width), BF16),
        compiler_params=pltpu.CompilerParams(vmem_limit_bytes=60 * MIB),
        cost_estimate=pl.CostEstimate(
            flops=devices * capacity * width * hidden, transcendentals=0,
            bytes_accessed=devices * capacity * (width + hidden) + 2 * width * hidden,
        ),
        name="forward_rows",
    )(here, rank, gate, rows_h.reshape(devices // 2, 2, capacity, hidden), weight)


ORDER = (3, 2, 1, 0)


def sum_kernel(capacity, turn, here_ref, rank_ref, own_ref, other_ref, *part_refs):
    for step, slot in enumerate(ORDER):

        @pl.when(pl.program_id(0) == step)
        def _():
            source = lane_sources(here_ref[0], (slot,), here_ref[0] % 2)[turn]
            both = [one_hot(chosen_rows(rank_ref, side, source, capacity)) for side in range(2)]
            rows = jnp.concatenate([own_ref[0], other_ref[0]], axis=0)
            part = lax.dot_general(
                jnp.concatenate(both, axis=0), rows, (((0,), (0,)), ((), ())), preferred_element_type=F32
            )
            part_refs[step][...] = part.astype(BF16)


def summed(here, rank, own, other, turn):
    _, capacity, width = own.shape
    tokens = rank.shape[2]

    def block(i, here):
        place = jnp.int32(0)
        for step, slot in enumerate(ORDER):
            place = jnp.where(i == step, lane_sources(here[0], (slot,), 0)[turn] // 2, place)
        return (place, 0, 0)

    return pl.pallas_call(
        functools.partial(sum_kernel, capacity, turn),
        grid_spec=pltpu.PrefetchScalarGridSpec(
            num_scalar_prefetch=1,
            grid=(len(ORDER),),
            in_specs=[
                pl.BlockSpec(rank.shape, lambda i, here: (0, 0, 0)),
                pl.BlockSpec((1, capacity, width), block),
                pl.BlockSpec((1, capacity, width), block),
            ],
            out_specs=[pl.BlockSpec((tokens, width), lambda i, here: (0, 0))] * len(ORDER),
        ),
        out_shape=[jax.ShapeDtypeStruct((tokens, width), BF16)] * len(ORDER),
        compiler_params=pltpu.CompilerParams(vmem_limit_bytes=60 * MIB),
        cost_estimate=pl.CostEstimate(
            flops=16 * tokens * capacity * width, transcendentals=0,
            bytes_accessed=8 * width * (tokens + 2 * capacity),
        ),
        name="summed",
    )(here, rank, own, other)


def added(*values):
    total = values[0].astype(F32)
    for value in values[1:]:
        total = total + value.astype(F32)
    return total.astype(BF16)


def passed(pairs, value):
    return lax.ppermute(value, "expert", [(a * 4 + lane, b * 4 + lane) for a, b in pairs for lane in range(4)])


def swapped_with(value, bit):
    devices = lax.axis_size("expert")
    return lax.ppermute(value, "expert", [(i, i ^ bit) for i in range(devices)])


OUTER, INNER = ((0, 1), (3, 2)), ((1, 2), (2, 1))
ENDS, ENDS_SWAP = ((1, 0), (2, 3)), ((0, 3), (3, 0))


def gate_kernel(*refs):
    pass


def after(values, *waited):
    count = len(values)
    anywhere = pl.BlockSpec(memory_space=pl.ANY)
    return pl.pallas_call(
        gate_kernel,
        in_specs=[anywhere] * (count + len(waited)),
        out_specs=[anywhere] * count,
        out_shape=[jax.ShapeDtypeStruct(value.shape, value.dtype) for value in values],
        input_output_aliases={i: i for i in range(count)},
        compiler_params=pltpu.CompilerParams(vmem_limit_bytes=60 * MIB),
        cost_estimate=pl.CostEstimate(flops=0, transcendentals=0, bytes_accessed=0),
        name="after",
    )(*values, *waited)


def dense_shards(h_rows, gates, expert_ids, cotangent, down_weight, swapped):
    devices = lax.axis_size("expert")
    here = lax.axis_index("expert").reshape(1)
    tokens, top, hidden = h_rows.shape
    capacity = min(tokens, 3 * tokens * top // (2 * devices))
    weight = down_weight[0]
    slot_ids = slots_of(expert_ids, swapped, devices)
    h_flat = h_rows.reshape(-1, hidden)

    own = cotangent
    from_end, from_inner, from_near_end = passed(OUTER, own), passed(INNER, own), passed(ENDS, own)
    from_far_end = passed(ENDS_SWAP, own)
    own_y = swapped_with(own, 2)
    routing = jnp.concatenate([slot_ids.T.astype(F32), gates.T], axis=0)
    routing = jnp.broadcast_to(routing, (devices,) + routing.shape)
    routing, flat_ids = after(
        (routing, slot_ids.reshape(1, -1)), from_end, from_inner, from_near_end, from_far_end, own_y
    )
    routing = lax.all_to_all(routing, "expert", split_axis=0, concat_axis=0, tiled=True)
    place, send_h = pack(flat_ids, h_flat, devices, capacity)
    rank, gate = route(here, routing, top)
    near, last = added(from_inner, from_near_end), added(from_end, from_far_end)
    middle_inner, middle_end = passed(INNER, from_end), passed(ENDS, from_inner)
    near_y = swapped_with(near, 2)
    middle = added(middle_inner, middle_end)
    send_h, = after((send_h,), middle, near_y)
    rows_h = lax.all_to_all(
        send_h.reshape(devices, capacity, hidden), "expert", split_axis=0, concat_axis=0, tiled=True
    )
    last_y = swapped_with(last, 2)
    middle_y = swapped_with(middle, 2)

    z_rows, back, sibling = scaled_rows(here, rank, gate, weight, [own, own_y, near, near_y], (0, 1), capacity, [])
    sibling = swapped_with(sibling, 1)
    z_rows, back, early = sibling_rows(here, weight, sibling, (0, 1), z_rows, back)
    z_rows, back, sibling_last = scaled_rows(
        here, rank, gate, weight, [middle, middle_y, last, last_y], (2, 3), capacity, [z_rows, back]
    )
    sibling_last = swapped_with(sibling_last, 1)
    z_rows, back, _ = sibling_rows(here, weight, sibling_last, (2, 3), z_rows, back)
    back_rows = lax.all_to_all(back, "expert", split_axis=0, concat_axis=0, tiled=True).reshape(-1, hidden)

    rows_h, = after((rows_h,), last_y, middle_y, early)
    other = swapped_with(forward_rows(here, rank, gate, rows_h, weight, 1), 1)
    mine = forward_rows(here, rank, gate, rows_h, weight, 0)
    across = [swapped_with(part, 2) for part in summed(here, rank, mine, other, 1)]
    beside = summed(here, rank, mine, other, 0)
    far, mid, close, kept = zip(beside, across)
    far, mid, close = added(*far), added(*mid), added(*close)
    ends = passed(ENDS_SWAP, far)
    mid_outer, mid_inner = passed(OUTER, mid), passed(INNER, mid)
    close_outer = passed(OUTER, close)
    close_inner = passed(INNER, added(close, mid_outer))
    far_ends = passed(ENDS, added(far, mid_inner))
    mixed = added(*kept, ends, close_outer, close_inner, far_ends)

    grad_sum = lax.dot_general(
        rows_h.reshape(-1, hidden), z_rows.reshape(devices * capacity, -1), (((0,), (0,)), ((), ())),
        preferred_element_type=F32,
    )
    h_grad, gate_grad = unpack(place.reshape(-1, 1), gates.reshape(-1, 1), h_flat, back_rows)
    return (
        mixed,
        gate_grad.reshape(tokens, top),
        h_grad.reshape(tokens, top, hidden),
        grad_sum.astype(BF16)[None],
    )


def shards(h_rows, *rest):
    devices = lax.axis_size("expert")
    dense = devices == 16 and devices <= 2 * h_rows.shape[1]
    return (dense_shards if dense else sparse_shards)(h_rows, *rest)


def solution(mesh):
    in_specs = (
        P(("groups", "expert"), None, None),
        P(("groups", "expert"), None),
        P(("groups", "expert"), None),
        P(("groups", "expert"), None),
        P("expert", None, None),
        P(),
    )
    out_specs = (
        P(("groups", "expert"), None),
        P(("groups", "expert"), None),
        P(("groups", "expert"), None, None),
        P(("groups", "expert"), None, None),
    )
    return jax.shard_map(shards, mesh=mesh, in_specs=in_specs, out_specs=out_specs, check_vma=False)
```

```python
import functools

import jax
import jax.numpy as jnp
from jax import lax
from jax.experimental import pallas as pl
from jax.experimental.pallas import tpu as pltpu
from jax.sharding import PartitionSpec as P

F32 = jnp.float32
BF16 = jnp.bfloat16
MIB = 1 << 20
BRIEF = pl.CostEstimate(flops=0, transcendentals=0, bytes_accessed=0)


def slots_of(ids, swapped, devices):
    half_way = devices // 2
    table = jnp.arange(devices, dtype=jnp.int32)
    table = (table + half_way * swapped[table % half_way]) % devices
    return jnp.sum(jnp.where(ids[..., None] == jnp.arange(devices, dtype=jnp.int32), table, 0), axis=-1)


def place_rows(values, target, ranks, devices, capacity):
    buffer = jnp.zeros((devices, capacity, values.shape[-1]), values.dtype)
    return buffer.at[target, ranks].set(values)


def sparse_shards(h_rows, gates, expert_ids, cotangent, down_weight, swapped):
    devices = lax.axis_size("expert")
    tokens_here, top_count, hidden = h_rows.shape
    width = cotangent.shape[1]
    capacity = min(tokens_here, 3 * tokens_here * top_count // (2 * devices))
    experts = jnp.arange(devices, dtype=jnp.int32)
    weight = down_weight[0]
    flat_ids = slots_of(expert_ids.reshape(-1), swapped, devices)
    onehot = (flat_ids[:, None] == experts[None, :]).astype(jnp.int32)
    ranks = jnp.sum((jnp.cumsum(onehot, axis=0) - onehot) * onehot, axis=1)
    send_h = place_rows(h_rows.reshape(-1, hidden), flat_ids, ranks, devices, capacity)
    received = lax.all_to_all(send_h, "expert", split_axis=0, concat_axis=0, tiled=True)
    result = jnp.einsum("sch,hd->scd", received, weight, preferred_element_type=F32)
    results = result.astype(BF16)
    returned = lax.all_to_all(results, "expert", split_axis=0, concat_axis=0, tiled=True)
    out_rows = returned[flat_ids, ranks].reshape(tokens_here, top_count, width)
    mixed = jnp.einsum("tk,tkd->td", gates, out_rows.astype(F32)).astype(BF16)
    gate_grad = jnp.einsum("td,tkd->tk", cotangent, out_rows, preferred_element_type=F32)
    scaled = (gates[:, :, None] * cotangent[:, None, :].astype(F32)).astype(BF16)
    send_z = place_rows(scaled.reshape(-1, width), flat_ids, ranks, devices, capacity)
    recv_z = lax.all_to_all(send_z, "expert", split_axis=0, concat_axis=0, tiled=True)
    flat_z = recv_z.reshape(-1, width)
    flat_h = received.reshape(-1, hidden)
    grad_sum = lax.dot_general(flat_h, flat_z, (((0,), (0,)), ((), ())), preferred_element_type=F32)
    back = lax.dot_general(flat_z, weight, (((1,), (1,)), ((), ())), preferred_element_type=F32).astype(BF16)
    back_rows = lax.all_to_all(
        back.reshape(devices, capacity, hidden), "expert", split_axis=0, concat_axis=0, tiled=True
    )
    h_grad = back_rows[flat_ids, ranks].reshape(tokens_here, top_count, hidden)
    return (mixed, gate_grad, h_grad, grad_sum.astype(BF16)[None])


def upper(size):
    rows = lax.broadcasted_iota(jnp.int32, (size, size), 0)
    columns = lax.broadcasted_iota(jnp.int32, (size, size), 1)
    return (rows < columns).astype(F32).astype(BF16)


def pack_kernel(devices, capacity, ids_ref, h_ref, place_ref, sent_ref, place_scratch):
    pairs = ids_ref.shape[1]
    rows = sent_ref.shape[0]

    @pl.when(pl.program_id(0) == 0)
    def _():
        before = jnp.zeros((devices, 1), F32)
        for tile in range(pairs // 128):
            ids = ids_ref[:, tile * 128:(tile + 1) * 128]
            named = lax.broadcasted_iota(jnp.int32, (devices, 128), 0) == ids
            ones = jnp.where(named, 1.0, 0.0)
            rank = jnp.dot(ones.astype(BF16), upper(128), preferred_element_type=F32) + before
            before = before + jnp.sum(ones, axis=1, keepdims=True)
            rank = jnp.sum(jnp.where(named, rank, 0.0), axis=0, keepdims=True)
            place_scratch[:, tile * 128:(tile + 1) * 128] = ids * capacity + rank.astype(jnp.int32)
        place_ref[...] = place_scratch[...]

    first = pl.program_id(0) * rows
    wanted = lax.broadcasted_iota(jnp.int32, (rows, pairs), 0) + first
    chosen = jnp.where(wanted == place_scratch[...], 1.0, 0.0).astype(BF16)
    sent_ref[...] = jnp.dot(chosen, h_ref[...], preferred_element_type=F32).astype(BF16)


def pack(ids, h_flat, devices, capacity, steps=4):
    pairs, hidden = h_flat.shape
    rows = devices * capacity // steps
    return pl.pallas_call(
        functools.partial(pack_kernel, devices, capacity),
        grid=(steps,),
        in_specs=[
            pl.BlockSpec((1, pairs), lambda i: (0, 0)),
            pl.BlockSpec((pairs, hidden), lambda i: (0, 0)),
        ],
        out_specs=[
            pl.BlockSpec((1, pairs), lambda i: (0, 0)),
            pl.BlockSpec((rows, hidden), lambda i: (i, 0)),
        ],
        out_shape=[
            jax.ShapeDtypeStruct((1, pairs), jnp.int32),
            jax.ShapeDtypeStruct((devices * capacity, hidden), BF16),
        ],
        scratch_shapes=[pltpu.VMEM((1, pairs), jnp.int32)],
        compiler_params=pltpu.CompilerParams(vmem_limit_bytes=60 * MIB),
        cost_estimate=BRIEF,
        name="pack",
    )(ids, h_flat)


def unpack_kernel(slots, place_ref, gate_ref, h_ref, back_ref, grad_ref, gate_grad_ref):
    rows = place_ref.shape[0]
    chosen = lax.broadcasted_iota(jnp.int32, (rows, slots), 1) == place_ref[...]
    grad = jnp.dot(jnp.where(chosen, 1.0, 0.0).astype(BF16), back_ref[...], preferred_element_type=F32)
    grad_ref[...] = grad.astype(BF16)
    gate_grad_ref[...] = jnp.sum(grad * h_ref[...].astype(F32), axis=1, keepdims=True) / gate_ref[...]


def unpack(place, gates, h_flat, back_rows, steps=4):
    pairs, hidden = h_flat.shape
    slots = back_rows.shape[0]
    rows = pairs // steps
    return pl.pallas_call(
        functools.partial(unpack_kernel, slots),
        grid=(steps,),
        in_specs=[
            pl.BlockSpec((rows, 1), lambda i: (i, 0)),
            pl.BlockSpec((rows, 1), lambda i: (i, 0)),
            pl.BlockSpec((rows, hidden), lambda i: (i, 0)),
            pl.BlockSpec((slots, hidden), lambda i: (0, 0)),
        ],
        out_specs=[
            pl.BlockSpec((rows, hidden), lambda i: (i, 0)),
            pl.BlockSpec((rows, 1), lambda i: (i, 0)),
        ],
        out_shape=[
            jax.ShapeDtypeStruct((pairs, hidden), BF16),
            jax.ShapeDtypeStruct((pairs, 1), F32),
        ],
        compiler_params=pltpu.CompilerParams(vmem_limit_bytes=60 * MIB),
        cost_estimate=BRIEF,
        name="unpack",
    )(place, gates, h_flat, back_rows)


def line_slots(position):
    near = jnp.minimum(position, 3 - position)
    turned = (near, near + 1, near + 2, 3 - 3 * near)
    return [jnp.where(position < 2, slot, 3 - slot) for slot in turned]


def route_kernel(devices, top, here_ref, routing_ref, rank_ref, gate_ref):
    for side in range(2):
        mine = (here_ref[0] ^ side).astype(F32)
        marks, picked = [], []
        for source in range(devices):
            ids = routing_ref[source, :top, :]
            gates = routing_ref[source, top:, :]
            named = ids == mine
            marks.append(jnp.sum(jnp.where(named, 1.0, 0.0), axis=0, keepdims=True))
            picked.append(jnp.sum(jnp.where(named, gates, 0.0), axis=0, keepdims=True))
        mark = jnp.concatenate(marks, axis=0)
        rank = jnp.dot(mark.astype(BF16), upper(mark.shape[1]), preferred_element_type=F32)
        rank_ref[side] = jnp.where(mark > 0, rank, -1.0).astype(jnp.int32)
        gate_ref[side] = jnp.concatenate(picked, axis=0)


def route(here, routing, top):
    devices, _, tokens = routing.shape
    return pl.pallas_call(
        functools.partial(route_kernel, devices, top),
        in_specs=[pl.BlockSpec(memory_space=pltpu.SMEM), pl.BlockSpec(memory_space=pltpu.VMEM)],
        out_specs=[pl.BlockSpec(memory_space=pltpu.VMEM)] * 2,
        out_shape=[
            jax.ShapeDtypeStruct((2, devices, tokens), jnp.int32),
            jax.ShapeDtypeStruct((2, devices, tokens), F32),
        ],
        cost_estimate=BRIEF,
        name="route",
    )(here, routing)


def chosen_rows(rank_ref, side, source, capacity):
    rank = rank_ref[side, pl.ds(source, 1), :]
    return lax.broadcasted_iota(jnp.int32, (capacity, rank.shape[1]), 0) == rank


def gate_column(gate_ref, chosen, side, source):
    return jnp.sum(jnp.where(chosen, gate_ref[side, pl.ds(source, 1), :], 0.0), axis=1, keepdims=True)


def one_hot(chosen):
    return jnp.where(chosen, 1.0, 0.0).astype(BF16)


def lane_sources(here, slots, lane):
    line, across = here // 4, (here // 2) % 2
    places = line_slots(line)
    return [places[slot] * 4 + (across ^ turn) * 2 + lane for slot in slots for turn in range(2)]


def place_out(pieces, sem):
    copies = [pltpu.make_async_copy(source, target, sem.at[i]) for i, (source, target) in enumerate(pieces)]
    for copy in copies:
        copy.start()
    return copies


def scale_kernel(capacity, slots, held, here_ref, rank_ref, gate_ref, weight_ref, *refs):
    count = 2 * len(slots)
    blocks, refs = refs[:count], refs[count + held:]
    z_ref, back_ref, sibling_ref, z_scratch, back_scratch, z_sem, back_sem = refs
    sources = lane_sources(here_ref[0], slots, here_ref[0] % 2)
    for i, source in enumerate(sources):
        chosen = [chosen_rows(rank_ref, side, source, capacity) for side in range(2)]
        gates = [gate_column(gate_ref, chosen[side], side, source) for side in range(2)]
        both = jnp.concatenate([one_hot(chosen[0]), one_hot(chosen[1])], axis=0)
        rows = jnp.dot(both, blocks[i][...], preferred_element_type=F32)
        z_scratch[i] = (rows[:capacity] * gates[0]).astype(BF16)
        sibling_ref[i] = (rows[capacity:] * gates[1]).astype(BF16)
    copies = place_out([(z_scratch.at[i], z_ref.at[source]) for i, source in enumerate(sources)], z_sem)
    flat = z_scratch[...].reshape(count * capacity, z_scratch.shape[2])
    back = lax.dot_general(flat, weight_ref[...], (((1,), (1,)), ((), ())), preferred_element_type=F32)
    back_scratch[...] = back.astype(BF16).reshape(back_scratch.shape)
    copies += place_out([(back_scratch.at[i], back_ref.at[source]) for i, source in enumerate(sources)], back_sem)
    for copy in copies:
        copy.wait()


def scaled_rows(here, rank, gate, weight, blocks, slots, capacity, buffers):
    devices = rank.shape[1]
    hidden, width = weight.shape
    count = len(blocks)
    tokens = blocks[0].shape[0]
    vmem, anywhere = pl.BlockSpec(memory_space=pltpu.VMEM), pl.BlockSpec(memory_space=pltpu.HBM)
    return pl.pallas_call(
        functools.partial(scale_kernel, capacity, slots, len(buffers)),
        in_specs=[pl.BlockSpec(memory_space=pltpu.SMEM)] + [vmem] * (3 + count) + [anywhere] * len(buffers),
        out_specs=[anywhere, anywhere, vmem],
        out_shape=[
            jax.ShapeDtypeStruct((devices, capacity, width), BF16),
            jax.ShapeDtypeStruct((devices, capacity, hidden), BF16),
            jax.ShapeDtypeStruct((count, capacity, width), BF16),
        ],
        scratch_shapes=[
            pltpu.VMEM((count, capacity, width), BF16),
            pltpu.VMEM((count, capacity, hidden), BF16),
            pltpu.SemaphoreType.DMA((count,)),
            pltpu.SemaphoreType.DMA((count,)),
        ],
        input_output_aliases={4 + count + i: i for i in range(len(buffers))},
        compiler_params=pltpu.CompilerParams(vmem_limit_bytes=60 * MIB),
        cost_estimate=BRIEF,
        name="scaled_rows",
    )(here, rank, gate, weight, *blocks, *buffers)


def sibling_kernel(capacity, slots, here_ref, weight_ref, rows_ref, _z, _back, z_ref, back_ref, token_ref, back_scratch, z_sem, back_sem):
    count = 2 * len(slots)
    sources = lane_sources(here_ref[0], slots, 1 - here_ref[0] % 2)
    copies = place_out([(rows_ref.at[i], z_ref.at[source]) for i, source in enumerate(sources)], z_sem)
    flat = rows_ref[...].reshape(count * capacity, rows_ref.shape[2])
    back = lax.dot_general(flat, weight_ref[...], (((1,), (1,)), ((), ())), preferred_element_type=F32)
    back_scratch[...] = back.astype(BF16).reshape(back_scratch.shape)
    copies += place_out([(back_scratch.at[i], back_ref.at[source]) for i, source in enumerate(sources)], back_sem)
    token_ref[...] = jnp.zeros_like(token_ref)
    for copy in copies:
        copy.wait()


def sibling_rows(here, weight, rows, slots, z_rows, back):
    count, capacity, width = rows.shape
    hidden = weight.shape[0]
    vmem, anywhere = pl.BlockSpec(memory_space=pltpu.VMEM), pl.BlockSpec(memory_space=pltpu.HBM)
    return pl.pallas_call(
        functools.partial(sibling_kernel, capacity, slots),
        in_specs=[pl.BlockSpec(memory_space=pltpu.SMEM), vmem, vmem, anywhere, anywhere],
        out_specs=[anywhere, anywhere, vmem],
        out_shape=[
            jax.ShapeDtypeStruct(z_rows.shape, BF16),
            jax.ShapeDtypeStruct(back.shape, BF16),
            jax.ShapeDtypeStruct((8, 128), F32),
        ],
        scratch_shapes=[
            pltpu.VMEM((count, capacity, hidden), BF16),
            pltpu.SemaphoreType.DMA((count,)),
            pltpu.SemaphoreType.DMA((count,)),
        ],
        input_output_aliases={3: 0, 4: 1},
        compiler_params=pltpu.CompilerParams(vmem_limit_bytes=60 * MIB),
        cost_estimate=BRIEF,
        name="sibling_rows",
    )(here, weight, rows, z_rows, back)


def forward_kernel(capacity, turn, here_ref, rank_ref, gate_ref, h_ref, weight_ref, out_ref):
    each = out_ref.shape[0]
    lane = (here_ref[0] % 2) ^ turn
    flat = h_ref[...].reshape(each * capacity, h_ref.shape[3])
    out = jnp.dot(flat, weight_ref[...], preferred_element_type=F32).astype(BF16).astype(F32)
    for j in range(each):
        source = (pl.program_id(0) * each + j) * 2 + lane
        gate = gate_column(gate_ref, chosen_rows(rank_ref, 0, source, capacity), 0, source)
        out_ref[j] = (out[j * capacity:(j + 1) * capacity, :] * gate).astype(BF16)


def forward_rows(here, rank, gate, rows_h, weight, turn, each=4):
    devices, capacity, hidden = rows_h.shape
    width = weight.shape[1]
    whole = pl.BlockSpec(rank.shape, lambda i, here: (0, 0, 0))
    return pl.pallas_call(
        functools.partial(forward_kernel, capacity, turn),
        grid_spec=pltpu.PrefetchScalarGridSpec(
            num_scalar_prefetch=1,
            grid=(devices // 2 // each,),
            in_specs=[
                whole,
                whole,
                pl.BlockSpec((each, 1, capacity, hidden), lambda i, here: (i, (here[0] % 2) ^ turn, 0, 0)),
                pl.BlockSpec((hidden, width), lambda i, here: (0, 0)),
            ],
            out_specs=pl.BlockSpec((each, capacity, width), lambda i, here: (i, 0, 0)),
        ),
        out_shape=jax.ShapeDtypeStruct((devices // 2, capacity, width), BF16),
        compiler_params=pltpu.CompilerParams(vmem_limit_bytes=60 * MIB),
        cost_estimate=BRIEF,
        name="forward_rows",
    )(here, rank, gate, rows_h.reshape(devices // 2, 2, capacity, hidden), weight)


ORDER = (3, 2, 1, 0)


def sum_kernel(capacity, turn, here_ref, rank_ref, own_ref, other_ref, *part_refs):
    for step, slot in enumerate(ORDER):

        @pl.when(pl.program_id(0) == step)
        def _():
            source = lane_sources(here_ref[0], (slot,), here_ref[0] % 2)[turn]
            both = [one_hot(chosen_rows(rank_ref, side, source, capacity)) for side in range(2)]
            rows = jnp.concatenate([own_ref[0], other_ref[0]], axis=0)
            part = lax.dot_general(
                jnp.concatenate(both, axis=0), rows, (((0,), (0,)), ((), ())), preferred_element_type=F32
            )
            part_refs[step][...] = part.astype(BF16)


def summed(here, rank, own, other, turn):
    _, capacity, width = own.shape
    tokens = rank.shape[2]

    def block(i, here):
        place = jnp.int32(0)
        for step, slot in enumerate(ORDER):
            place = jnp.where(i == step, lane_sources(here[0], (slot,), 0)[turn] // 2, place)
        return (place, 0, 0)

    return pl.pallas_call(
        functools.partial(sum_kernel, capacity, turn),
        grid_spec=pltpu.PrefetchScalarGridSpec(
            num_scalar_prefetch=1,
            grid=(len(ORDER),),
            in_specs=[
                pl.BlockSpec(rank.shape, lambda i, here: (0, 0, 0)),
                pl.BlockSpec((1, capacity, width), block),
                pl.BlockSpec((1, capacity, width), block),
            ],
            out_specs=[pl.BlockSpec((tokens, width), lambda i, here: (0, 0))] * len(ORDER),
        ),
        out_shape=[jax.ShapeDtypeStruct((tokens, width), BF16)] * len(ORDER),
        compiler_params=pltpu.CompilerParams(vmem_limit_bytes=60 * MIB),
        cost_estimate=BRIEF,
        name="summed",
    )(here, rank, own, other)


def added(*values):
    total = values[0].astype(F32)
    for value in values[1:]:
        total = total + value.astype(F32)
    return total.astype(BF16)


def passed(pairs, value):
    return lax.ppermute(value, "expert", [(a * 4 + lane, b * 4 + lane) for a, b in pairs for lane in range(4)])


def swapped_with(value, bit):
    devices = lax.axis_size("expert")
    return lax.ppermute(value, "expert", [(i, i ^ bit) for i in range(devices)])


OUTER, INNER = ((0, 1), (3, 2)), ((1, 2), (2, 1))
ENDS, ENDS_SWAP = ((1, 0), (2, 3)), ((0, 3), (3, 0))


def gate_kernel(*refs):
    pass


def after(values, *waited):
    count = len(values)
    anywhere = pl.BlockSpec(memory_space=pl.ANY)
    return pl.pallas_call(
        gate_kernel,
        in_specs=[anywhere] * (count + len(waited)),
        out_specs=[anywhere] * count,
        out_shape=[jax.ShapeDtypeStruct(value.shape, value.dtype) for value in values],
        input_output_aliases={i: i for i in range(count)},
        compiler_params=pltpu.CompilerParams(vmem_limit_bytes=60 * MIB),
        cost_estimate=BRIEF,
        name="after",
    )(*values, *waited)


def dense_shards(h_rows, gates, expert_ids, cotangent, down_weight, swapped):
    devices = lax.axis_size("expert")
    here = lax.axis_index("expert").reshape(1)
    tokens, top, hidden = h_rows.shape
    capacity = min(tokens, 3 * tokens * top // (2 * devices))
    weight = down_weight[0]
    slot_ids = slots_of(expert_ids, swapped, devices)
    h_flat = h_rows.reshape(-1, hidden)

    own = cotangent
    from_end, from_inner, from_near_end = passed(OUTER, own), passed(INNER, own), passed(ENDS, own)
    from_far_end = passed(ENDS_SWAP, own)
    own_y = swapped_with(own, 2)
    routing = jnp.concatenate([slot_ids.T.astype(F32), gates.T], axis=0)
    routing = jnp.broadcast_to(routing, (devices,) + routing.shape)
    place, send_h = pack(slot_ids.reshape(1, -1), h_flat, devices, capacity)
    routing = lax.all_to_all(routing, "expert", split_axis=0, concat_axis=0, tiled=True)
    rank, gate = route(here, routing, top)
    send_h, = after((send_h,), from_end, from_inner, from_near_end, from_far_end, own_y, rank)
    rows_h = lax.all_to_all(
        send_h.reshape(devices, capacity, hidden), "expert", split_axis=0, concat_axis=0, tiled=True
    )
    near, last = added(from_inner, from_near_end), added(from_end, from_far_end)
    middle_inner, middle_end = passed(INNER, from_end), passed(ENDS, from_inner)
    near_y = swapped_with(near, 2)
    middle = added(middle_inner, middle_end)
    last_y = swapped_with(last, 2)
    middle_y = swapped_with(middle, 2)

    z_rows, back, sibling = scaled_rows(here, rank, gate, weight, [own, own_y, near, near_y], (0, 1), capacity, [])
    sibling = swapped_with(sibling, 1)
    z_rows, back, early = sibling_rows(here, weight, sibling, (0, 1), z_rows, back)
    rows_h, = after((rows_h,), early, middle, last_y)
    other = swapped_with(forward_rows(here, rank, gate, rows_h, weight, 1), 1)
    mine = forward_rows(here, rank, gate, rows_h, weight, 0)
    leaving = summed(here, rank, mine, other, 1)
    across = [swapped_with(part, 2) for part in leaving]
    last_y, = after((last_y,), leaving[0])
    z_rows, back, sibling_last = scaled_rows(
        here, rank, gate, weight, [middle, middle_y, last, last_y], (2, 3), capacity, [z_rows, back]
    )
    sibling_last = swapped_with(sibling_last, 1)
    z_rows, back, _ = sibling_rows(here, weight, sibling_last, (2, 3), z_rows, back)
    back_rows = lax.all_to_all(back, "expert", split_axis=0, concat_axis=0, tiled=True).reshape(-1, hidden)

    beside = summed(here, rank, mine, other, 0)
    far, mid, close, kept = zip(beside, across)
    far, mid, close = added(*far), added(*mid), added(*close)
    ends = passed(ENDS_SWAP, far)
    mid_outer, mid_inner = passed(OUTER, mid), passed(INNER, mid)
    close_outer = passed(OUTER, close)
    close_inner = passed(INNER, added(close, mid_outer))
    far_ends = passed(ENDS, added(far, mid_inner))
    mixed = added(*kept, ends, close_outer, close_inner, far_ends)

    grad_sum = lax.dot_general(
        rows_h.reshape(-1, hidden), z_rows.reshape(devices * capacity, -1), (((0,), (0,)), ((), ())),
        preferred_element_type=F32,
    )
    h_grad, gate_grad = unpack(place.reshape(-1, 1), gates.reshape(-1, 1), h_flat, back_rows)
    return (
        mixed,
        gate_grad.reshape(tokens, top),
        h_grad.reshape(tokens, top, hidden),
        grad_sum.astype(BF16)[None],
    )


def shards(h_rows, *rest):
    devices = lax.axis_size("expert")
    dense = devices == 16 and devices <= 2 * h_rows.shape[1]
    return (dense_shards if dense else sparse_shards)(h_rows, *rest)


def solution(mesh):
    in_specs = (
        P(("groups", "expert"), None, None),
        P(("groups", "expert"), None),
        P(("groups", "expert"), None),
        P(("groups", "expert"), None),
        P("expert", None, None),
        P(),
    )
    out_specs = (
        P(("groups", "expert"), None),
        P(("groups", "expert"), None),
        P(("groups", "expert"), None, None),
        P(("groups", "expert"), None, None),
    )
    return jax.shard_map(shards, mesh=mesh, in_specs=in_specs, out_specs=out_specs, check_vma=False)
```

```python
import functools

import jax
import jax.numpy as jnp
from jax import lax
from jax.experimental import pallas as pl
from jax.experimental.pallas import tpu as pltpu
from jax.sharding import PartitionSpec as P

F32 = jnp.float32
BF16 = jnp.bfloat16
MIB = 1 << 20
BRIEF = pl.CostEstimate(flops=0, transcendentals=0, bytes_accessed=0)


def slots_of(ids, swapped, devices):
    half_way = devices // 2
    table = jnp.arange(devices, dtype=jnp.int32)
    table = (table + half_way * swapped[table % half_way]) % devices
    return jnp.sum(jnp.where(ids[..., None] == jnp.arange(devices, dtype=jnp.int32), table, 0), axis=-1)


def place_rows(values, target, ranks, devices, capacity):
    buffer = jnp.zeros((devices, capacity, values.shape[-1]), values.dtype)
    return buffer.at[target, ranks].set(values)


def sparse_shards(h_rows, gates, expert_ids, cotangent, down_weight, swapped):
    devices = lax.axis_size("expert")
    tokens_here, top_count, hidden = h_rows.shape
    width = cotangent.shape[1]
    capacity = min(tokens_here, 3 * tokens_here * top_count // (2 * devices))
    experts = jnp.arange(devices, dtype=jnp.int32)
    weight = down_weight[0]
    flat_ids = slots_of(expert_ids.reshape(-1), swapped, devices)
    onehot = (flat_ids[:, None] == experts[None, :]).astype(jnp.int32)
    ranks = jnp.sum((jnp.cumsum(onehot, axis=0) - onehot) * onehot, axis=1)
    send_h = place_rows(h_rows.reshape(-1, hidden), flat_ids, ranks, devices, capacity)
    received = lax.all_to_all(send_h, "expert", split_axis=0, concat_axis=0, tiled=True)
    result = jnp.einsum("sch,hd->scd", received, weight, preferred_element_type=F32)
    results = result.astype(BF16)
    returned = lax.all_to_all(results, "expert", split_axis=0, concat_axis=0, tiled=True)
    out_rows = returned[flat_ids, ranks].reshape(tokens_here, top_count, width)
    mixed = jnp.einsum("tk,tkd->td", gates, out_rows.astype(F32)).astype(BF16)
    gate_grad = jnp.einsum("td,tkd->tk", cotangent, out_rows, preferred_element_type=F32)
    scaled = (gates[:, :, None] * cotangent[:, None, :].astype(F32)).astype(BF16)
    send_z = place_rows(scaled.reshape(-1, width), flat_ids, ranks, devices, capacity)
    recv_z = lax.all_to_all(send_z, "expert", split_axis=0, concat_axis=0, tiled=True)
    flat_z = recv_z.reshape(-1, width)
    flat_h = received.reshape(-1, hidden)
    grad_sum = lax.dot_general(flat_h, flat_z, (((0,), (0,)), ((), ())), preferred_element_type=F32)
    back = lax.dot_general(flat_z, weight, (((1,), (1,)), ((), ())), preferred_element_type=F32).astype(BF16)
    back_rows = lax.all_to_all(
        back.reshape(devices, capacity, hidden), "expert", split_axis=0, concat_axis=0, tiled=True
    )
    h_grad = back_rows[flat_ids, ranks].reshape(tokens_here, top_count, hidden)
    return (mixed, gate_grad, h_grad, grad_sum.astype(BF16)[None])


def upper(size):
    rows = lax.broadcasted_iota(jnp.int32, (size, size), 0)
    columns = lax.broadcasted_iota(jnp.int32, (size, size), 1)
    return (rows < columns).astype(F32).astype(BF16)


def pack_kernel(devices, capacity, ids_ref, h_ref, place_ref, sent_ref, place_scratch):
    pairs = ids_ref.shape[1]
    rows = sent_ref.shape[0]

    @pl.when(pl.program_id(0) == 0)
    def _():
        before = jnp.zeros((devices, 1), F32)
        for tile in range(pairs // 128):
            ids = ids_ref[:, tile * 128:(tile + 1) * 128]
            named = lax.broadcasted_iota(jnp.int32, (devices, 128), 0) == ids
            ones = jnp.where(named, 1.0, 0.0)
            rank = jnp.dot(ones.astype(BF16), upper(128), preferred_element_type=F32) + before
            before = before + jnp.sum(ones, axis=1, keepdims=True)
            rank = jnp.sum(jnp.where(named, rank, 0.0), axis=0, keepdims=True)
            place_scratch[:, tile * 128:(tile + 1) * 128] = ids * capacity + rank.astype(jnp.int32)
        place_ref[...] = place_scratch[...]

    first = pl.program_id(0) * rows
    wanted = lax.broadcasted_iota(jnp.int32, (rows, pairs), 0) + first
    chosen = jnp.where(wanted == place_scratch[...], 1.0, 0.0).astype(BF16)
    sent_ref[...] = jnp.dot(chosen, h_ref[...], preferred_element_type=F32).astype(BF16)


def pack(ids, h_flat, devices, capacity, steps=4):
    pairs, hidden = h_flat.shape
    rows = devices * capacity // steps
    return pl.pallas_call(
        functools.partial(pack_kernel, devices, capacity),
        grid=(steps,),
        in_specs=[
            pl.BlockSpec((1, pairs), lambda i: (0, 0)),
            pl.BlockSpec((pairs, hidden), lambda i: (0, 0)),
        ],
        out_specs=[
            pl.BlockSpec((1, pairs), lambda i: (0, 0)),
            pl.BlockSpec((rows, hidden), lambda i: (i, 0)),
        ],
        out_shape=[
            jax.ShapeDtypeStruct((1, pairs), jnp.int32),
            jax.ShapeDtypeStruct((devices * capacity, hidden), BF16),
        ],
        scratch_shapes=[pltpu.VMEM((1, pairs), jnp.int32)],
        compiler_params=pltpu.CompilerParams(vmem_limit_bytes=60 * MIB),
        cost_estimate=BRIEF,
        name="pack",
    )(ids, h_flat)


def unpack_kernel(slots, place_ref, gate_ref, h_ref, back_ref, grad_ref, gate_grad_ref):
    rows = place_ref.shape[0]
    chosen = lax.broadcasted_iota(jnp.int32, (rows, slots), 1) == place_ref[...]
    grad = jnp.dot(jnp.where(chosen, 1.0, 0.0).astype(BF16), back_ref[...], preferred_element_type=F32)
    grad_ref[...] = grad.astype(BF16)
    gate_grad_ref[...] = jnp.sum(grad * h_ref[...].astype(F32), axis=1, keepdims=True) / gate_ref[...]


def unpack(place, gates, h_flat, back_rows, steps=4):
    pairs, hidden = h_flat.shape
    slots = back_rows.shape[0]
    rows = pairs // steps
    return pl.pallas_call(
        functools.partial(unpack_kernel, slots),
        grid=(steps,),
        in_specs=[
            pl.BlockSpec((rows, 1), lambda i: (i, 0)),
            pl.BlockSpec((rows, 1), lambda i: (i, 0)),
            pl.BlockSpec((rows, hidden), lambda i: (i, 0)),
            pl.BlockSpec((slots, hidden), lambda i: (0, 0)),
        ],
        out_specs=[
            pl.BlockSpec((rows, hidden), lambda i: (i, 0)),
            pl.BlockSpec((rows, 1), lambda i: (i, 0)),
        ],
        out_shape=[
            jax.ShapeDtypeStruct((pairs, hidden), BF16),
            jax.ShapeDtypeStruct((pairs, 1), F32),
        ],
        compiler_params=pltpu.CompilerParams(vmem_limit_bytes=60 * MIB),
        cost_estimate=BRIEF,
        name="unpack",
    )(place, gates, h_flat, back_rows)


def line_slots(position):
    near = jnp.minimum(position, 3 - position)
    turned = (near, near + 1, near + 2, 3 - 3 * near)
    return [jnp.where(position < 2, slot, 3 - slot) for slot in turned]


def route_kernel(devices, top, here_ref, routing_ref, rank_ref, gate_ref):
    for side in range(2):
        mine = (here_ref[0] ^ side).astype(F32)
        marks, picked = [], []
        for source in range(devices):
            ids = routing_ref[source, :top, :]
            gates = routing_ref[source, top:, :]
            named = ids == mine
            marks.append(jnp.sum(jnp.where(named, 1.0, 0.0), axis=0, keepdims=True))
            picked.append(jnp.sum(jnp.where(named, gates, 0.0), axis=0, keepdims=True))
        mark = jnp.concatenate(marks, axis=0)
        rank = jnp.dot(mark.astype(BF16), upper(mark.shape[1]), preferred_element_type=F32)
        rank_ref[side] = jnp.where(mark > 0, rank, -1.0).astype(jnp.int32)
        gate_ref[side] = jnp.concatenate(picked, axis=0)


def route(here, routing, top):
    devices, _, tokens = routing.shape
    return pl.pallas_call(
        functools.partial(route_kernel, devices, top),
        in_specs=[pl.BlockSpec(memory_space=pltpu.SMEM), pl.BlockSpec(memory_space=pltpu.VMEM)],
        out_specs=[pl.BlockSpec(memory_space=pltpu.VMEM)] * 2,
        out_shape=[
            jax.ShapeDtypeStruct((2, devices, tokens), jnp.int32),
            jax.ShapeDtypeStruct((2, devices, tokens), F32),
        ],
        cost_estimate=BRIEF,
        name="route",
    )(here, routing)


def chosen_rows(rank_ref, side, source, capacity):
    rank = rank_ref[side, pl.ds(source, 1), :]
    return lax.broadcasted_iota(jnp.int32, (capacity, rank.shape[1]), 0) == rank


def gate_column(gate_ref, chosen, side, source):
    return jnp.sum(jnp.where(chosen, gate_ref[side, pl.ds(source, 1), :], 0.0), axis=1, keepdims=True)


def one_hot(chosen):
    return jnp.where(chosen, 1.0, 0.0).astype(BF16)


def lane_sources(here, slots, lane):
    line, across = here // 4, (here // 2) % 2
    places = line_slots(line)
    return [places[slot] * 4 + (across ^ turn) * 2 + lane for slot in slots for turn in range(2)]


def place_out(pieces, sem):
    copies = [pltpu.make_async_copy(source, target, sem.at[i]) for i, (source, target) in enumerate(pieces)]
    for copy in copies:
        copy.start()
    return copies


def scale_kernel(capacity, slots, held, here_ref, rank_ref, gate_ref, weight_ref, *refs):
    count = 2 * len(slots)
    blocks, refs = refs[:count], refs[count + held:]
    z_ref, back_ref, sibling_ref, z_scratch, back_scratch, z_sem, back_sem = refs
    sources = lane_sources(here_ref[0], slots, here_ref[0] % 2)
    for i, source in enumerate(sources):
        chosen = [chosen_rows(rank_ref, side, source, capacity) for side in range(2)]
        gates = [gate_column(gate_ref, chosen[side], side, source) for side in range(2)]
        both = jnp.concatenate([one_hot(chosen[0]), one_hot(chosen[1])], axis=0)
        rows = jnp.dot(both, blocks[i][...], preferred_element_type=F32)
        z_scratch[i] = (rows[:capacity] * gates[0]).astype(BF16)
        sibling_ref[i] = (rows[capacity:] * gates[1]).astype(BF16)
    copies = place_out([(z_scratch.at[i], z_ref.at[source]) for i, source in enumerate(sources)], z_sem)
    flat = z_scratch[...].reshape(count * capacity, z_scratch.shape[2])
    back = lax.dot_general(flat, weight_ref[...], (((1,), (1,)), ((), ())), preferred_element_type=F32)
    back_scratch[...] = back.astype(BF16).reshape(back_scratch.shape)
    copies += place_out([(back_scratch.at[i], back_ref.at[source]) for i, source in enumerate(sources)], back_sem)
    for copy in copies:
        copy.wait()


def scaled_rows(here, rank, gate, weight, blocks, slots, capacity, buffers):
    devices = rank.shape[1]
    hidden, width = weight.shape
    count = len(blocks)
    tokens = blocks[0].shape[0]
    vmem, anywhere = pl.BlockSpec(memory_space=pltpu.VMEM), pl.BlockSpec(memory_space=pltpu.HBM)
    return pl.pallas_call(
        functools.partial(scale_kernel, capacity, slots, len(buffers)),
        in_specs=[pl.BlockSpec(memory_space=pltpu.SMEM)] + [vmem] * (3 + count) + [anywhere] * len(buffers),
        out_specs=[anywhere, anywhere, vmem],
        out_shape=[
            jax.ShapeDtypeStruct((devices, capacity, width), BF16),
            jax.ShapeDtypeStruct((devices, capacity, hidden), BF16),
            jax.ShapeDtypeStruct((count, capacity, width), BF16),
        ],
        scratch_shapes=[
            pltpu.VMEM((count, capacity, width), BF16),
            pltpu.VMEM((count, capacity, hidden), BF16),
            pltpu.SemaphoreType.DMA((count,)),
            pltpu.SemaphoreType.DMA((count,)),
        ],
        input_output_aliases={4 + count + i: i for i in range(len(buffers))},
        compiler_params=pltpu.CompilerParams(vmem_limit_bytes=60 * MIB),
        cost_estimate=BRIEF,
        name="scaled_rows",
    )(here, rank, gate, weight, *blocks, *buffers)


def sibling_kernel(capacity, slots, here_ref, weight_ref, rows_ref, _z, _back, z_ref, back_ref, token_ref, back_scratch, z_sem, back_sem):
    count = 2 * len(slots)
    sources = lane_sources(here_ref[0], slots, 1 - here_ref[0] % 2)
    copies = place_out([(rows_ref.at[i], z_ref.at[source]) for i, source in enumerate(sources)], z_sem)
    flat = rows_ref[...].reshape(count * capacity, rows_ref.shape[2])
    back = lax.dot_general(flat, weight_ref[...], (((1,), (1,)), ((), ())), preferred_element_type=F32)
    back_scratch[...] = back.astype(BF16).reshape(back_scratch.shape)
    copies += place_out([(back_scratch.at[i], back_ref.at[source]) for i, source in enumerate(sources)], back_sem)
    token_ref[...] = jnp.zeros_like(token_ref)
    for copy in copies:
        copy.wait()


def sibling_rows(here, weight, rows, slots, z_rows, back):
    count, capacity, width = rows.shape
    hidden = weight.shape[0]
    vmem, anywhere = pl.BlockSpec(memory_space=pltpu.VMEM), pl.BlockSpec(memory_space=pltpu.HBM)
    return pl.pallas_call(
        functools.partial(sibling_kernel, capacity, slots),
        in_specs=[pl.BlockSpec(memory_space=pltpu.SMEM), vmem, vmem, anywhere, anywhere],
        out_specs=[anywhere, anywhere, vmem],
        out_shape=[
            jax.ShapeDtypeStruct(z_rows.shape, BF16),
            jax.ShapeDtypeStruct(back.shape, BF16),
            jax.ShapeDtypeStruct((8, 128), F32),
        ],
        scratch_shapes=[
            pltpu.VMEM((count, capacity, hidden), BF16),
            pltpu.SemaphoreType.DMA((count,)),
            pltpu.SemaphoreType.DMA((count,)),
        ],
        input_output_aliases={3: 0, 4: 1},
        compiler_params=pltpu.CompilerParams(vmem_limit_bytes=60 * MIB),
        cost_estimate=BRIEF,
        name="sibling_rows",
    )(here, weight, rows, z_rows, back)


def forward_kernel(capacity, turn, here_ref, rank_ref, gate_ref, h_ref, weight_ref, out_ref):
    each = out_ref.shape[0]
    lane = (here_ref[0] % 2) ^ turn
    flat = h_ref[...].reshape(each * capacity, h_ref.shape[3])
    out = jnp.dot(flat, weight_ref[...], preferred_element_type=F32).astype(BF16).astype(F32)
    for j in range(each):
        source = (pl.program_id(0) * each + j) * 2 + lane
        gate = gate_column(gate_ref, chosen_rows(rank_ref, 0, source, capacity), 0, source)
        out_ref[j] = (out[j * capacity:(j + 1) * capacity, :] * gate).astype(BF16)


def forward_rows(here, rank, gate, rows_h, weight, turn, each=4):
    devices, capacity, hidden = rows_h.shape
    width = weight.shape[1]
    whole = pl.BlockSpec(rank.shape, lambda i, here: (0, 0, 0))
    return pl.pallas_call(
        functools.partial(forward_kernel, capacity, turn),
        grid_spec=pltpu.PrefetchScalarGridSpec(
            num_scalar_prefetch=1,
            grid=(devices // 2 // each,),
            in_specs=[
                whole,
                whole,
                pl.BlockSpec((each, 1, capacity, hidden), lambda i, here: (i, (here[0] % 2) ^ turn, 0, 0)),
                pl.BlockSpec((hidden, width), lambda i, here: (0, 0)),
            ],
            out_specs=pl.BlockSpec((each, capacity, width), lambda i, here: (i, 0, 0)),
        ),
        out_shape=jax.ShapeDtypeStruct((devices // 2, capacity, width), BF16),
        compiler_params=pltpu.CompilerParams(vmem_limit_bytes=60 * MIB),
        cost_estimate=BRIEF,
        name="forward_rows",
    )(here, rank, gate, rows_h.reshape(devices // 2, 2, capacity, hidden), weight)


ORDER = (3, 2, 1, 0)


def sum_kernel(capacity, turn, here_ref, rank_ref, own_ref, other_ref, *part_refs):
    for step, slot in enumerate(ORDER):

        @pl.when(pl.program_id(0) == step)
        def _():
            source = lane_sources(here_ref[0], (slot,), here_ref[0] % 2)[turn]
            both = [one_hot(chosen_rows(rank_ref, side, source, capacity)) for side in range(2)]
            rows = jnp.concatenate([own_ref[0], other_ref[0]], axis=0)
            part = lax.dot_general(
                jnp.concatenate(both, axis=0), rows, (((0,), (0,)), ((), ())), preferred_element_type=F32
            )
            part_refs[step][...] = part.astype(BF16)


def summed(here, rank, own, other, turn):
    _, capacity, width = own.shape
    tokens = rank.shape[2]

    def block(i, here):
        place = jnp.int32(0)
        for step, slot in enumerate(ORDER):
            place = jnp.where(i == step, lane_sources(here[0], (slot,), 0)[turn] // 2, place)
        return (place, 0, 0)

    return pl.pallas_call(
        functools.partial(sum_kernel, capacity, turn),
        grid_spec=pltpu.PrefetchScalarGridSpec(
            num_scalar_prefetch=1,
            grid=(len(ORDER),),
            in_specs=[
                pl.BlockSpec(rank.shape, lambda i, here: (0, 0, 0)),
                pl.BlockSpec((1, capacity, width), block),
                pl.BlockSpec((1, capacity, width), block),
            ],
            out_specs=[pl.BlockSpec((tokens, width), lambda i, here: (0, 0))] * len(ORDER),
        ),
        out_shape=[jax.ShapeDtypeStruct((tokens, width), BF16)] * len(ORDER),
        compiler_params=pltpu.CompilerParams(vmem_limit_bytes=60 * MIB),
        cost_estimate=BRIEF,
        name="summed",
    )(here, rank, own, other)


def added(*values):
    total = values[0].astype(F32)
    for value in values[1:]:
        total = total + value.astype(F32)
    return total.astype(BF16)


def passed(pairs, value):
    return lax.ppermute(value, "expert", [(a * 4 + lane, b * 4 + lane) for a, b in pairs for lane in range(4)])


def swapped_with(value, bit):
    devices = lax.axis_size("expert")
    return lax.ppermute(value, "expert", [(i, i ^ bit) for i in range(devices)])


OUTER, INNER = ((0, 1), (3, 2)), ((1, 2), (2, 1))
ENDS = ((1, 0), (2, 3))


def gate_kernel(*refs):
    pass


def after(values, *waited):
    count = len(values)
    anywhere = pl.BlockSpec(memory_space=pl.ANY)
    return pl.pallas_call(
        gate_kernel,
        in_specs=[anywhere] * (count + len(waited)),
        out_specs=[anywhere] * count,
        out_shape=[jax.ShapeDtypeStruct(value.shape, value.dtype) for value in values],
        input_output_aliases={i: i for i in range(count)},
        compiler_params=pltpu.CompilerParams(vmem_limit_bytes=60 * MIB),
        cost_estimate=BRIEF,
        name="after",
    )(*values, *waited)


def dense_shards(h_rows, gates, expert_ids, cotangent, down_weight, swapped):
    devices = lax.axis_size("expert")
    here = lax.axis_index("expert").reshape(1)
    tokens, top, hidden = h_rows.shape
    capacity = min(tokens, 3 * tokens * top // (2 * devices))
    weight = down_weight[0]
    slot_ids = slots_of(expert_ids, swapped, devices)
    h_flat = h_rows.reshape(-1, hidden)

    routing = jnp.concatenate([slot_ids.T.astype(F32), gates.T], axis=0)
    routing = jnp.broadcast_to(routing, (devices,) + routing.shape)
    routing = lax.all_to_all(routing, "expert", split_axis=0, concat_axis=0, tiled=True)
    rank, gate = route(here, routing, top)
    place, send_h = pack(slot_ids.reshape(1, -1), h_flat, devices, capacity)

    own = cotangent
    from_end, from_inner, from_near_end = passed(OUTER, own), passed(INNER, own), passed(ENDS, own)
    own_y = swapped_with(own, 2)
    near = added(from_inner, from_near_end)
    start_end, start_inner, near = after((from_end, from_inner, near), own_y)
    from_far, from_middle = passed(INNER, start_end), passed(ENDS, start_inner)
    near_y = swapped_with(near, 2)
    middle = added(from_far, from_middle)
    start_far, middle = after((from_far, middle), near_y, rank)
    last = added(from_end, passed(ENDS, start_far))
    middle_y = swapped_with(middle, 2)
    z_rows, back, sibling = scaled_rows(here, rank, gate, weight, [own, own_y, near, near_y], (0, 1), capacity, [])
    send_h, last = after((send_h, last), middle_y, sibling)
    sibling = swapped_with(sibling, 1)
    rows_h = lax.all_to_all(
        send_h.reshape(devices, capacity, hidden), "expert", split_axis=0, concat_axis=0, tiled=True
    )
    last_y = swapped_with(last, 2)

    z_rows, back, _ = sibling_rows(here, weight, sibling, (0, 1), z_rows, back)
    z_rows, back, sibling_last = scaled_rows(
        here, rank, gate, weight, [middle, middle_y, last, last_y], (2, 3), capacity, [z_rows, back]
    )
    sibling_last = swapped_with(sibling_last, 1)
    z_rows, back, ready = sibling_rows(here, weight, sibling_last, (2, 3), z_rows, back)
    back_rows = lax.all_to_all(back, "expert", split_axis=0, concat_axis=0, tiled=True).reshape(-1, hidden)

    rows_h, = after((rows_h,), ready)
    other = swapped_with(forward_rows(here, rank, gate, rows_h, weight, 1), 1)
    mine = forward_rows(here, rank, gate, rows_h, weight, 0)
    across = [swapped_with(part, 2) for part in summed(here, rank, mine, other, 1)]
    beside = summed(here, rank, mine, other, 0)
    far, mid, close, kept = zip(beside, across)
    outer1 = passed(OUTER, added(*far))
    mid = added(*mid, outer1)
    outer2, inner2 = passed(OUTER, mid), passed(INNER, mid)
    close, = after((added(*close, outer2),), back_rows)
    outer3, inner3 = passed(OUTER, close), passed(INNER, close)
    ends3 = passed(ENDS, added(*far, inner2))
    mixed = added(*kept, outer3, inner3, ends3)

    grad_sum = lax.dot_general(
        rows_h.reshape(-1, hidden), z_rows.reshape(devices * capacity, -1), (((0,), (0,)), ((), ())),
        preferred_element_type=F32,
    )
    h_grad, gate_grad = unpack(place.reshape(-1, 1), gates.reshape(-1, 1), h_flat, back_rows)
    return (
        mixed,
        gate_grad.reshape(tokens, top),
        h_grad.reshape(tokens, top, hidden),
        grad_sum.astype(BF16)[None],
    )


def shards(h_rows, *rest):
    devices = lax.axis_size("expert")
    dense = devices == 16 and devices <= 2 * h_rows.shape[1]
    return (dense_shards if dense else sparse_shards)(h_rows, *rest)


def solution(mesh):
    in_specs = (
        P(("groups", "expert"), None, None),
        P(("groups", "expert"), None),
        P(("groups", "expert"), None),
        P(("groups", "expert"), None),
        P("expert", None, None),
        P(),
    )
    out_specs = (
        P(("groups", "expert"), None),
        P(("groups", "expert"), None),
        P(("groups", "expert"), None, None),
        P(("groups", "expert"), None, None),
    )
    return jax.shard_map(shards, mesh=mesh, in_specs=in_specs, out_specs=out_specs, check_vma=False)
```

```python
import functools

import jax
import jax.numpy as jnp
from jax import lax
from jax.experimental import pallas as pl
from jax.experimental.pallas import tpu as pltpu
from jax.sharding import PartitionSpec as P

F32 = jnp.float32
BF16 = jnp.bfloat16
MIB = 1 << 20
BRIEF = pl.CostEstimate(flops=0, transcendentals=0, bytes_accessed=0)


def slots_of(ids, swapped, devices):
    half_way = devices // 2
    table = jnp.arange(devices, dtype=jnp.int32)
    table = (table + half_way * swapped[table % half_way]) % devices
    return jnp.sum(jnp.where(ids[..., None] == jnp.arange(devices, dtype=jnp.int32), table, 0), axis=-1)


def place_rows(values, target, ranks, devices, capacity):
    buffer = jnp.zeros((devices, capacity, values.shape[-1]), values.dtype)
    return buffer.at[target, ranks].set(values)


def sparse_shards(h_rows, gates, expert_ids, cotangent, down_weight, swapped):
    devices = lax.axis_size("expert")
    tokens_here, top_count, hidden = h_rows.shape
    width = cotangent.shape[1]
    capacity = min(tokens_here, 3 * tokens_here * top_count // (2 * devices))
    experts = jnp.arange(devices, dtype=jnp.int32)
    weight = down_weight[0]
    flat_ids = slots_of(expert_ids.reshape(-1), swapped, devices)
    onehot = (flat_ids[:, None] == experts[None, :]).astype(jnp.int32)
    ranks = jnp.sum((jnp.cumsum(onehot, axis=0) - onehot) * onehot, axis=1)
    send_h = place_rows(h_rows.reshape(-1, hidden), flat_ids, ranks, devices, capacity)
    received = lax.all_to_all(send_h, "expert", split_axis=0, concat_axis=0, tiled=True)
    result = jnp.einsum("sch,hd->scd", received, weight, preferred_element_type=F32)
    results = result.astype(BF16)
    returned = lax.all_to_all(results, "expert", split_axis=0, concat_axis=0, tiled=True)
    out_rows = returned[flat_ids, ranks].reshape(tokens_here, top_count, width)
    mixed = jnp.einsum("tk,tkd->td", gates, out_rows.astype(F32)).astype(BF16)
    gate_grad = jnp.einsum("td,tkd->tk", cotangent, out_rows, preferred_element_type=F32)
    scaled = (gates[:, :, None] * cotangent[:, None, :].astype(F32)).astype(BF16)
    send_z = place_rows(scaled.reshape(-1, width), flat_ids, ranks, devices, capacity)
    recv_z = lax.all_to_all(send_z, "expert", split_axis=0, concat_axis=0, tiled=True)
    flat_z = recv_z.reshape(-1, width)
    flat_h = received.reshape(-1, hidden)
    grad_sum = lax.dot_general(flat_h, flat_z, (((0,), (0,)), ((), ())), preferred_element_type=F32)
    back = lax.dot_general(flat_z, weight, (((1,), (1,)), ((), ())), preferred_element_type=F32).astype(BF16)
    back_rows = lax.all_to_all(
        back.reshape(devices, capacity, hidden), "expert", split_axis=0, concat_axis=0, tiled=True
    )
    h_grad = back_rows[flat_ids, ranks].reshape(tokens_here, top_count, hidden)
    return (mixed, gate_grad, h_grad, grad_sum.astype(BF16)[None])


def upper(size):
    rows = lax.broadcasted_iota(jnp.int32, (size, size), 0)
    columns = lax.broadcasted_iota(jnp.int32, (size, size), 1)
    return (rows < columns).astype(F32).astype(BF16)


def pack_kernel(devices, capacity, ids_ref, h_ref, place_ref, sent_ref, place_scratch):
    pairs = ids_ref.shape[1]
    rows = sent_ref.shape[0]

    @pl.when(pl.program_id(0) == 0)
    def _():
        before = jnp.zeros((devices, 1), F32)
        for tile in range(pairs // 128):
            ids = ids_ref[:, tile * 128:(tile + 1) * 128]
            named = lax.broadcasted_iota(jnp.int32, (devices, 128), 0) == ids
            ones = jnp.where(named, 1.0, 0.0)
            rank = jnp.dot(ones.astype(BF16), upper(128), preferred_element_type=F32) + before
            before = before + jnp.sum(ones, axis=1, keepdims=True)
            rank = jnp.sum(jnp.where(named, rank, 0.0), axis=0, keepdims=True)
            place_scratch[:, tile * 128:(tile + 1) * 128] = ids * capacity + rank.astype(jnp.int32)
        place_ref[...] = place_scratch[...]

    first = pl.program_id(0) * rows
    wanted = lax.broadcasted_iota(jnp.int32, (rows, pairs), 0) + first
    chosen = jnp.where(wanted == place_scratch[...], 1.0, 0.0).astype(BF16)
    sent_ref[...] = jnp.dot(chosen, h_ref[...], preferred_element_type=F32).astype(BF16)


def pack(ids, h_flat, devices, capacity, steps=4):
    pairs, hidden = h_flat.shape
    rows = devices * capacity // steps
    return pl.pallas_call(
        functools.partial(pack_kernel, devices, capacity),
        grid=(steps,),
        in_specs=[
            pl.BlockSpec((1, pairs), lambda i: (0, 0)),
            pl.BlockSpec((pairs, hidden), lambda i: (0, 0)),
        ],
        out_specs=[
            pl.BlockSpec((1, pairs), lambda i: (0, 0)),
            pl.BlockSpec((rows, hidden), lambda i: (i, 0)),
        ],
        out_shape=[
            jax.ShapeDtypeStruct((1, pairs), jnp.int32),
            jax.ShapeDtypeStruct((devices * capacity, hidden), BF16),
        ],
        scratch_shapes=[pltpu.VMEM((1, pairs), jnp.int32)],
        compiler_params=pltpu.CompilerParams(vmem_limit_bytes=60 * MIB),
        cost_estimate=BRIEF,
        name="pack",
    )(ids, h_flat)


def unpack_kernel(slots, place_ref, gate_ref, h_ref, back_ref, grad_ref, gate_grad_ref):
    rows = place_ref.shape[0]
    chosen = lax.broadcasted_iota(jnp.int32, (rows, slots), 1) == place_ref[...]
    grad = jnp.dot(jnp.where(chosen, 1.0, 0.0).astype(BF16), back_ref[...], preferred_element_type=F32)
    grad_ref[...] = grad.astype(BF16)
    gate_grad_ref[...] = jnp.sum(grad * h_ref[...].astype(F32), axis=1, keepdims=True) / gate_ref[...]


def unpack(place, gates, h_flat, back_rows, steps=4):
    pairs, hidden = h_flat.shape
    slots = back_rows.shape[0]
    rows = pairs // steps
    return pl.pallas_call(
        functools.partial(unpack_kernel, slots),
        grid=(steps,),
        in_specs=[
            pl.BlockSpec((rows, 1), lambda i: (i, 0)),
            pl.BlockSpec((rows, 1), lambda i: (i, 0)),
            pl.BlockSpec((rows, hidden), lambda i: (i, 0)),
            pl.BlockSpec((slots, hidden), lambda i: (0, 0)),
        ],
        out_specs=[
            pl.BlockSpec((rows, hidden), lambda i: (i, 0)),
            pl.BlockSpec((rows, 1), lambda i: (i, 0)),
        ],
        out_shape=[
            jax.ShapeDtypeStruct((pairs, hidden), BF16),
            jax.ShapeDtypeStruct((pairs, 1), F32),
        ],
        compiler_params=pltpu.CompilerParams(vmem_limit_bytes=60 * MIB),
        cost_estimate=BRIEF,
        name="unpack",
    )(place, gates, h_flat, back_rows)


def line_slots(position):
    near = jnp.minimum(position, 3 - position)
    turned = (near, near + 1, near + 2, 3 - 3 * near)
    return [jnp.where(position < 2, slot, 3 - slot) for slot in turned]


def route_kernel(devices, top, here_ref, routing_ref, rank_ref, gate_ref):
    for side in range(2):
        mine = (here_ref[0] ^ side).astype(F32)
        marks, picked = [], []
        for source in range(devices):
            ids = routing_ref[source, :top, :]
            gates = routing_ref[source, top:, :]
            named = ids == mine
            marks.append(jnp.sum(jnp.where(named, 1.0, 0.0), axis=0, keepdims=True))
            picked.append(jnp.sum(jnp.where(named, gates, 0.0), axis=0, keepdims=True))
        mark = jnp.concatenate(marks, axis=0)
        rank = jnp.dot(mark.astype(BF16), upper(mark.shape[1]), preferred_element_type=F32)
        rank_ref[side] = jnp.where(mark > 0, rank, -1.0).astype(jnp.int32)
        gate_ref[side] = jnp.concatenate(picked, axis=0)


def route(here, routing, top):
    devices, _, tokens = routing.shape
    return pl.pallas_call(
        functools.partial(route_kernel, devices, top),
        in_specs=[pl.BlockSpec(memory_space=pltpu.SMEM), pl.BlockSpec(memory_space=pltpu.VMEM)],
        out_specs=[pl.BlockSpec(memory_space=pltpu.VMEM)] * 2,
        out_shape=[
            jax.ShapeDtypeStruct((2, devices, tokens), jnp.int32),
            jax.ShapeDtypeStruct((2, devices, tokens), F32),
        ],
        cost_estimate=BRIEF,
        name="route",
    )(here, routing)


def chosen_rows(rank_ref, side, source, capacity):
    rank = rank_ref[side, pl.ds(source, 1), :]
    return lax.broadcasted_iota(jnp.int32, (capacity, rank.shape[1]), 0) == rank


def gate_column(gate_ref, chosen, side, source):
    return jnp.sum(jnp.where(chosen, gate_ref[side, pl.ds(source, 1), :], 0.0), axis=1, keepdims=True)


def one_hot(chosen):
    return jnp.where(chosen, 1.0, 0.0).astype(BF16)


def lane_sources(here, slots, lane):
    line, across = here // 4, (here // 2) % 2
    places = line_slots(line)
    return [places[slot] * 4 + (across ^ turn) * 2 + lane for slot in slots for turn in range(2)]


def place_out(pieces, sem):
    copies = [pltpu.make_async_copy(source, target, sem.at[i]) for i, (source, target) in enumerate(pieces)]
    for copy in copies:
        copy.start()
    return copies


def scale_kernel(capacity, slots, held, here_ref, rank_ref, gate_ref, weight_ref, *refs):
    count = 2 * len(slots)
    blocks, refs = refs[:count], refs[count + held:]
    z_ref, back_ref, sibling_ref, z_scratch, back_scratch, z_sem, back_sem = refs
    sources = lane_sources(here_ref[0], slots, here_ref[0] % 2)
    for i, source in enumerate(sources):
        chosen = [chosen_rows(rank_ref, side, source, capacity) for side in range(2)]
        gates = [gate_column(gate_ref, chosen[side], side, source) for side in range(2)]
        both = jnp.concatenate([one_hot(chosen[0]), one_hot(chosen[1])], axis=0)
        rows = jnp.dot(both, blocks[i][...], preferred_element_type=F32)
        z_scratch[i] = (rows[:capacity] * gates[0]).astype(BF16)
        sibling_ref[i] = (rows[capacity:] * gates[1]).astype(BF16)
    copies = place_out([(z_scratch.at[i], z_ref.at[source]) for i, source in enumerate(sources)], z_sem)
    flat = z_scratch[...].reshape(count * capacity, z_scratch.shape[2])
    back = lax.dot_general(flat, weight_ref[...], (((1,), (1,)), ((), ())), preferred_element_type=F32)
    back_scratch[...] = back.astype(BF16).reshape(back_scratch.shape)
    copies += place_out([(back_scratch.at[i], back_ref.at[source]) for i, source in enumerate(sources)], back_sem)
    for copy in copies:
        copy.wait()


def scaled_rows(here, rank, gate, weight, blocks, slots, capacity, buffers):
    devices = rank.shape[1]
    hidden, width = weight.shape
    count = len(blocks)
    tokens = blocks[0].shape[0]
    vmem, anywhere = pl.BlockSpec(memory_space=pltpu.VMEM), pl.BlockSpec(memory_space=pltpu.HBM)
    return pl.pallas_call(
        functools.partial(scale_kernel, capacity, slots, len(buffers)),
        in_specs=[pl.BlockSpec(memory_space=pltpu.SMEM)] + [vmem] * (3 + count) + [anywhere] * len(buffers),
        out_specs=[anywhere, anywhere, vmem],
        out_shape=[
            jax.ShapeDtypeStruct((devices, capacity, width), BF16),
            jax.ShapeDtypeStruct((devices, capacity, hidden), BF16),
            jax.ShapeDtypeStruct((count, capacity, width), BF16),
        ],
        scratch_shapes=[
            pltpu.VMEM((count, capacity, width), BF16),
            pltpu.VMEM((count, capacity, hidden), BF16),
            pltpu.SemaphoreType.DMA((count,)),
            pltpu.SemaphoreType.DMA((count,)),
        ],
        input_output_aliases={4 + count + i: i for i in range(len(buffers))},
        compiler_params=pltpu.CompilerParams(vmem_limit_bytes=60 * MIB),
        cost_estimate=BRIEF,
        name="scaled_rows",
    )(here, rank, gate, weight, *blocks, *buffers)


def sibling_kernel(capacity, slots, here_ref, weight_ref, rows_ref, _z, _back, z_ref, back_ref, token_ref, back_scratch, z_sem, back_sem):
    count = 2 * len(slots)
    sources = lane_sources(here_ref[0], slots, 1 - here_ref[0] % 2)
    copies = place_out([(rows_ref.at[i], z_ref.at[source]) for i, source in enumerate(sources)], z_sem)
    flat = rows_ref[...].reshape(count * capacity, rows_ref.shape[2])
    back = lax.dot_general(flat, weight_ref[...], (((1,), (1,)), ((), ())), preferred_element_type=F32)
    back_scratch[...] = back.astype(BF16).reshape(back_scratch.shape)
    copies += place_out([(back_scratch.at[i], back_ref.at[source]) for i, source in enumerate(sources)], back_sem)
    token_ref[...] = jnp.zeros_like(token_ref)
    for copy in copies:
        copy.wait()


def sibling_rows(here, weight, rows, slots, z_rows, back):
    count, capacity, width = rows.shape
    hidden = weight.shape[0]
    vmem, anywhere = pl.BlockSpec(memory_space=pltpu.VMEM), pl.BlockSpec(memory_space=pltpu.HBM)
    return pl.pallas_call(
        functools.partial(sibling_kernel, capacity, slots),
        in_specs=[pl.BlockSpec(memory_space=pltpu.SMEM), vmem, vmem, anywhere, anywhere],
        out_specs=[anywhere, anywhere, vmem],
        out_shape=[
            jax.ShapeDtypeStruct(z_rows.shape, BF16),
            jax.ShapeDtypeStruct(back.shape, BF16),
            jax.ShapeDtypeStruct((8, 128), F32),
        ],
        scratch_shapes=[
            pltpu.VMEM((count, capacity, hidden), BF16),
            pltpu.SemaphoreType.DMA((count,)),
            pltpu.SemaphoreType.DMA((count,)),
        ],
        input_output_aliases={3: 0, 4: 1},
        compiler_params=pltpu.CompilerParams(vmem_limit_bytes=60 * MIB),
        cost_estimate=BRIEF,
        name="sibling_rows",
    )(here, weight, rows, z_rows, back)


def forward_kernel(capacity, slots, turn, here_ref, rank_ref, gate_ref, weight_ref, *refs):
    blocks, out_ref = refs[:-1], refs[-1]
    sources = lane_sources(here_ref[0], slots, (here_ref[0] % 2) ^ turn)
    flat = jnp.concatenate([block[0, 0] for block in blocks], axis=0)
    out = jnp.dot(flat, weight_ref[...], preferred_element_type=F32).astype(BF16).astype(F32)
    for j, source in enumerate(sources):
        gate = gate_column(gate_ref, chosen_rows(rank_ref, 0, source, capacity), 0, source)
        out_ref[j] = (out[j * capacity:(j + 1) * capacity, :] * gate).astype(BF16)


def forward_rows(here, rank, gate, rows_h, weight, slots, turn):
    devices, capacity, hidden = rows_h.shape
    width = weight.shape[1]
    count = 2 * len(slots)

    def block(j):
        return lambda i, here: (lane_sources(here[0], slots, 0)[j] // 2, (here[0] % 2) ^ turn, 0, 0)

    whole = pl.BlockSpec(rank.shape, lambda i, here: (0, 0, 0))
    rows = rows_h.reshape(devices // 2, 2, capacity, hidden)
    return pl.pallas_call(
        functools.partial(forward_kernel, capacity, slots, turn),
        grid_spec=pltpu.PrefetchScalarGridSpec(
            num_scalar_prefetch=1,
            grid=(1,),
            in_specs=[whole, whole, pl.BlockSpec((hidden, width), lambda i, here: (0, 0))]
            + [pl.BlockSpec((1, 1, capacity, hidden), block(j)) for j in range(count)],
            out_specs=pl.BlockSpec((count, capacity, width), lambda i, here: (0, 0, 0)),
        ),
        out_shape=jax.ShapeDtypeStruct((count, capacity, width), BF16),
        compiler_params=pltpu.CompilerParams(vmem_limit_bytes=60 * MIB),
        cost_estimate=BRIEF,
        name="forward_rows",
    )(here, rank, gate, weight, *[rows] * count)


def sum_kernel(capacity, slots, turn, here_ref, rank_ref, own_ref, other_ref, *part_refs):
    for step, slot in enumerate(slots):

        @pl.when(pl.program_id(0) == step)
        def _():
            source = lane_sources(here_ref[0], (slot,), here_ref[0] % 2)[turn]
            both = [one_hot(chosen_rows(rank_ref, side, source, capacity)) for side in range(2)]
            rows = jnp.concatenate([own_ref[0], other_ref[0]], axis=0)
            part = lax.dot_general(
                jnp.concatenate(both, axis=0), rows, (((0,), (0,)), ((), ())), preferred_element_type=F32
            )
            part_refs[step][...] = part.astype(BF16)


def summed(here, rank, own, other, slots, turn):
    _, capacity, width = own.shape
    tokens = rank.shape[2]
    block = pl.BlockSpec((1, capacity, width), lambda i, here: (2 * i + turn, 0, 0))
    return pl.pallas_call(
        functools.partial(sum_kernel, capacity, slots, turn),
        grid_spec=pltpu.PrefetchScalarGridSpec(
            num_scalar_prefetch=1,
            grid=(len(slots),),
            in_specs=[pl.BlockSpec(rank.shape, lambda i, here: (0, 0, 0)), block, block],
            out_specs=[pl.BlockSpec((tokens, width), lambda i, here: (0, 0))] * len(slots),
        ),
        out_shape=[jax.ShapeDtypeStruct((tokens, width), BF16)] * len(slots),
        compiler_params=pltpu.CompilerParams(vmem_limit_bytes=60 * MIB),
        cost_estimate=BRIEF,
        name="summed",
    )(here, rank, own, other)


def added(*values):
    total = values[0].astype(F32)
    for value in values[1:]:
        total = total + value.astype(F32)
    return total.astype(BF16)


def passed(pairs, value):
    return lax.ppermute(value, "expert", [(a * 4 + lane, b * 4 + lane) for a, b in pairs for lane in range(4)])


def swapped_with(value, bit):
    devices = lax.axis_size("expert")
    return lax.ppermute(value, "expert", [(i, i ^ bit) for i in range(devices)])


OUTER, INNER = ((0, 1), (3, 2)), ((1, 2), (2, 1))
ENDS = ((1, 0), (2, 3))


def gate_kernel(*refs):
    pass


def after(values, *waited):
    count = len(values)
    anywhere = pl.BlockSpec(memory_space=pl.ANY)
    return pl.pallas_call(
        gate_kernel,
        in_specs=[anywhere] * (count + len(waited)),
        out_specs=[anywhere] * count,
        out_shape=[jax.ShapeDtypeStruct(value.shape, value.dtype) for value in values],
        input_output_aliases={i: i for i in range(count)},
        compiler_params=pltpu.CompilerParams(vmem_limit_bytes=60 * MIB),
        cost_estimate=BRIEF,
        name="after",
    )(*values, *waited)


def dense_shards(h_rows, gates, expert_ids, cotangent, down_weight, swapped):
    devices = lax.axis_size("expert")
    here = lax.axis_index("expert").reshape(1)
    tokens, top, hidden = h_rows.shape
    capacity = min(tokens, 3 * tokens * top // (2 * devices))
    weight = down_weight[0]
    slot_ids = slots_of(expert_ids, swapped, devices)
    h_flat = h_rows.reshape(-1, hidden)

    routing = jnp.concatenate([slot_ids.T.astype(F32), gates.T], axis=0)
    routing = jnp.broadcast_to(routing, (devices,) + routing.shape)
    place, send_h = pack(slot_ids.reshape(1, -1), h_flat, devices, capacity)

    own = cotangent
    from_end, from_inner, from_near_end = passed(OUTER, own), passed(INNER, own), passed(ENDS, own)
    own_y = swapped_with(own, 2)
    near = added(from_inner, from_near_end)
    start_end, start_inner, near = after((from_end, from_inner, near), own_y)
    from_far, from_middle = passed(INNER, start_end), passed(ENDS, start_inner)
    near_y = swapped_with(near, 2)
    middle = added(from_far, from_middle)
    start_far, middle, routing = after((from_far, middle, routing), near_y, send_h)
    last = added(from_end, passed(ENDS, start_far))
    middle_y = swapped_with(middle, 2)
    routing = lax.all_to_all(routing, "expert", split_axis=0, concat_axis=0, tiled=True)
    rank, gate = route(here, routing, top)
    send_h, last = after((send_h, last), middle_y, rank)
    rows_h = lax.all_to_all(
        send_h.reshape(devices, capacity, hidden), "expert", split_axis=0, concat_axis=0, tiled=True
    )
    last_y = swapped_with(last, 2)

    z_rows, back, sibling = scaled_rows(here, rank, gate, weight, [own, own_y, near, near_y], (0, 1), capacity, [])
    sibling = swapped_with(sibling, 1)
    z_rows, back, _ = sibling_rows(here, weight, sibling, (0, 1), z_rows, back)
    z_rows, back, sibling_last = scaled_rows(
        here, rank, gate, weight, [middle, middle_y, last, last_y], (2, 3), capacity, [z_rows, back]
    )
    sibling_last = swapped_with(sibling_last, 1)
    z_rows, back, ready = sibling_rows(here, weight, sibling_last, (2, 3), z_rows, back)
    back_rows = lax.all_to_all(back, "expert", split_axis=0, concat_axis=0, tiled=True).reshape(-1, hidden)

    rows_h, = after((rows_h,), ready)
    beside, across = [], []
    for slots in ((3, 2), (1, 0)):
        other = swapped_with(forward_rows(here, rank, gate, rows_h, weight, slots, 1), 1)
        mine = forward_rows(here, rank, gate, rows_h, weight, slots, 0)
        across += [swapped_with(part, 2) for part in summed(here, rank, mine, other, slots, 1)]
        beside += summed(here, rank, mine, other, slots, 0)
    grad_sum = lax.dot_general(
        rows_h.reshape(-1, hidden), z_rows.reshape(devices * capacity, -1), (((0,), (0,)), ((), ())),
        preferred_element_type=F32,
    )
    weight_grad = grad_sum.astype(BF16)[None]
    far, mid, close, kept = zip(beside, across)
    far = (*after((far[0],), weight_grad), far[1])
    outer1 = passed(OUTER, added(*far))
    mid = added(*mid, outer1)
    outer2, inner2 = passed(OUTER, mid), passed(INNER, mid)
    close, = after((added(*close, outer2),), back_rows)
    outer3, inner3 = passed(OUTER, close), passed(INNER, close)
    ends3 = passed(ENDS, added(*far, inner2))
    mixed = added(*kept, outer3, inner3, ends3)

    h_grad, gate_grad = unpack(place.reshape(-1, 1), gates.reshape(-1, 1), h_flat, back_rows)
    return (
        mixed,
        gate_grad.reshape(tokens, top),
        h_grad.reshape(tokens, top, hidden),
        weight_grad,
    )


def shards(h_rows, *rest):
    devices = lax.axis_size("expert")
    dense = devices == 16 and devices <= 2 * h_rows.shape[1]
    return (dense_shards if dense else sparse_shards)(h_rows, *rest)


def solution(mesh):
    in_specs = (
        P(("groups", "expert"), None, None),
        P(("groups", "expert"), None),
        P(("groups", "expert"), None),
        P(("groups", "expert"), None),
        P("expert", None, None),
        P(),
    )
    out_specs = (
        P(("groups", "expert"), None),
        P(("groups", "expert"), None),
        P(("groups", "expert"), None, None),
        P(("groups", "expert"), None, None),
    )
    return jax.shard_map(shards, mesh=mesh, in_specs=in_specs, out_specs=out_specs, check_vma=False)
```

```python
import functools

import jax
import jax.numpy as jnp
from jax import lax
from jax.experimental import pallas as pl
from jax.experimental.pallas import tpu as pltpu
from jax.sharding import PartitionSpec as P

F32 = jnp.float32
BF16 = jnp.bfloat16
MIB = 1 << 20
BRIEF = pl.CostEstimate(flops=0, transcendentals=0, bytes_accessed=0)


def slots_of(ids, swapped, devices):
    half_way = devices // 2
    table = jnp.arange(devices, dtype=jnp.int32)
    table = (table + half_way * swapped[table % half_way]) % devices
    return jnp.sum(jnp.where(ids[..., None] == jnp.arange(devices, dtype=jnp.int32), table, 0), axis=-1)


def place_rows(values, target, ranks, devices, capacity):
    buffer = jnp.zeros((devices, capacity, values.shape[-1]), values.dtype)
    return buffer.at[target, ranks].set(values)


def sparse_shards(h_rows, gates, expert_ids, cotangent, down_weight, swapped):
    devices = lax.axis_size("expert")
    tokens_here, top_count, hidden = h_rows.shape
    width = cotangent.shape[1]
    capacity = min(tokens_here, 3 * tokens_here * top_count // (2 * devices))
    experts = jnp.arange(devices, dtype=jnp.int32)
    weight = down_weight[0]
    flat_ids = slots_of(expert_ids.reshape(-1), swapped, devices)
    onehot = (flat_ids[:, None] == experts[None, :]).astype(jnp.int32)
    ranks = jnp.sum((jnp.cumsum(onehot, axis=0) - onehot) * onehot, axis=1)
    send_h = place_rows(h_rows.reshape(-1, hidden), flat_ids, ranks, devices, capacity)
    received = lax.all_to_all(send_h, "expert", split_axis=0, concat_axis=0, tiled=True)
    result = jnp.einsum("sch,hd->scd", received, weight, preferred_element_type=F32)
    results = result.astype(BF16)
    returned = lax.all_to_all(results, "expert", split_axis=0, concat_axis=0, tiled=True)
    out_rows = returned[flat_ids, ranks].reshape(tokens_here, top_count, width)
    mixed = jnp.einsum("tk,tkd->td", gates, out_rows.astype(F32)).astype(BF16)
    gate_grad = jnp.einsum("td,tkd->tk", cotangent, out_rows, preferred_element_type=F32)
    scaled = (gates[:, :, None] * cotangent[:, None, :].astype(F32)).astype(BF16)
    send_z = place_rows(scaled.reshape(-1, width), flat_ids, ranks, devices, capacity)
    recv_z = lax.all_to_all(send_z, "expert", split_axis=0, concat_axis=0, tiled=True)
    flat_z = recv_z.reshape(-1, width)
    flat_h = received.reshape(-1, hidden)
    grad_sum = lax.dot_general(flat_h, flat_z, (((0,), (0,)), ((), ())), preferred_element_type=F32)
    back = lax.dot_general(flat_z, weight, (((1,), (1,)), ((), ())), preferred_element_type=F32).astype(BF16)
    back_rows = lax.all_to_all(
        back.reshape(devices, capacity, hidden), "expert", split_axis=0, concat_axis=0, tiled=True
    )
    h_grad = back_rows[flat_ids, ranks].reshape(tokens_here, top_count, hidden)
    return (mixed, gate_grad, h_grad, grad_sum.astype(BF16)[None])


def upper(size):
    rows = lax.broadcasted_iota(jnp.int32, (size, size), 0)
    columns = lax.broadcasted_iota(jnp.int32, (size, size), 1)
    return (rows < columns).astype(F32).astype(BF16)


def pack_kernel(devices, capacity, ids_ref, h_ref, place_ref, sent_ref, place_scratch):
    pairs = ids_ref.shape[1]
    rows = sent_ref.shape[0]

    @pl.when(pl.program_id(0) == 0)
    def _():
        before = jnp.zeros((devices, 1), F32)
        for tile in range(pairs // 128):
            ids = ids_ref[:, tile * 128:(tile + 1) * 128]
            named = lax.broadcasted_iota(jnp.int32, (devices, 128), 0) == ids
            ones = jnp.where(named, 1.0, 0.0)
            rank = jnp.dot(ones.astype(BF16), upper(128), preferred_element_type=F32) + before
            before = before + jnp.sum(ones, axis=1, keepdims=True)
            rank = jnp.sum(jnp.where(named, rank, 0.0), axis=0, keepdims=True)
            place_scratch[:, tile * 128:(tile + 1) * 128] = ids * capacity + rank.astype(jnp.int32)
        place_ref[...] = place_scratch[...]

    first = pl.program_id(0) * rows
    wanted = lax.broadcasted_iota(jnp.int32, (rows, pairs), 0) + first
    chosen = jnp.where(wanted == place_scratch[...], 1.0, 0.0).astype(BF16)
    sent_ref[...] = jnp.dot(chosen, h_ref[...], preferred_element_type=F32).astype(BF16)


def pack(ids, h_flat, devices, capacity, steps=4):
    pairs, hidden = h_flat.shape
    rows = devices * capacity // steps
    return pl.pallas_call(
        functools.partial(pack_kernel, devices, capacity),
        grid=(steps,),
        in_specs=[
            pl.BlockSpec((1, pairs), lambda i: (0, 0)),
            pl.BlockSpec((pairs, hidden), lambda i: (0, 0)),
        ],
        out_specs=[
            pl.BlockSpec((1, pairs), lambda i: (0, 0)),
            pl.BlockSpec((rows, hidden), lambda i: (i, 0)),
        ],
        out_shape=[
            jax.ShapeDtypeStruct((1, pairs), jnp.int32),
            jax.ShapeDtypeStruct((devices * capacity, hidden), BF16),
        ],
        scratch_shapes=[pltpu.VMEM((1, pairs), jnp.int32)],
        compiler_params=pltpu.CompilerParams(vmem_limit_bytes=60 * MIB),
        cost_estimate=BRIEF,
        name="pack",
    )(ids, h_flat)


def unpack_kernel(slots, place_ref, gate_ref, h_ref, back_ref, grad_ref, gate_grad_ref):
    rows = place_ref.shape[0]
    chosen = lax.broadcasted_iota(jnp.int32, (rows, slots), 1) == place_ref[...]
    grad = jnp.dot(jnp.where(chosen, 1.0, 0.0).astype(BF16), back_ref[...], preferred_element_type=F32)
    grad_ref[...] = grad.astype(BF16)
    gate_grad_ref[...] = jnp.sum(grad * h_ref[...].astype(F32), axis=1, keepdims=True) / gate_ref[...]


def unpack(place, gates, h_flat, back_rows, steps=4):
    pairs, hidden = h_flat.shape
    slots = back_rows.shape[0]
    rows = pairs // steps
    return pl.pallas_call(
        functools.partial(unpack_kernel, slots),
        grid=(steps,),
        in_specs=[
            pl.BlockSpec((rows, 1), lambda i: (i, 0)),
            pl.BlockSpec((rows, 1), lambda i: (i, 0)),
            pl.BlockSpec((rows, hidden), lambda i: (i, 0)),
            pl.BlockSpec((slots, hidden), lambda i: (0, 0)),
        ],
        out_specs=[
            pl.BlockSpec((rows, hidden), lambda i: (i, 0)),
            pl.BlockSpec((rows, 1), lambda i: (i, 0)),
        ],
        out_shape=[
            jax.ShapeDtypeStruct((pairs, hidden), BF16),
            jax.ShapeDtypeStruct((pairs, 1), F32),
        ],
        compiler_params=pltpu.CompilerParams(vmem_limit_bytes=60 * MIB),
        cost_estimate=BRIEF,
        name="unpack",
    )(place, gates, h_flat, back_rows)


def line_slots(position):
    near = jnp.minimum(position, 3 - position)
    turned = (near, near + 1, near + 2, 3 - 3 * near)
    return [jnp.where(position < 2, slot, 3 - slot) for slot in turned]


def route_kernel(devices, top, here_ref, routing_ref, rank_ref, gate_ref):
    for side in range(2):
        mine = (here_ref[0] ^ side).astype(F32)
        marks, picked = [], []
        for source in range(devices):
            ids = routing_ref[source, :top, :]
            gates = routing_ref[source, top:, :]
            named = ids == mine
            marks.append(jnp.sum(jnp.where(named, 1.0, 0.0), axis=0, keepdims=True))
            picked.append(jnp.sum(jnp.where(named, gates, 0.0), axis=0, keepdims=True))
        mark = jnp.concatenate(marks, axis=0)
        rank = jnp.dot(mark.astype(BF16), upper(mark.shape[1]), preferred_element_type=F32)
        rank_ref[side] = jnp.where(mark > 0, rank, -1.0).astype(jnp.int32)
        gate_ref[side] = jnp.concatenate(picked, axis=0)


def route(here, routing, top):
    devices, _, tokens = routing.shape
    return pl.pallas_call(
        functools.partial(route_kernel, devices, top),
        in_specs=[pl.BlockSpec(memory_space=pltpu.SMEM), pl.BlockSpec(memory_space=pltpu.VMEM)],
        out_specs=[pl.BlockSpec(memory_space=pltpu.VMEM)] * 2,
        out_shape=[
            jax.ShapeDtypeStruct((2, devices, tokens), jnp.int32),
            jax.ShapeDtypeStruct((2, devices, tokens), F32),
        ],
        cost_estimate=BRIEF,
        name="route",
    )(here, routing)


def chosen_rows(rank_ref, side, source, capacity):
    rank = rank_ref[side, pl.ds(source, 1), :]
    return lax.broadcasted_iota(jnp.int32, (capacity, rank.shape[1]), 0) == rank


def gate_column(gate_ref, chosen, side, source):
    return jnp.sum(jnp.where(chosen, gate_ref[side, pl.ds(source, 1), :], 0.0), axis=1, keepdims=True)


def one_hot(chosen):
    return jnp.where(chosen, 1.0, 0.0).astype(BF16)


def lane_sources(here, slots, lane):
    line, across = here // 4, (here // 2) % 2
    places = line_slots(line)
    return [places[slot] * 4 + (across ^ turn) * 2 + lane for slot in slots for turn in range(2)]


def place_out(pieces, sem):
    copies = [pltpu.make_async_copy(source, target, sem.at[i]) for i, (source, target) in enumerate(pieces)]
    for copy in copies:
        copy.start()
    return copies


def scale_kernel(capacity, slots, held, here_ref, rank_ref, gate_ref, weight_ref, *refs):
    count = 2 * len(slots)
    blocks, refs = refs[:count], refs[count + held:]
    z_ref, back_ref, sibling_ref, z_scratch, back_scratch, z_sem, back_sem = refs
    sources = lane_sources(here_ref[0], slots, here_ref[0] % 2)
    for i, source in enumerate(sources):
        chosen = [chosen_rows(rank_ref, side, source, capacity) for side in range(2)]
        gates = [gate_column(gate_ref, chosen[side], side, source) for side in range(2)]
        both = jnp.concatenate([one_hot(chosen[0]), one_hot(chosen[1])], axis=0)
        rows = jnp.dot(both, blocks[i][...], preferred_element_type=F32)
        z_scratch[i] = (rows[:capacity] * gates[0]).astype(BF16)
        sibling_ref[i] = (rows[capacity:] * gates[1]).astype(BF16)
    copies = place_out([(z_scratch.at[i], z_ref.at[source]) for i, source in enumerate(sources)], z_sem)
    flat = z_scratch[...].reshape(count * capacity, z_scratch.shape[2])
    back = lax.dot_general(flat, weight_ref[...], (((1,), (1,)), ((), ())), preferred_element_type=F32)
    back_scratch[...] = back.astype(BF16).reshape(back_scratch.shape)
    copies += place_out([(back_scratch.at[i], back_ref.at[source]) for i, source in enumerate(sources)], back_sem)
    for copy in copies:
        copy.wait()


def scaled_rows(here, rank, gate, weight, blocks, slots, capacity, buffers):
    devices = rank.shape[1]
    hidden, width = weight.shape
    count = len(blocks)
    tokens = blocks[0].shape[0]
    vmem, anywhere = pl.BlockSpec(memory_space=pltpu.VMEM), pl.BlockSpec(memory_space=pltpu.HBM)
    return pl.pallas_call(
        functools.partial(scale_kernel, capacity, slots, len(buffers)),
        in_specs=[pl.BlockSpec(memory_space=pltpu.SMEM)] + [vmem] * (3 + count) + [anywhere] * len(buffers),
        out_specs=[anywhere, anywhere, vmem],
        out_shape=[
            jax.ShapeDtypeStruct((devices, capacity, width), BF16),
            jax.ShapeDtypeStruct((devices, capacity, hidden), BF16),
            jax.ShapeDtypeStruct((count, capacity, width), BF16),
        ],
        scratch_shapes=[
            pltpu.VMEM((count, capacity, width), BF16),
            pltpu.VMEM((count, capacity, hidden), BF16),
            pltpu.SemaphoreType.DMA((count,)),
            pltpu.SemaphoreType.DMA((count,)),
        ],
        input_output_aliases={4 + count + i: i for i in range(len(buffers))},
        compiler_params=pltpu.CompilerParams(vmem_limit_bytes=60 * MIB),
        cost_estimate=BRIEF,
        name="scaled_rows",
    )(here, rank, gate, weight, *blocks, *buffers)


def sibling_kernel(capacity, slots, here_ref, weight_ref, rows_ref, _z, _back, z_ref, back_ref, token_ref, back_scratch, z_sem, back_sem):
    count = 2 * len(slots)
    sources = lane_sources(here_ref[0], slots, 1 - here_ref[0] % 2)
    copies = place_out([(rows_ref.at[i], z_ref.at[source]) for i, source in enumerate(sources)], z_sem)
    flat = rows_ref[...].reshape(count * capacity, rows_ref.shape[2])
    back = lax.dot_general(flat, weight_ref[...], (((1,), (1,)), ((), ())), preferred_element_type=F32)
    back_scratch[...] = back.astype(BF16).reshape(back_scratch.shape)
    copies += place_out([(back_scratch.at[i], back_ref.at[source]) for i, source in enumerate(sources)], back_sem)
    token_ref[...] = jnp.zeros_like(token_ref)
    for copy in copies:
        copy.wait()


def sibling_rows(here, weight, rows, slots, z_rows, back):
    count, capacity, width = rows.shape
    hidden = weight.shape[0]
    vmem, anywhere = pl.BlockSpec(memory_space=pltpu.VMEM), pl.BlockSpec(memory_space=pltpu.HBM)
    return pl.pallas_call(
        functools.partial(sibling_kernel, capacity, slots),
        in_specs=[pl.BlockSpec(memory_space=pltpu.SMEM), vmem, vmem, anywhere, anywhere],
        out_specs=[anywhere, anywhere, vmem],
        out_shape=[
            jax.ShapeDtypeStruct(z_rows.shape, BF16),
            jax.ShapeDtypeStruct(back.shape, BF16),
            jax.ShapeDtypeStruct((8, 128), F32),
        ],
        scratch_shapes=[
            pltpu.VMEM((count, capacity, hidden), BF16),
            pltpu.SemaphoreType.DMA((count,)),
            pltpu.SemaphoreType.DMA((count,)),
        ],
        input_output_aliases={3: 0, 4: 1},
        compiler_params=pltpu.CompilerParams(vmem_limit_bytes=60 * MIB),
        cost_estimate=BRIEF,
        name="sibling_rows",
    )(here, weight, rows, z_rows, back)


def forward_kernel(capacity, slots, turn, here_ref, rank_ref, gate_ref, weight_ref, *refs):
    blocks, out_ref = refs[:2 * len(slots)], refs[-1]
    sources = lane_sources(here_ref[0], slots, (here_ref[0] % 2) ^ turn)
    flat = jnp.concatenate([block[0, 0] for block in blocks], axis=0)
    out = jnp.dot(flat, weight_ref[...], preferred_element_type=F32).astype(BF16).astype(F32)
    for j, source in enumerate(sources):
        gate = gate_column(gate_ref, chosen_rows(rank_ref, 0, source, capacity), 0, source)
        out_ref[j] = (out[j * capacity:(j + 1) * capacity, :] * gate).astype(BF16)


def forward_rows(here, rank, gate, rows_h, weight, slots, turn, waited):
    devices, capacity, hidden = rows_h.shape
    width = weight.shape[1]
    count = 2 * len(slots)

    def block(j):
        return lambda i, here: (lane_sources(here[0], slots, 0)[j] // 2, (here[0] % 2) ^ turn, 0, 0)

    whole = pl.BlockSpec(rank.shape, lambda i, here: (0, 0, 0))
    rows = rows_h.reshape(devices // 2, 2, capacity, hidden)
    return pl.pallas_call(
        functools.partial(forward_kernel, capacity, slots, turn),
        grid_spec=pltpu.PrefetchScalarGridSpec(
            num_scalar_prefetch=1,
            grid=(1,),
            in_specs=[whole, whole, pl.BlockSpec((hidden, width), lambda i, here: (0, 0))]
            + [pl.BlockSpec((1, 1, capacity, hidden), block(j)) for j in range(count)]
            + [pl.BlockSpec(memory_space=pl.ANY)] * len(waited),
            out_specs=pl.BlockSpec((count, capacity, width), lambda i, here: (0, 0, 0)),
        ),
        out_shape=jax.ShapeDtypeStruct((count, capacity, width), BF16),
        compiler_params=pltpu.CompilerParams(vmem_limit_bytes=60 * MIB),
        cost_estimate=BRIEF,
        name="forward_rows",
    )(here, rank, gate, weight, *[rows] * count, *waited)


def sum_kernel(capacity, slots, turn, here_ref, rank_ref, own_ref, other_ref, *part_refs):
    for step, slot in enumerate(slots):

        @pl.when(pl.program_id(0) == step)
        def _():
            source = lane_sources(here_ref[0], (slot,), here_ref[0] % 2)[turn]
            both = [one_hot(chosen_rows(rank_ref, side, source, capacity)) for side in range(2)]
            rows = jnp.concatenate([own_ref[0], other_ref[0]], axis=0)
            part = lax.dot_general(
                jnp.concatenate(both, axis=0), rows, (((0,), (0,)), ((), ())), preferred_element_type=F32
            )
            part_refs[step][...] = part.astype(BF16)


def summed(here, rank, own, other, slots, turn):
    _, capacity, width = own.shape
    tokens = rank.shape[2]
    block = pl.BlockSpec((1, capacity, width), lambda i, here: (2 * i + turn, 0, 0))
    return pl.pallas_call(
        functools.partial(sum_kernel, capacity, slots, turn),
        grid_spec=pltpu.PrefetchScalarGridSpec(
            num_scalar_prefetch=1,
            grid=(len(slots),),
            in_specs=[pl.BlockSpec(rank.shape, lambda i, here: (0, 0, 0)), block, block],
            out_specs=[pl.BlockSpec((tokens, width), lambda i, here: (0, 0))] * len(slots),
        ),
        out_shape=[jax.ShapeDtypeStruct((tokens, width), BF16)] * len(slots),
        compiler_params=pltpu.CompilerParams(vmem_limit_bytes=60 * MIB),
        cost_estimate=BRIEF,
        name="summed",
    )(here, rank, own, other)


def added(*values):
    total = values[0].astype(F32)
    for value in values[1:]:
        total = total + value.astype(F32)
    return total.astype(BF16)


def passed(pairs, value):
    return lax.ppermute(value, "expert", [(a * 4 + lane, b * 4 + lane) for a, b in pairs for lane in range(4)])


def swapped_with(value, bit):
    devices = lax.axis_size("expert")
    return lax.ppermute(value, "expert", [(i, i ^ bit) for i in range(devices)])


OUTER, INNER = ((0, 1), (3, 2)), ((1, 2), (2, 1))
ENDS, ENDS_SWAP = ((1, 0), (2, 3)), ((0, 3), (3, 0))


def gate_kernel(*refs):
    pass


def after(values, *waited):
    count = len(values)
    anywhere = pl.BlockSpec(memory_space=pl.ANY)
    return pl.pallas_call(
        gate_kernel,
        in_specs=[anywhere] * (count + len(waited)),
        out_specs=[anywhere] * count,
        out_shape=[jax.ShapeDtypeStruct(value.shape, value.dtype) for value in values],
        input_output_aliases={i: i for i in range(count)},
        compiler_params=pltpu.CompilerParams(vmem_limit_bytes=60 * MIB),
        cost_estimate=BRIEF,
        name="after",
    )(*values, *waited)


def dense_shards(h_rows, gates, expert_ids, cotangent, down_weight, swapped):
    devices = lax.axis_size("expert")
    here = lax.axis_index("expert").reshape(1)
    tokens, top, hidden = h_rows.shape
    capacity = min(tokens, 3 * tokens * top // (2 * devices))
    weight = down_weight[0]
    slot_ids = slots_of(expert_ids, swapped, devices)
    h_flat = h_rows.reshape(-1, hidden)

    routing = jnp.concatenate([slot_ids.T.astype(F32), gates.T], axis=0)
    routing = jnp.broadcast_to(routing, (devices,) + routing.shape)
    place, send_h = pack(slot_ids.reshape(1, -1), h_flat, devices, capacity)

    own = cotangent
    from_end, from_inner, from_near_end = passed(OUTER, own), passed(INNER, own), passed(ENDS, own)
    own_y = swapped_with(own, 2)
    near = added(from_inner, from_near_end)
    start_end, start_inner, near = after((from_end, from_inner, near), own_y)
    from_far, from_middle = passed(INNER, start_end), passed(ENDS, start_inner)
    near_y = swapped_with(near, 2)
    middle = added(from_far, from_middle)
    start_far, middle, routing = after((from_far, middle, routing), near_y, send_h)
    last = added(from_end, passed(ENDS, start_far))
    middle_y = swapped_with(middle, 2)
    routing = lax.all_to_all(routing, "expert", split_axis=0, concat_axis=0, tiled=True)
    rank, gate = route(here, routing, top)
    send_h, last = after((send_h, last), middle_y, rank)
    rows_h = lax.all_to_all(
        send_h.reshape(devices, capacity, hidden), "expert", split_axis=0, concat_axis=0, tiled=True
    )
    last_y = swapped_with(last, 2)

    z_rows, back, sibling = scaled_rows(here, rank, gate, weight, [own, own_y, near, near_y], (0, 1), capacity, [])
    sibling = swapped_with(sibling, 1)
    z_rows, back, _ = sibling_rows(here, weight, sibling, (0, 1), z_rows, back)
    z_rows, back, sibling_last = scaled_rows(
        here, rank, gate, weight, [middle, middle_y, last, last_y], (2, 3), capacity, [z_rows, back]
    )
    sibling_last = swapped_with(sibling_last, 1)
    z_rows, back, ready = sibling_rows(here, weight, sibling_last, (2, 3), z_rows, back)
    back_rows = lax.all_to_all(back, "expert", split_axis=0, concat_axis=0, tiled=True).reshape(-1, hidden)

    rows_h, = after((rows_h,), ready)
    beside, across, passing = [], [], []
    for slots in ((2, 3), (1, 0)):
        other = swapped_with(forward_rows(here, rank, gate, rows_h, weight, slots, 1, [*passing]), 1)
        mine = forward_rows(here, rank, gate, rows_h, weight, slots, 0, [*passing, *across[:1]])
        passing = summed(here, rank, mine, other, slots, 1)
        beside += summed(here, rank, mine, other, slots, 0)
        across += [swapped_with(part, 2) for part in passing]
    grad_sum = lax.dot_general(
        rows_h.reshape(-1, hidden), z_rows.reshape(devices * capacity, -1), (((0,), (0,)), ((), ())),
        preferred_element_type=F32,
    )
    weight_grad = grad_sum.astype(BF16)[None]
    mid, far, close, kept = zip(beside, across)
    mid, far, close = added(*mid), added(*far), added(*close)
    mid_outer, mid_inner = passed(OUTER, mid), passed(INNER, mid)
    far_far = passed(ENDS_SWAP, far)
    close_outer = passed(OUTER, close)
    mid_outer, = after((mid_outer,), weight_grad)
    close_inner = passed(INNER, added(close, mid_outer))
    mid_inner, = after((mid_inner,), back_rows)
    far_ends = passed(ENDS, added(far, mid_inner))
    mixed = added(*kept, far_far, close_outer, close_inner, far_ends)
    h_grad, gate_grad = unpack(place.reshape(-1, 1), gates.reshape(-1, 1), h_flat, back_rows)
    return (
        mixed,
        gate_grad.reshape(tokens, top),
        h_grad.reshape(tokens, top, hidden),
        weight_grad,
    )


def shards(h_rows, *rest):
    devices = lax.axis_size("expert")
    dense = devices == 16 and devices <= 2 * h_rows.shape[1]
    return (dense_shards if dense else sparse_shards)(h_rows, *rest)


def solution(mesh):
    in_specs = (
        P(("groups", "expert"), None, None),
        P(("groups", "expert"), None),
        P(("groups", "expert"), None),
        P(("groups", "expert"), None),
        P("expert", None, None),
        P(),
    )
    out_specs = (
        P(("groups", "expert"), None),
        P(("groups", "expert"), None),
        P(("groups", "expert"), None, None),
        P(("groups", "expert"), None, None),
    )
    return jax.shard_map(shards, mesh=mesh, in_specs=in_specs, out_specs=out_specs, check_vma=False)
```

```python
import functools

import jax
import jax.numpy as jnp
from jax import lax
from jax.experimental import pallas as pl
from jax.experimental.pallas import tpu as pltpu
from jax.sharding import PartitionSpec as P

F32 = jnp.float32
BF16 = jnp.bfloat16
MIB = 1 << 20
BRIEF = pl.CostEstimate(flops=0, transcendentals=0, bytes_accessed=0)


def slots_of(ids, swapped, devices):
    half_way = devices // 2
    table = jnp.arange(devices, dtype=jnp.int32)
    table = (table + half_way * swapped[table % half_way]) % devices
    return jnp.sum(jnp.where(ids[..., None] == jnp.arange(devices, dtype=jnp.int32), table, 0), axis=-1)


def place_rows(values, target, ranks, devices, capacity):
    buffer = jnp.zeros((devices, capacity, values.shape[-1]), values.dtype)
    return buffer.at[target, ranks].set(values)


def sparse_shards(h_rows, gates, expert_ids, cotangent, down_weight, swapped):
    devices = lax.axis_size("expert")
    tokens_here, top_count, hidden = h_rows.shape
    width = cotangent.shape[1]
    capacity = min(tokens_here, 3 * tokens_here * top_count // (2 * devices))
    experts = jnp.arange(devices, dtype=jnp.int32)
    weight = down_weight[0]
    flat_ids = slots_of(expert_ids.reshape(-1), swapped, devices)
    onehot = (flat_ids[:, None] == experts[None, :]).astype(jnp.int32)
    ranks = jnp.sum((jnp.cumsum(onehot, axis=0) - onehot) * onehot, axis=1)
    send_h = place_rows(h_rows.reshape(-1, hidden), flat_ids, ranks, devices, capacity)
    received = lax.all_to_all(send_h, "expert", split_axis=0, concat_axis=0, tiled=True)
    result = jnp.einsum("sch,hd->scd", received, weight, preferred_element_type=F32)
    results = result.astype(BF16)
    returned = lax.all_to_all(results, "expert", split_axis=0, concat_axis=0, tiled=True)
    out_rows = returned[flat_ids, ranks].reshape(tokens_here, top_count, width)
    mixed = jnp.einsum("tk,tkd->td", gates, out_rows.astype(F32)).astype(BF16)
    gate_grad = jnp.einsum("td,tkd->tk", cotangent, out_rows, preferred_element_type=F32)
    scaled = (gates[:, :, None] * cotangent[:, None, :].astype(F32)).astype(BF16)
    send_z = place_rows(scaled.reshape(-1, width), flat_ids, ranks, devices, capacity)
    recv_z = lax.all_to_all(send_z, "expert", split_axis=0, concat_axis=0, tiled=True)
    flat_z = recv_z.reshape(-1, width)
    flat_h = received.reshape(-1, hidden)
    grad_sum = lax.dot_general(flat_h, flat_z, (((0,), (0,)), ((), ())), preferred_element_type=F32)
    back = lax.dot_general(flat_z, weight, (((1,), (1,)), ((), ())), preferred_element_type=F32).astype(BF16)
    back_rows = lax.all_to_all(
        back.reshape(devices, capacity, hidden), "expert", split_axis=0, concat_axis=0, tiled=True
    )
    h_grad = back_rows[flat_ids, ranks].reshape(tokens_here, top_count, hidden)
    return (mixed, gate_grad, h_grad, grad_sum.astype(BF16)[None])


def upper(size):
    rows = lax.broadcasted_iota(jnp.int32, (size, size), 0)
    columns = lax.broadcasted_iota(jnp.int32, (size, size), 1)
    return (rows < columns).astype(F32).astype(BF16)


def pack_kernel(devices, capacity, ids_ref, h_ref, place_ref, sent_ref, place_scratch):
    pairs = ids_ref.shape[1]
    rows = sent_ref.shape[0]

    @pl.when(pl.program_id(0) == 0)
    def _():
        before = jnp.zeros((devices, 1), F32)
        for tile in range(pairs // 128):
            ids = ids_ref[:, tile * 128:(tile + 1) * 128]
            named = lax.broadcasted_iota(jnp.int32, (devices, 128), 0) == ids
            ones = jnp.where(named, 1.0, 0.0)
            rank = jnp.dot(ones.astype(BF16), upper(128), preferred_element_type=F32) + before
            before = before + jnp.sum(ones, axis=1, keepdims=True)
            rank = jnp.sum(jnp.where(named, rank, 0.0), axis=0, keepdims=True)
            place_scratch[:, tile * 128:(tile + 1) * 128] = ids * capacity + rank.astype(jnp.int32)
        place_ref[...] = place_scratch[...]

    first = pl.program_id(0) * rows
    wanted = lax.broadcasted_iota(jnp.int32, (rows, pairs), 0) + first
    chosen = jnp.where(wanted == place_scratch[...], 1.0, 0.0).astype(BF16)
    sent_ref[...] = jnp.dot(chosen, h_ref[...], preferred_element_type=F32).astype(BF16)


def pack(ids, h_flat, devices, capacity, steps=4):
    pairs, hidden = h_flat.shape
    rows = devices * capacity // steps
    return pl.pallas_call(
        functools.partial(pack_kernel, devices, capacity),
        grid=(steps,),
        in_specs=[
            pl.BlockSpec((1, pairs), lambda i: (0, 0)),
            pl.BlockSpec((pairs, hidden), lambda i: (0, 0)),
        ],
        out_specs=[
            pl.BlockSpec((1, pairs), lambda i: (0, 0)),
            pl.BlockSpec((rows, hidden), lambda i: (i, 0)),
        ],
        out_shape=[
            jax.ShapeDtypeStruct((1, pairs), jnp.int32),
            jax.ShapeDtypeStruct((devices * capacity, hidden), BF16),
        ],
        scratch_shapes=[pltpu.VMEM((1, pairs), jnp.int32)],
        compiler_params=pltpu.CompilerParams(vmem_limit_bytes=60 * MIB),
        cost_estimate=BRIEF,
        name="pack",
    )(ids, h_flat)


def unpack_kernel(slots, place_ref, gate_ref, h_ref, back_ref, grad_ref, gate_grad_ref):
    rows = place_ref.shape[0]
    chosen = lax.broadcasted_iota(jnp.int32, (rows, slots), 1) == place_ref[...]
    grad = jnp.dot(jnp.where(chosen, 1.0, 0.0).astype(BF16), back_ref[...], preferred_element_type=F32)
    grad_ref[...] = grad.astype(BF16)
    gate_grad_ref[...] = jnp.sum(grad * h_ref[...].astype(F32), axis=1, keepdims=True) / gate_ref[...]


def unpack(place, gates, h_flat, back_rows, steps=4):
    pairs, hidden = h_flat.shape
    slots = back_rows.shape[0]
    rows = pairs // steps
    return pl.pallas_call(
        functools.partial(unpack_kernel, slots),
        grid=(steps,),
        in_specs=[
            pl.BlockSpec((rows, 1), lambda i: (i, 0)),
            pl.BlockSpec((rows, 1), lambda i: (i, 0)),
            pl.BlockSpec((rows, hidden), lambda i: (i, 0)),
            pl.BlockSpec((slots, hidden), lambda i: (0, 0)),
        ],
        out_specs=[
            pl.BlockSpec((rows, hidden), lambda i: (i, 0)),
            pl.BlockSpec((rows, 1), lambda i: (i, 0)),
        ],
        out_shape=[
            jax.ShapeDtypeStruct((pairs, hidden), BF16),
            jax.ShapeDtypeStruct((pairs, 1), F32),
        ],
        compiler_params=pltpu.CompilerParams(vmem_limit_bytes=60 * MIB),
        cost_estimate=BRIEF,
        name="unpack",
    )(place, gates, h_flat, back_rows)


def line_slots(position):
    near = jnp.minimum(position, 3 - position)
    turned = (near, near + 1, near + 2, 3 - 3 * near)
    return [jnp.where(position < 2, slot, 3 - slot) for slot in turned]


def route_kernel(devices, top, here_ref, routing_ref, rank_ref, gate_ref):
    for side in range(2):
        mine = (here_ref[0] ^ side).astype(F32)
        marks, picked = [], []
        for source in range(devices):
            ids = routing_ref[source, :top, :]
            gates = routing_ref[source, top:, :]
            named = ids == mine
            marks.append(jnp.sum(jnp.where(named, 1.0, 0.0), axis=0, keepdims=True))
            picked.append(jnp.sum(jnp.where(named, gates, 0.0), axis=0, keepdims=True))
        mark = jnp.concatenate(marks, axis=0)
        rank = jnp.dot(mark.astype(BF16), upper(mark.shape[1]), preferred_element_type=F32)
        rank_ref[side] = jnp.where(mark > 0, rank, -1.0).astype(jnp.int32)
        gate_ref[side] = jnp.concatenate(picked, axis=0)


def route(here, routing, top):
    devices, _, tokens = routing.shape
    return pl.pallas_call(
        functools.partial(route_kernel, devices, top),
        in_specs=[pl.BlockSpec(memory_space=pltpu.SMEM), pl.BlockSpec(memory_space=pltpu.VMEM)],
        out_specs=[pl.BlockSpec(memory_space=pltpu.VMEM)] * 2,
        out_shape=[
            jax.ShapeDtypeStruct((2, devices, tokens), jnp.int32),
            jax.ShapeDtypeStruct((2, devices, tokens), F32),
        ],
        cost_estimate=BRIEF,
        name="route",
    )(here, routing)


def chosen_rows(rank_ref, side, source, capacity):
    rank = rank_ref[side, pl.ds(source, 1), :]
    return lax.broadcasted_iota(jnp.int32, (capacity, rank.shape[1]), 0) == rank


def gate_column(gate_ref, chosen, side, source):
    return jnp.sum(jnp.where(chosen, gate_ref[side, pl.ds(source, 1), :], 0.0), axis=1, keepdims=True)


def one_hot(chosen):
    return jnp.where(chosen, 1.0, 0.0).astype(BF16)


def lane_sources(here, slots, lane):
    line, across = here // 4, (here // 2) % 2
    places = line_slots(line)
    return [places[slot] * 4 + (across ^ turn) * 2 + lane for slot in slots for turn in range(2)]


def place_out(pieces, sem):
    copies = [pltpu.make_async_copy(source, target, sem.at[i]) for i, (source, target) in enumerate(pieces)]
    for copy in copies:
        copy.start()
    return copies


def scale_kernel(capacity, slots, held, here_ref, rank_ref, gate_ref, weight_ref, *refs):
    count = 2 * len(slots)
    blocks, refs = refs[:count], refs[count + held:]
    z_ref, back_ref, sibling_ref, z_scratch, back_scratch, z_sem, back_sem = refs
    sources = lane_sources(here_ref[0], slots, here_ref[0] % 2)
    for i, source in enumerate(sources):
        chosen = [chosen_rows(rank_ref, side, source, capacity) for side in range(2)]
        gates = [gate_column(gate_ref, chosen[side], side, source) for side in range(2)]
        both = jnp.concatenate([one_hot(chosen[0]), one_hot(chosen[1])], axis=0)
        rows = jnp.dot(both, blocks[i][...], preferred_element_type=F32)
        z_scratch[i] = (rows[:capacity] * gates[0]).astype(BF16)
        sibling_ref[i] = (rows[capacity:] * gates[1]).astype(BF16)
    copies = place_out([(z_scratch.at[i], z_ref.at[source]) for i, source in enumerate(sources)], z_sem)
    flat = z_scratch[...].reshape(count * capacity, z_scratch.shape[2])
    back = lax.dot_general(flat, weight_ref[...], (((1,), (1,)), ((), ())), preferred_element_type=F32)
    back_scratch[...] = back.astype(BF16).reshape(back_scratch.shape)
    copies += place_out([(back_scratch.at[i], back_ref.at[source]) for i, source in enumerate(sources)], back_sem)
    for copy in copies:
        copy.wait()


def scaled_rows(here, rank, gate, weight, blocks, slots, capacity, buffers):
    devices = rank.shape[1]
    hidden, width = weight.shape
    count = len(blocks)
    tokens = blocks[0].shape[0]
    vmem, anywhere = pl.BlockSpec(memory_space=pltpu.VMEM), pl.BlockSpec(memory_space=pltpu.HBM)
    return pl.pallas_call(
        functools.partial(scale_kernel, capacity, slots, len(buffers)),
        in_specs=[pl.BlockSpec(memory_space=pltpu.SMEM)] + [vmem] * (3 + count) + [anywhere] * len(buffers),
        out_specs=[anywhere, anywhere, vmem],
        out_shape=[
            jax.ShapeDtypeStruct((devices, capacity, width), BF16),
            jax.ShapeDtypeStruct((devices, capacity, hidden), BF16),
            jax.ShapeDtypeStruct((count, capacity, width), BF16),
        ],
        scratch_shapes=[
            pltpu.VMEM((count, capacity, width), BF16),
            pltpu.VMEM((count, capacity, hidden), BF16),
            pltpu.SemaphoreType.DMA((count,)),
            pltpu.SemaphoreType.DMA((count,)),
        ],
        input_output_aliases={4 + count + i: i for i in range(len(buffers))},
        compiler_params=pltpu.CompilerParams(vmem_limit_bytes=60 * MIB),
        cost_estimate=BRIEF,
        name="scaled_rows",
    )(here, rank, gate, weight, *blocks, *buffers)


def sibling_kernel(capacity, slots, here_ref, weight_ref, rows_ref, _z, _back, z_ref, back_ref, token_ref, back_scratch, z_sem, back_sem):
    count = 2 * len(slots)
    sources = lane_sources(here_ref[0], slots, 1 - here_ref[0] % 2)
    copies = place_out([(rows_ref.at[i], z_ref.at[source]) for i, source in enumerate(sources)], z_sem)
    flat = rows_ref[...].reshape(count * capacity, rows_ref.shape[2])
    back = lax.dot_general(flat, weight_ref[...], (((1,), (1,)), ((), ())), preferred_element_type=F32)
    back_scratch[...] = back.astype(BF16).reshape(back_scratch.shape)
    copies += place_out([(back_scratch.at[i], back_ref.at[source]) for i, source in enumerate(sources)], back_sem)
    token_ref[...] = jnp.zeros_like(token_ref)
    for copy in copies:
        copy.wait()


def sibling_rows(here, weight, rows, slots, z_rows, back):
    count, capacity, width = rows.shape
    hidden = weight.shape[0]
    vmem, anywhere = pl.BlockSpec(memory_space=pltpu.VMEM), pl.BlockSpec(memory_space=pltpu.HBM)
    return pl.pallas_call(
        functools.partial(sibling_kernel, capacity, slots),
        in_specs=[pl.BlockSpec(memory_space=pltpu.SMEM), vmem, vmem, anywhere, anywhere],
        out_specs=[anywhere, anywhere, vmem],
        out_shape=[
            jax.ShapeDtypeStruct(z_rows.shape, BF16),
            jax.ShapeDtypeStruct(back.shape, BF16),
            jax.ShapeDtypeStruct((8, 128), F32),
        ],
        scratch_shapes=[
            pltpu.VMEM((count, capacity, hidden), BF16),
            pltpu.SemaphoreType.DMA((count,)),
            pltpu.SemaphoreType.DMA((count,)),
        ],
        input_output_aliases={3: 0, 4: 1},
        compiler_params=pltpu.CompilerParams(vmem_limit_bytes=60 * MIB),
        cost_estimate=BRIEF,
        name="sibling_rows",
    )(here, weight, rows, z_rows, back)


def forward_kernel(capacity, slots, turn, here_ref, rank_ref, gate_ref, weight_ref, *refs):
    blocks, out_ref = refs[:2 * len(slots)], refs[-1]
    sources = lane_sources(here_ref[0], slots, (here_ref[0] % 2) ^ turn)
    flat = jnp.concatenate([block[0, 0] for block in blocks], axis=0)
    out = jnp.dot(flat, weight_ref[...], preferred_element_type=F32).astype(BF16).astype(F32)
    for j, source in enumerate(sources):
        gate = gate_column(gate_ref, chosen_rows(rank_ref, 0, source, capacity), 0, source)
        out_ref[j] = (out[j * capacity:(j + 1) * capacity, :] * gate).astype(BF16)


def forward_rows(here, rank, gate, rows_h, weight, slots, turn, waited):
    devices, capacity, hidden = rows_h.shape
    width = weight.shape[1]
    count = 2 * len(slots)

    def block(j):
        return lambda i, here: (lane_sources(here[0], slots, 0)[j] // 2, (here[0] % 2) ^ turn, 0, 0)

    whole = pl.BlockSpec(rank.shape, lambda i, here: (0, 0, 0))
    rows = rows_h.reshape(devices // 2, 2, capacity, hidden)
    return pl.pallas_call(
        functools.partial(forward_kernel, capacity, slots, turn),
        grid_spec=pltpu.PrefetchScalarGridSpec(
            num_scalar_prefetch=1,
            grid=(1,),
            in_specs=[whole, whole, pl.BlockSpec((hidden, width), lambda i, here: (0, 0))]
            + [pl.BlockSpec((1, 1, capacity, hidden), block(j)) for j in range(count)]
            + [pl.BlockSpec(memory_space=pl.ANY)] * len(waited),
            out_specs=pl.BlockSpec((count, capacity, width), lambda i, here: (0, 0, 0)),
        ),
        out_shape=jax.ShapeDtypeStruct((count, capacity, width), BF16),
        compiler_params=pltpu.CompilerParams(vmem_limit_bytes=60 * MIB),
        cost_estimate=BRIEF,
        name="forward_rows",
    )(here, rank, gate, weight, *[rows] * count, *waited)


def sum_kernel(capacity, slots, turn, here_ref, rank_ref, own_ref, other_ref, *part_refs):
    for step, slot in enumerate(slots):

        @pl.when(pl.program_id(0) == step)
        def _():
            source = lane_sources(here_ref[0], (slot,), here_ref[0] % 2)[turn]
            both = [one_hot(chosen_rows(rank_ref, side, source, capacity)) for side in range(2)]
            rows = jnp.concatenate([own_ref[0], other_ref[0]], axis=0)
            part = lax.dot_general(
                jnp.concatenate(both, axis=0), rows, (((0,), (0,)), ((), ())), preferred_element_type=F32
            )
            part_refs[step][...] = part.astype(BF16)


def summed(here, rank, own, other, slots, turn):
    _, capacity, width = own.shape
    tokens = rank.shape[2]
    block = pl.BlockSpec((1, capacity, width), lambda i, here: (2 * i + turn, 0, 0))
    return pl.pallas_call(
        functools.partial(sum_kernel, capacity, slots, turn),
        grid_spec=pltpu.PrefetchScalarGridSpec(
            num_scalar_prefetch=1,
            grid=(len(slots),),
            in_specs=[pl.BlockSpec(rank.shape, lambda i, here: (0, 0, 0)), block, block],
            out_specs=[pl.BlockSpec((tokens, width), lambda i, here: (0, 0))] * len(slots),
        ),
        out_shape=[jax.ShapeDtypeStruct((tokens, width), BF16)] * len(slots),
        compiler_params=pltpu.CompilerParams(vmem_limit_bytes=60 * MIB),
        cost_estimate=BRIEF,
        name="summed",
    )(here, rank, own, other)


def added(*values):
    total = values[0].astype(F32)
    for value in values[1:]:
        total = total + value.astype(F32)
    return total.astype(BF16)


def passed(pairs, value):
    return lax.ppermute(value, "expert", [(a * 4 + lane, b * 4 + lane) for a, b in pairs for lane in range(4)])


def swapped_with(value, bit):
    devices = lax.axis_size("expert")
    return lax.ppermute(value, "expert", [(i, i ^ bit) for i in range(devices)])


OUTER, INNER = ((0, 1), (3, 2)), ((1, 2), (2, 1))
ENDS, ENDS_SWAP = ((1, 0), (2, 3)), ((0, 3), (3, 0))


def gate_kernel(*refs):
    pass


def after(values, *waited):
    count = len(values)
    anywhere = pl.BlockSpec(memory_space=pl.ANY)
    return pl.pallas_call(
        gate_kernel,
        in_specs=[anywhere] * (count + len(waited)),
        out_specs=[anywhere] * count,
        out_shape=[jax.ShapeDtypeStruct(value.shape, value.dtype) for value in values],
        input_output_aliases={i: i for i in range(count)},
        compiler_params=pltpu.CompilerParams(vmem_limit_bytes=60 * MIB),
        cost_estimate=BRIEF,
        name="after",
    )(*values, *waited)


def dense_shards(h_rows, gates, expert_ids, cotangent, down_weight, swapped):
    devices = lax.axis_size("expert")
    here = lax.axis_index("expert").reshape(1)
    tokens, top, hidden = h_rows.shape
    capacity = min(tokens, 3 * tokens * top // (2 * devices))
    weight = down_weight[0]
    slot_ids = slots_of(expert_ids, swapped, devices)
    h_flat = h_rows.reshape(-1, hidden)

    routing = jnp.concatenate([slot_ids.T.astype(F32), gates.T], axis=0)
    routing = jnp.broadcast_to(routing, (devices,) + routing.shape)
    place, send_h = pack(slot_ids.reshape(1, -1), h_flat, devices, capacity)

    own = cotangent
    from_end, from_inner, from_near_end = passed(OUTER, own), passed(INNER, own), passed(ENDS, own)
    own_y = swapped_with(own, 2)
    near = added(from_inner, from_near_end)
    start_end, start_inner, near = after((from_end, from_inner, near), own_y)
    from_far, from_middle = passed(INNER, start_end), passed(ENDS, start_inner)
    near_y = swapped_with(near, 2)
    middle = added(from_far, from_middle)
    start_far, middle, routing = after((from_far, middle, routing), near_y, send_h)
    last = added(from_end, passed(ENDS, start_far))
    middle_y = swapped_with(middle, 2)
    routing = lax.all_to_all(routing, "expert", split_axis=0, concat_axis=0, tiled=True)
    rank, gate = route(here, routing, top)
    send_h, last = after((send_h, last), middle_y, rank)
    rows_h = lax.all_to_all(
        send_h.reshape(devices, capacity, hidden), "expert", split_axis=0, concat_axis=0, tiled=True
    )
    last_y = swapped_with(last, 2)

    z_rows, back, sibling = scaled_rows(here, rank, gate, weight, [own, own_y, near, near_y], (0, 1), capacity, [])
    sibling = swapped_with(sibling, 1)
    z_rows, back, _ = sibling_rows(here, weight, sibling, (0, 1), z_rows, back)
    z_rows, back, sibling_last = scaled_rows(
        here, rank, gate, weight, [middle, middle_y, last, last_y], (2, 3), capacity, [z_rows, back]
    )
    sibling_last = swapped_with(sibling_last, 1)
    z_rows, back, ready = sibling_rows(here, weight, sibling_last, (2, 3), z_rows, back)
    back_rows = lax.all_to_all(back, "expert", split_axis=0, concat_axis=0, tiled=True).reshape(-1, hidden)

    rows_h, = after((rows_h,), ready)
    beside, across, passing = [], [], []
    for slots in ((2, 3), (1, 0)):
        other = swapped_with(forward_rows(here, rank, gate, rows_h, weight, slots, 1, [*passing]), 1)
        mine = forward_rows(here, rank, gate, rows_h, weight, slots, 0, [*passing])
        passing = summed(here, rank, mine, other, slots, 1)
        beside += summed(here, rank, mine, other, slots, 0)
        across += [swapped_with(part, 2) for part in passing]
    grad_sum = lax.dot_general(
        rows_h.reshape(-1, hidden), z_rows.reshape(devices * capacity, -1), (((0,), (0,)), ((), ())),
        preferred_element_type=F32,
    )
    weight_grad = grad_sum.astype(BF16)[None]
    beside[0], = after((beside[0],), across[1], weight_grad, *passing)
    mid, far, close, kept = zip(beside, across)
    mid, far = after((added(*mid), added(*far)))
    mid_outer, mid_inner = passed(OUTER, mid), passed(INNER, mid)
    far_far = passed(ENDS_SWAP, far)
    close, = after((added(*close),), far_far, back_rows)
    close_outer = passed(OUTER, close)
    close_inner = passed(INNER, added(close, mid_outer))
    far_ends = passed(ENDS, added(far, mid_inner))
    mixed = added(*kept, far_far, close_outer, close_inner, far_ends)
    h_grad, gate_grad = unpack(place.reshape(-1, 1), gates.reshape(-1, 1), h_flat, back_rows)
    return (
        mixed,
        gate_grad.reshape(tokens, top),
        h_grad.reshape(tokens, top, hidden),
        weight_grad,
    )


def shards(h_rows, *rest):
    devices = lax.axis_size("expert")
    dense = devices == 16 and devices <= 2 * h_rows.shape[1]
    return (dense_shards if dense else sparse_shards)(h_rows, *rest)


def solution(mesh):
    in_specs = (
        P(("groups", "expert"), None, None),
        P(("groups", "expert"), None),
        P(("groups", "expert"), None),
        P(("groups", "expert"), None),
        P("expert", None, None),
        P(),
    )
    out_specs = (
        P(("groups", "expert"), None),
        P(("groups", "expert"), None),
        P(("groups", "expert"), None, None),
        P(("groups", "expert"), None, None),
    )
    return jax.shard_map(shards, mesh=mesh, in_specs=in_specs, out_specs=out_specs, check_vma=False)
```

```python
import functools

import jax
import jax.numpy as jnp
from jax import lax
from jax.experimental import pallas as pl
from jax.experimental.pallas import tpu as pltpu
from jax.sharding import PartitionSpec as P

F32 = jnp.float32
BF16 = jnp.bfloat16
MIB = 1 << 20
BRIEF = pl.CostEstimate(flops=0, transcendentals=0, bytes_accessed=0)


def slots_of(ids, swapped, devices):
    half_way = devices // 2
    table = jnp.arange(devices, dtype=jnp.int32)
    table = (table + half_way * swapped[table % half_way]) % devices
    return jnp.sum(jnp.where(ids[..., None] == jnp.arange(devices, dtype=jnp.int32), table, 0), axis=-1)


def place_rows(values, target, ranks, devices, capacity):
    buffer = jnp.zeros((devices, capacity, values.shape[-1]), values.dtype)
    return buffer.at[target, ranks].set(values)


def sparse_shards(h_rows, gates, expert_ids, cotangent, down_weight, swapped):
    devices = lax.axis_size("expert")
    tokens_here, top_count, hidden = h_rows.shape
    width = cotangent.shape[1]
    capacity = min(tokens_here, 3 * tokens_here * top_count // (2 * devices))
    experts = jnp.arange(devices, dtype=jnp.int32)
    weight = down_weight[0]
    flat_ids = slots_of(expert_ids.reshape(-1), swapped, devices)
    onehot = (flat_ids[:, None] == experts[None, :]).astype(jnp.int32)
    ranks = jnp.sum((jnp.cumsum(onehot, axis=0) - onehot) * onehot, axis=1)
    send_h = place_rows(h_rows.reshape(-1, hidden), flat_ids, ranks, devices, capacity)
    received = lax.all_to_all(send_h, "expert", split_axis=0, concat_axis=0, tiled=True)
    result = jnp.einsum("sch,hd->scd", received, weight, preferred_element_type=F32)
    results = result.astype(BF16)
    returned = lax.all_to_all(results, "expert", split_axis=0, concat_axis=0, tiled=True)
    out_rows = returned[flat_ids, ranks].reshape(tokens_here, top_count, width)
    mixed = jnp.einsum("tk,tkd->td", gates, out_rows.astype(F32)).astype(BF16)
    gate_grad = jnp.einsum("td,tkd->tk", cotangent, out_rows, preferred_element_type=F32)
    scaled = (gates[:, :, None] * cotangent[:, None, :].astype(F32)).astype(BF16)
    send_z = place_rows(scaled.reshape(-1, width), flat_ids, ranks, devices, capacity)
    recv_z = lax.all_to_all(send_z, "expert", split_axis=0, concat_axis=0, tiled=True)
    flat_z = recv_z.reshape(-1, width)
    flat_h = received.reshape(-1, hidden)
    grad_sum = lax.dot_general(flat_h, flat_z, (((0,), (0,)), ((), ())), preferred_element_type=F32)
    back = lax.dot_general(flat_z, weight, (((1,), (1,)), ((), ())), preferred_element_type=F32).astype(BF16)
    back_rows = lax.all_to_all(
        back.reshape(devices, capacity, hidden), "expert", split_axis=0, concat_axis=0, tiled=True
    )
    h_grad = back_rows[flat_ids, ranks].reshape(tokens_here, top_count, hidden)
    return (mixed, gate_grad, h_grad, grad_sum.astype(BF16)[None])


def upper(size):
    rows = lax.broadcasted_iota(jnp.int32, (size, size), 0)
    columns = lax.broadcasted_iota(jnp.int32, (size, size), 1)
    return (rows < columns).astype(F32).astype(BF16)


def pack_kernel(devices, capacity, ids_ref, h_ref, place_ref, sent_ref, place_scratch):
    pairs = ids_ref.shape[1]
    rows = sent_ref.shape[0]

    @pl.when(pl.program_id(0) == 0)
    def _():
        before = jnp.zeros((devices, 1), F32)
        for tile in range(pairs // 128):
            ids = ids_ref[:, tile * 128:(tile + 1) * 128]
            named = lax.broadcasted_iota(jnp.int32, (devices, 128), 0) == ids
            ones = jnp.where(named, 1.0, 0.0)
            rank = jnp.dot(ones.astype(BF16), upper(128), preferred_element_type=F32) + before
            before = before + jnp.sum(ones, axis=1, keepdims=True)
            rank = jnp.sum(jnp.where(named, rank, 0.0), axis=0, keepdims=True)
            place_scratch[:, tile * 128:(tile + 1) * 128] = ids * capacity + rank.astype(jnp.int32)
        place_ref[...] = place_scratch[...]

    first = pl.program_id(0) * rows
    wanted = lax.broadcasted_iota(jnp.int32, (rows, pairs), 0) + first
    chosen = jnp.where(wanted == place_scratch[...], 1.0, 0.0).astype(BF16)
    sent_ref[...] = jnp.dot(chosen, h_ref[...], preferred_element_type=F32).astype(BF16)


def pack(ids, h_flat, devices, capacity, steps=4):
    pairs, hidden = h_flat.shape
    rows = devices * capacity // steps
    return pl.pallas_call(
        functools.partial(pack_kernel, devices, capacity),
        grid=(steps,),
        in_specs=[
            pl.BlockSpec((1, pairs), lambda i: (0, 0)),
            pl.BlockSpec((pairs, hidden), lambda i: (0, 0)),
        ],
        out_specs=[
            pl.BlockSpec((1, pairs), lambda i: (0, 0)),
            pl.BlockSpec((rows, hidden), lambda i: (i, 0)),
        ],
        out_shape=[
            jax.ShapeDtypeStruct((1, pairs), jnp.int32),
            jax.ShapeDtypeStruct((devices * capacity, hidden), BF16),
        ],
        scratch_shapes=[pltpu.VMEM((1, pairs), jnp.int32)],
        compiler_params=pltpu.CompilerParams(vmem_limit_bytes=60 * MIB),
        cost_estimate=BRIEF,
        name="pack",
    )(ids, h_flat)


def unpack_kernel(slots, place_ref, gate_ref, h_ref, back_ref, grad_ref, gate_grad_ref):
    rows = place_ref.shape[0]
    chosen = lax.broadcasted_iota(jnp.int32, (rows, slots), 1) == place_ref[...]
    grad = jnp.dot(jnp.where(chosen, 1.0, 0.0).astype(BF16), back_ref[...], preferred_element_type=F32)
    grad_ref[...] = grad.astype(BF16)
    gate_grad_ref[...] = jnp.sum(grad * h_ref[...].astype(F32), axis=1, keepdims=True) / gate_ref[...]


def unpack(place, gates, h_flat, back_rows, steps=4):
    pairs, hidden = h_flat.shape
    slots = back_rows.shape[0]
    rows = pairs // steps
    return pl.pallas_call(
        functools.partial(unpack_kernel, slots),
        grid=(steps,),
        in_specs=[
            pl.BlockSpec((rows, 1), lambda i: (i, 0)),
            pl.BlockSpec((rows, 1), lambda i: (i, 0)),
            pl.BlockSpec((rows, hidden), lambda i: (i, 0)),
            pl.BlockSpec((slots, hidden), lambda i: (0, 0)),
        ],
        out_specs=[
            pl.BlockSpec((rows, hidden), lambda i: (i, 0)),
            pl.BlockSpec((rows, 1), lambda i: (i, 0)),
        ],
        out_shape=[
            jax.ShapeDtypeStruct((pairs, hidden), BF16),
            jax.ShapeDtypeStruct((pairs, 1), F32),
        ],
        compiler_params=pltpu.CompilerParams(vmem_limit_bytes=60 * MIB),
        cost_estimate=BRIEF,
        name="unpack",
    )(place, gates, h_flat, back_rows)


def line_slots(position):
    near = jnp.minimum(position, 3 - position)
    turned = (near, near + 1, near + 2, 3 - 3 * near)
    return [jnp.where(position < 2, slot, 3 - slot) for slot in turned]


def route_kernel(devices, top, here_ref, routing_ref, rank_ref, gate_ref):
    for side in range(2):
        mine = (here_ref[0] ^ side).astype(F32)
        marks, picked = [], []
        for source in range(devices):
            ids = routing_ref[source, :top, :]
            gates = routing_ref[source, top:, :]
            named = ids == mine
            marks.append(jnp.sum(jnp.where(named, 1.0, 0.0), axis=0, keepdims=True))
            picked.append(jnp.sum(jnp.where(named, gates, 0.0), axis=0, keepdims=True))
        mark = jnp.concatenate(marks, axis=0)
        rank = jnp.dot(mark.astype(BF16), upper(mark.shape[1]), preferred_element_type=F32)
        rank_ref[side] = jnp.where(mark > 0, rank, -1.0).astype(jnp.int32)
        gate_ref[side] = jnp.concatenate(picked, axis=0)


def route(here, routing, top):
    devices, _, tokens = routing.shape
    return pl.pallas_call(
        functools.partial(route_kernel, devices, top),
        in_specs=[pl.BlockSpec(memory_space=pltpu.SMEM), pl.BlockSpec(memory_space=pltpu.VMEM)],
        out_specs=[pl.BlockSpec(memory_space=pltpu.VMEM)] * 2,
        out_shape=[
            jax.ShapeDtypeStruct((2, devices, tokens), jnp.int32),
            jax.ShapeDtypeStruct((2, devices, tokens), F32),
        ],
        cost_estimate=BRIEF,
        name="route",
    )(here, routing)


def chosen_rows(rank_ref, side, source, capacity):
    rank = rank_ref[side, pl.ds(source, 1), :]
    return lax.broadcasted_iota(jnp.int32, (capacity, rank.shape[1]), 0) == rank


def gate_column(gate_ref, chosen, side, source):
    return jnp.sum(jnp.where(chosen, gate_ref[side, pl.ds(source, 1), :], 0.0), axis=1, keepdims=True)


def one_hot(chosen):
    return jnp.where(chosen, 1.0, 0.0).astype(BF16)


def lane_sources(here, slots, lane):
    line, across = here // 4, (here // 2) % 2
    places = line_slots(line)
    return [places[slot] * 4 + (across ^ turn) * 2 + lane for slot in slots for turn in range(2)]


def place_out(pieces, sem):
    copies = [pltpu.make_async_copy(source, target, sem.at[i]) for i, (source, target) in enumerate(pieces)]
    for copy in copies:
        copy.start()
    return copies


def scale_kernel(capacity, slots, held, here_ref, rank_ref, gate_ref, weight_ref, *refs):
    count = 2 * len(slots)
    blocks, refs = refs[:count], refs[count + held:]
    z_ref, back_ref, sibling_ref, z_scratch, back_scratch, z_sem, back_sem = refs
    sources = lane_sources(here_ref[0], slots, here_ref[0] % 2)
    for i, source in enumerate(sources):
        chosen = [chosen_rows(rank_ref, side, source, capacity) for side in range(2)]
        gates = [gate_column(gate_ref, chosen[side], side, source) for side in range(2)]
        both = jnp.concatenate([one_hot(chosen[0]), one_hot(chosen[1])], axis=0)
        rows = jnp.dot(both, blocks[i][...], preferred_element_type=F32)
        z_scratch[i] = (rows[:capacity] * gates[0]).astype(BF16)
        sibling_ref[i] = (rows[capacity:] * gates[1]).astype(BF16)
    copies = place_out([(z_scratch.at[i], z_ref.at[source]) for i, source in enumerate(sources)], z_sem)
    flat = z_scratch[...].reshape(count * capacity, z_scratch.shape[2])
    back = lax.dot_general(flat, weight_ref[...], (((1,), (1,)), ((), ())), preferred_element_type=F32)
    back_scratch[...] = back.astype(BF16).reshape(back_scratch.shape)
    copies += place_out([(back_scratch.at[i], back_ref.at[source]) for i, source in enumerate(sources)], back_sem)
    for copy in copies:
        copy.wait()


def scaled_rows(here, rank, gate, weight, blocks, slots, capacity, buffers):
    devices = rank.shape[1]
    hidden, width = weight.shape
    count = len(blocks)
    tokens = blocks[0].shape[0]
    vmem, anywhere = pl.BlockSpec(memory_space=pltpu.VMEM), pl.BlockSpec(memory_space=pltpu.HBM)
    return pl.pallas_call(
        functools.partial(scale_kernel, capacity, slots, len(buffers)),
        in_specs=[pl.BlockSpec(memory_space=pltpu.SMEM)] + [vmem] * (3 + count) + [anywhere] * len(buffers),
        out_specs=[anywhere, anywhere, vmem],
        out_shape=[
            jax.ShapeDtypeStruct((devices, capacity, width), BF16),
            jax.ShapeDtypeStruct((devices, capacity, hidden), BF16),
            jax.ShapeDtypeStruct((count, capacity, width), BF16),
        ],
        scratch_shapes=[
            pltpu.VMEM((count, capacity, width), BF16),
            pltpu.VMEM((count, capacity, hidden), BF16),
            pltpu.SemaphoreType.DMA((count,)),
            pltpu.SemaphoreType.DMA((count,)),
        ],
        input_output_aliases={4 + count + i: i for i in range(len(buffers))},
        compiler_params=pltpu.CompilerParams(vmem_limit_bytes=60 * MIB),
        cost_estimate=BRIEF,
        name="scaled_rows",
    )(here, rank, gate, weight, *blocks, *buffers)


def sibling_kernel(capacity, slots, here_ref, weight_ref, rows_ref, _z, _back, z_ref, back_ref, token_ref, back_scratch, z_sem, back_sem):
    count = 2 * len(slots)
    sources = lane_sources(here_ref[0], slots, 1 - here_ref[0] % 2)
    copies = place_out([(rows_ref.at[i], z_ref.at[source]) for i, source in enumerate(sources)], z_sem)
    flat = rows_ref[...].reshape(count * capacity, rows_ref.shape[2])
    back = lax.dot_general(flat, weight_ref[...], (((1,), (1,)), ((), ())), preferred_element_type=F32)
    back_scratch[...] = back.astype(BF16).reshape(back_scratch.shape)
    copies += place_out([(back_scratch.at[i], back_ref.at[source]) for i, source in enumerate(sources)], back_sem)
    token_ref[...] = jnp.zeros_like(token_ref)
    for copy in copies:
        copy.wait()


def sibling_rows(here, weight, rows, slots, z_rows, back):
    count, capacity, width = rows.shape
    hidden = weight.shape[0]
    vmem, anywhere = pl.BlockSpec(memory_space=pltpu.VMEM), pl.BlockSpec(memory_space=pltpu.HBM)
    return pl.pallas_call(
        functools.partial(sibling_kernel, capacity, slots),
        in_specs=[pl.BlockSpec(memory_space=pltpu.SMEM), vmem, vmem, anywhere, anywhere],
        out_specs=[anywhere, anywhere, vmem],
        out_shape=[
            jax.ShapeDtypeStruct(z_rows.shape, BF16),
            jax.ShapeDtypeStruct(back.shape, BF16),
            jax.ShapeDtypeStruct((8, 128), F32),
        ],
        scratch_shapes=[
            pltpu.VMEM((count, capacity, hidden), BF16),
            pltpu.SemaphoreType.DMA((count,)),
            pltpu.SemaphoreType.DMA((count,)),
        ],
        input_output_aliases={3: 0, 4: 1},
        compiler_params=pltpu.CompilerParams(vmem_limit_bytes=60 * MIB),
        cost_estimate=BRIEF,
        name="sibling_rows",
    )(here, weight, rows, z_rows, back)


def forward_kernel(capacity, slots, turn, here_ref, rank_ref, gate_ref, weight_ref, *refs):
    blocks, out_ref = refs[:2 * len(slots)], refs[-1]
    sources = lane_sources(here_ref[0], slots, (here_ref[0] % 2) ^ turn)
    flat = jnp.concatenate([block[0, 0] for block in blocks], axis=0)
    out = jnp.dot(flat, weight_ref[...], preferred_element_type=F32).astype(BF16).astype(F32)
    for j, source in enumerate(sources):
        gate = gate_column(gate_ref, chosen_rows(rank_ref, 0, source, capacity), 0, source)
        out_ref[j] = (out[j * capacity:(j + 1) * capacity, :] * gate).astype(BF16)


def forward_rows(here, rank, gate, rows_h, weight, slots, turn, waited):
    devices, capacity, hidden = rows_h.shape
    width = weight.shape[1]
    count = 2 * len(slots)

    def block(j):
        return lambda i, here: (lane_sources(here[0], slots, 0)[j] // 2, (here[0] % 2) ^ turn, 0, 0)

    whole = pl.BlockSpec(rank.shape, lambda i, here: (0, 0, 0))
    rows = rows_h.reshape(devices // 2, 2, capacity, hidden)
    return pl.pallas_call(
        functools.partial(forward_kernel, capacity, slots, turn),
        grid_spec=pltpu.PrefetchScalarGridSpec(
            num_scalar_prefetch=1,
            grid=(1,),
            in_specs=[whole, whole, pl.BlockSpec((hidden, width), lambda i, here: (0, 0))]
            + [pl.BlockSpec((1, 1, capacity, hidden), block(j)) for j in range(count)]
            + [pl.BlockSpec(memory_space=pl.ANY)] * len(waited),
            out_specs=pl.BlockSpec((count, capacity, width), lambda i, here: (0, 0, 0)),
        ),
        out_shape=jax.ShapeDtypeStruct((count, capacity, width), BF16),
        compiler_params=pltpu.CompilerParams(vmem_limit_bytes=60 * MIB),
        cost_estimate=BRIEF,
        name="forward_rows",
    )(here, rank, gate, weight, *[rows] * count, *waited)


def sum_kernel(capacity, slots, turn, here_ref, rank_ref, own_ref, other_ref, *part_refs):
    for step, slot in enumerate(slots):

        @pl.when(pl.program_id(0) == step)
        def _():
            source = lane_sources(here_ref[0], (slot,), here_ref[0] % 2)[turn]
            both = [one_hot(chosen_rows(rank_ref, side, source, capacity)) for side in range(2)]
            rows = jnp.concatenate([own_ref[0], other_ref[0]], axis=0)
            part = lax.dot_general(
                jnp.concatenate(both, axis=0), rows, (((0,), (0,)), ((), ())), preferred_element_type=F32
            )
            part_refs[step][...] = part.astype(BF16)


def summed(here, rank, own, other, slots, turn):
    _, capacity, width = own.shape
    tokens = rank.shape[2]
    block = pl.BlockSpec((1, capacity, width), lambda i, here: (2 * i + turn, 0, 0))
    return pl.pallas_call(
        functools.partial(sum_kernel, capacity, slots, turn),
        grid_spec=pltpu.PrefetchScalarGridSpec(
            num_scalar_prefetch=1,
            grid=(len(slots),),
            in_specs=[pl.BlockSpec(rank.shape, lambda i, here: (0, 0, 0)), block, block],
            out_specs=[pl.BlockSpec((tokens, width), lambda i, here: (0, 0))] * len(slots),
        ),
        out_shape=[jax.ShapeDtypeStruct((tokens, width), BF16)] * len(slots),
        compiler_params=pltpu.CompilerParams(vmem_limit_bytes=60 * MIB),
        cost_estimate=BRIEF,
        name="summed",
    )(here, rank, own, other)


def added(*values):
    total = values[0].astype(F32)
    for value in values[1:]:
        total = total + value.astype(F32)
    return total.astype(BF16)


def passed(pairs, value):
    return lax.ppermute(value, "expert", [(a * 4 + lane, b * 4 + lane) for a, b in pairs for lane in range(4)])


def swapped_with(value, bit):
    devices = lax.axis_size("expert")
    return lax.ppermute(value, "expert", [(i, i ^ bit) for i in range(devices)])


OUTER, INNER = ((0, 1), (3, 2)), ((1, 2), (2, 1))
ENDS, ENDS_SWAP = ((1, 0), (2, 3)), ((0, 3), (3, 0))


def gate_kernel(*refs):
    pass


def after(values, *waited):
    count = len(values)
    anywhere = pl.BlockSpec(memory_space=pl.ANY)
    return pl.pallas_call(
        gate_kernel,
        in_specs=[anywhere] * (count + len(waited)),
        out_specs=[anywhere] * count,
        out_shape=[jax.ShapeDtypeStruct(value.shape, value.dtype) for value in values],
        input_output_aliases={i: i for i in range(count)},
        compiler_params=pltpu.CompilerParams(vmem_limit_bytes=60 * MIB),
        cost_estimate=BRIEF,
        name="after",
    )(*values, *waited)


def dense_shards(h_rows, gates, expert_ids, cotangent, down_weight, swapped):
    devices = lax.axis_size("expert")
    here = lax.axis_index("expert").reshape(1)
    tokens, top, hidden = h_rows.shape
    capacity = min(tokens, 3 * tokens * top // (2 * devices))
    weight = down_weight[0]
    slot_ids = slots_of(expert_ids, swapped, devices)
    h_flat = h_rows.reshape(-1, hidden)

    routing = jnp.concatenate([slot_ids.T.astype(F32), gates.T], axis=0)
    routing = jnp.broadcast_to(routing, (devices,) + routing.shape)
    place, send_h = pack(slot_ids.reshape(1, -1), h_flat, devices, capacity)

    own = cotangent
    from_end, from_inner, from_near_end = passed(OUTER, own), passed(INNER, own), passed(ENDS, own)
    own_y = swapped_with(own, 2)
    near = added(from_inner, from_near_end)
    start_end, start_inner, near = after((from_end, from_inner, near), own_y)
    from_far, from_middle = passed(INNER, start_end), passed(ENDS, start_inner)
    near_y = swapped_with(near, 2)
    middle = added(from_far, from_middle)
    start_far, middle, routing = after((from_far, middle, routing), near_y, send_h)
    last = added(from_end, passed(ENDS, start_far))
    middle_y = swapped_with(middle, 2)
    routing = lax.all_to_all(routing, "expert", split_axis=0, concat_axis=0, tiled=True)
    rank, gate = route(here, routing, top)
    send_h, last = after((send_h, last), middle_y, rank)
    rows_h = lax.all_to_all(
        send_h.reshape(devices, capacity, hidden), "expert", split_axis=0, concat_axis=0, tiled=True
    )
    last_y = swapped_with(last, 2)

    z_rows, back, sibling = scaled_rows(here, rank, gate, weight, [own, own_y, near, near_y], (0, 1), capacity, [])
    sibling = swapped_with(sibling, 1)
    z_rows, back, _ = sibling_rows(here, weight, sibling, (0, 1), z_rows, back)
    z_rows, back, sibling_last = scaled_rows(
        here, rank, gate, weight, [middle, middle_y, last, last_y], (2, 3), capacity, [z_rows, back]
    )
    sibling_last = swapped_with(sibling_last, 1)
    z_rows, back, ready = sibling_rows(here, weight, sibling_last, (2, 3), z_rows, back)
    back_rows = lax.all_to_all(back, "expert", split_axis=0, concat_axis=0, tiled=True).reshape(-1, hidden)

    rows_h, = after((rows_h,), ready)
    beside, leaving, waited = [], [], []
    for slots in ((2, 3), (1, 0)):
        other = swapped_with(forward_rows(here, rank, gate, rows_h, weight, slots, 1, waited), 1)
        mine = forward_rows(here, rank, gate, rows_h, weight, slots, 0, waited)
        leaving += summed(here, rank, mine, other, slots, 1)
        beside += summed(here, rank, mine, other, slots, 0)
        waited = leaving[:1]
    across = [swapped_with(leaving[0], 2)]
    mid, = after((added(beside[0], across[0]),))
    leaving[1], = after((leaving[1],), mid)
    across += [swapped_with(part, 2) for part in leaving[1:]]
    z_rows, = after((z_rows,), across[0])
    grad_sum = lax.dot_general(
        rows_h.reshape(-1, hidden), z_rows.reshape(devices * capacity, -1), (((0,), (0,)), ((), ())),
        preferred_element_type=F32,
    )
    weight_grad = grad_sum.astype(BF16)[None]
    _, far, close, kept = zip(beside, across)
    mid_outer, mid_inner = passed(OUTER, mid), passed(INNER, mid)
    far, = after((added(*far),))
    far_far = passed(ENDS_SWAP, far)
    close, = after((added(*close),), back_rows, weight_grad)
    close_outer = passed(OUTER, close)
    close_inner = passed(INNER, added(close, mid_outer))
    far_ends = passed(ENDS, added(far, mid_inner))
    mixed = added(*kept, far_far, close_outer, close_inner, far_ends)
    h_grad, gate_grad = unpack(place.reshape(-1, 1), gates.reshape(-1, 1), h_flat, back_rows)
    return (
        mixed,
        gate_grad.reshape(tokens, top),
        h_grad.reshape(tokens, top, hidden),
        weight_grad,
    )


def shards(h_rows, *rest):
    devices = lax.axis_size("expert")
    dense = devices == 16 and devices <= 2 * h_rows.shape[1]
    return (dense_shards if dense else sparse_shards)(h_rows, *rest)


def solution(mesh):
    in_specs = (
        P(("groups", "expert"), None, None),
        P(("groups", "expert"), None),
        P(("groups", "expert"), None),
        P(("groups", "expert"), None),
        P("expert", None, None),
        P(),
    )
    out_specs = (
        P(("groups", "expert"), None),
        P(("groups", "expert"), None),
        P(("groups", "expert"), None, None),
        P(("groups", "expert"), None, None),
    )
    return jax.shard_map(shards, mesh=mesh, in_specs=in_specs, out_specs=out_specs, check_vma=False)
```

```python
import functools

import jax
import jax.numpy as jnp
from jax import lax
from jax.experimental import pallas as pl
from jax.experimental.pallas import tpu as pltpu
from jax.sharding import PartitionSpec as P

F32 = jnp.float32
BF16 = jnp.bfloat16
MIB = 1 << 20
BRIEF = pl.CostEstimate(flops=0, transcendentals=0, bytes_accessed=0)


def slots_of(ids, swapped, devices):
    half_way = devices // 2
    table = jnp.arange(devices, dtype=jnp.int32)
    table = (table + half_way * swapped[table % half_way]) % devices
    return jnp.sum(jnp.where(ids[..., None] == jnp.arange(devices, dtype=jnp.int32), table, 0), axis=-1)


def place_rows(values, target, ranks, devices, capacity):
    buffer = jnp.zeros((devices, capacity, values.shape[-1]), values.dtype)
    return buffer.at[target, ranks].set(values)


def sparse_shards(h_rows, gates, expert_ids, cotangent, down_weight, swapped):
    devices = lax.axis_size("expert")
    tokens_here, top_count, hidden = h_rows.shape
    width = cotangent.shape[1]
    capacity = min(tokens_here, 3 * tokens_here * top_count // (2 * devices))
    experts = jnp.arange(devices, dtype=jnp.int32)
    weight = down_weight[0]
    flat_ids = slots_of(expert_ids.reshape(-1), swapped, devices)
    onehot = (flat_ids[:, None] == experts[None, :]).astype(jnp.int32)
    ranks = jnp.sum((jnp.cumsum(onehot, axis=0) - onehot) * onehot, axis=1)
    send_h = place_rows(h_rows.reshape(-1, hidden), flat_ids, ranks, devices, capacity)
    received = lax.all_to_all(send_h, "expert", split_axis=0, concat_axis=0, tiled=True)
    result = jnp.einsum("sch,hd->scd", received, weight, preferred_element_type=F32)
    results = result.astype(BF16)
    returned = lax.all_to_all(results, "expert", split_axis=0, concat_axis=0, tiled=True)
    out_rows = returned[flat_ids, ranks].reshape(tokens_here, top_count, width)
    mixed = jnp.einsum("tk,tkd->td", gates, out_rows.astype(F32)).astype(BF16)
    gate_grad = jnp.einsum("td,tkd->tk", cotangent, out_rows, preferred_element_type=F32)
    scaled = (gates[:, :, None] * cotangent[:, None, :].astype(F32)).astype(BF16)
    send_z = place_rows(scaled.reshape(-1, width), flat_ids, ranks, devices, capacity)
    recv_z = lax.all_to_all(send_z, "expert", split_axis=0, concat_axis=0, tiled=True)
    flat_z = recv_z.reshape(-1, width)
    flat_h = received.reshape(-1, hidden)
    grad_sum = lax.dot_general(flat_h, flat_z, (((0,), (0,)), ((), ())), preferred_element_type=F32)
    back = lax.dot_general(flat_z, weight, (((1,), (1,)), ((), ())), preferred_element_type=F32).astype(BF16)
    back_rows = lax.all_to_all(
        back.reshape(devices, capacity, hidden), "expert", split_axis=0, concat_axis=0, tiled=True
    )
    h_grad = back_rows[flat_ids, ranks].reshape(tokens_here, top_count, hidden)
    return (mixed, gate_grad, h_grad, grad_sum.astype(BF16)[None])


def upper(size):
    rows = lax.broadcasted_iota(jnp.int32, (size, size), 0)
    columns = lax.broadcasted_iota(jnp.int32, (size, size), 1)
    return (rows < columns).astype(F32).astype(BF16)


def pack_kernel(devices, capacity, ids_ref, h_ref, place_ref, sent_ref, place_scratch):
    pairs = ids_ref.shape[1]
    rows = sent_ref.shape[0]

    @pl.when(pl.program_id(0) == 0)
    def _():
        before = jnp.zeros((devices, 1), F32)
        for tile in range(pairs // 128):
            ids = ids_ref[:, tile * 128:(tile + 1) * 128]
            named = lax.broadcasted_iota(jnp.int32, (devices, 128), 0) == ids
            ones = jnp.where(named, 1.0, 0.0)
            rank = jnp.dot(ones.astype(BF16), upper(128), preferred_element_type=F32) + before
            before = before + jnp.sum(ones, axis=1, keepdims=True)
            rank = jnp.sum(jnp.where(named, rank, 0.0), axis=0, keepdims=True)
            place_scratch[:, tile * 128:(tile + 1) * 128] = ids * capacity + rank.astype(jnp.int32)
        place_ref[...] = place_scratch[...]

    first = pl.program_id(0) * rows
    wanted = lax.broadcasted_iota(jnp.int32, (rows, pairs), 0) + first
    chosen = jnp.where(wanted == place_scratch[...], 1.0, 0.0).astype(BF16)
    sent_ref[...] = jnp.dot(chosen, h_ref[...], preferred_element_type=F32).astype(BF16)


def pack(ids, h_flat, devices, capacity, steps=4):
    pairs, hidden = h_flat.shape
    rows = devices * capacity // steps
    return pl.pallas_call(
        functools.partial(pack_kernel, devices, capacity),
        grid=(steps,),
        in_specs=[
            pl.BlockSpec((1, pairs), lambda i: (0, 0)),
            pl.BlockSpec((pairs, hidden), lambda i: (0, 0)),
        ],
        out_specs=[
            pl.BlockSpec((1, pairs), lambda i: (0, 0)),
            pl.BlockSpec((rows, hidden), lambda i: (i, 0)),
        ],
        out_shape=[
            jax.ShapeDtypeStruct((1, pairs), jnp.int32),
            jax.ShapeDtypeStruct((devices * capacity, hidden), BF16),
        ],
        scratch_shapes=[pltpu.VMEM((1, pairs), jnp.int32)],
        compiler_params=pltpu.CompilerParams(vmem_limit_bytes=60 * MIB),
        cost_estimate=BRIEF,
        name="pack",
    )(ids, h_flat)


def unpack_kernel(slots, place_ref, gate_ref, h_ref, back_ref, grad_ref, gate_grad_ref):
    rows = place_ref.shape[0]
    chosen = lax.broadcasted_iota(jnp.int32, (rows, slots), 1) == place_ref[...]
    grad = jnp.dot(jnp.where(chosen, 1.0, 0.0).astype(BF16), back_ref[...], preferred_element_type=F32)
    grad_ref[...] = grad.astype(BF16)
    gate_grad_ref[...] = jnp.sum(grad * h_ref[...].astype(F32), axis=1, keepdims=True) / gate_ref[...]


def unpack(place, gates, h_flat, back_rows, steps=4):
    pairs, hidden = h_flat.shape
    slots = back_rows.shape[0]
    rows = pairs // steps
    return pl.pallas_call(
        functools.partial(unpack_kernel, slots),
        grid=(steps,),
        in_specs=[
            pl.BlockSpec((rows, 1), lambda i: (i, 0)),
            pl.BlockSpec((rows, 1), lambda i: (i, 0)),
            pl.BlockSpec((rows, hidden), lambda i: (i, 0)),
            pl.BlockSpec((slots, hidden), lambda i: (0, 0)),
        ],
        out_specs=[
            pl.BlockSpec((rows, hidden), lambda i: (i, 0)),
            pl.BlockSpec((rows, 1), lambda i: (i, 0)),
        ],
        out_shape=[
            jax.ShapeDtypeStruct((pairs, hidden), BF16),
            jax.ShapeDtypeStruct((pairs, 1), F32),
        ],
        compiler_params=pltpu.CompilerParams(vmem_limit_bytes=60 * MIB),
        cost_estimate=BRIEF,
        name="unpack",
    )(place, gates, h_flat, back_rows)


def line_slots(position):
    near = jnp.minimum(position, 3 - position)
    turned = (near, near + 1, near + 2, 3 - 3 * near)
    return [jnp.where(position < 2, slot, 3 - slot) for slot in turned]


def route_kernel(devices, top, here_ref, routing_ref, rank_ref, gate_ref):
    for side in range(2):
        mine = (here_ref[0] ^ side).astype(F32)
        marks, picked = [], []
        for source in range(devices):
            ids = routing_ref[source, :top, :]
            gates = routing_ref[source, top:, :]
            named = ids == mine
            marks.append(jnp.sum(jnp.where(named, 1.0, 0.0), axis=0, keepdims=True))
            picked.append(jnp.sum(jnp.where(named, gates, 0.0), axis=0, keepdims=True))
        mark = jnp.concatenate(marks, axis=0)
        rank = jnp.dot(mark.astype(BF16), upper(mark.shape[1]), preferred_element_type=F32)
        rank_ref[side] = jnp.where(mark > 0, rank, -1.0).astype(jnp.int32)
        gate_ref[side] = jnp.concatenate(picked, axis=0)


def route(here, routing, top):
    devices, _, tokens = routing.shape
    return pl.pallas_call(
        functools.partial(route_kernel, devices, top),
        in_specs=[pl.BlockSpec(memory_space=pltpu.SMEM), pl.BlockSpec(memory_space=pltpu.VMEM)],
        out_specs=[pl.BlockSpec(memory_space=pltpu.VMEM)] * 2,
        out_shape=[
            jax.ShapeDtypeStruct((2, devices, tokens), jnp.int32),
            jax.ShapeDtypeStruct((2, devices, tokens), F32),
        ],
        cost_estimate=BRIEF,
        name="route",
    )(here, routing)


def chosen_rows(rank_ref, side, source, capacity):
    rank = rank_ref[side, pl.ds(source, 1), :]
    return lax.broadcasted_iota(jnp.int32, (capacity, rank.shape[1]), 0) == rank


def gate_column(gate_ref, chosen, side, source):
    return jnp.sum(jnp.where(chosen, gate_ref[side, pl.ds(source, 1), :], 0.0), axis=1, keepdims=True)


def one_hot(chosen):
    return jnp.where(chosen, 1.0, 0.0).astype(BF16)


def lane_sources(here, slots, lane):
    line, across = here // 4, (here // 2) % 2
    places = line_slots(line)
    return [places[slot] * 4 + (across ^ turn) * 2 + lane for slot in slots for turn in range(2)]


def place_out(pieces, sem):
    copies = [pltpu.make_async_copy(source, target, sem.at[i]) for i, (source, target) in enumerate(pieces)]
    for copy in copies:
        copy.start()
    return copies


def scale_kernel(capacity, slots, held, here_ref, rank_ref, gate_ref, weight_ref, *refs):
    count = 2 * len(slots)
    blocks, refs = refs[:count], refs[count + held:]
    z_ref, back_ref, sibling_ref, z_scratch, back_scratch, z_sem, back_sem = refs
    sources = lane_sources(here_ref[0], slots, here_ref[0] % 2)
    for i, source in enumerate(sources):
        chosen = [chosen_rows(rank_ref, side, source, capacity) for side in range(2)]
        gates = [gate_column(gate_ref, chosen[side], side, source) for side in range(2)]
        both = jnp.concatenate([one_hot(chosen[0]), one_hot(chosen[1])], axis=0)
        rows = jnp.dot(both, blocks[i][...], preferred_element_type=F32)
        z_scratch[i] = (rows[:capacity] * gates[0]).astype(BF16)
        sibling_ref[i] = (rows[capacity:] * gates[1]).astype(BF16)
    copies = place_out([(z_scratch.at[i], z_ref.at[source]) for i, source in enumerate(sources)], z_sem)
    flat = z_scratch[...].reshape(count * capacity, z_scratch.shape[2])
    back = lax.dot_general(flat, weight_ref[...], (((1,), (1,)), ((), ())), preferred_element_type=F32)
    back_scratch[...] = back.astype(BF16).reshape(back_scratch.shape)
    copies += place_out([(back_scratch.at[i], back_ref.at[source]) for i, source in enumerate(sources)], back_sem)
    for copy in copies:
        copy.wait()


def scaled_rows(here, rank, gate, weight, blocks, slots, capacity, buffers):
    devices = rank.shape[1]
    hidden, width = weight.shape
    count = len(blocks)
    tokens = blocks[0].shape[0]
    vmem, anywhere = pl.BlockSpec(memory_space=pltpu.VMEM), pl.BlockSpec(memory_space=pltpu.HBM)
    return pl.pallas_call(
        functools.partial(scale_kernel, capacity, slots, len(buffers)),
        in_specs=[pl.BlockSpec(memory_space=pltpu.SMEM)] + [vmem] * (3 + count) + [anywhere] * len(buffers),
        out_specs=[anywhere, anywhere, vmem],
        out_shape=[
            jax.ShapeDtypeStruct((devices, capacity, width), BF16),
            jax.ShapeDtypeStruct((devices, capacity, hidden), BF16),
            jax.ShapeDtypeStruct((count, capacity, width), BF16),
        ],
        scratch_shapes=[
            pltpu.VMEM((count, capacity, width), BF16),
            pltpu.VMEM((count, capacity, hidden), BF16),
            pltpu.SemaphoreType.DMA((count,)),
            pltpu.SemaphoreType.DMA((count,)),
        ],
        input_output_aliases={4 + count + i: i for i in range(len(buffers))},
        compiler_params=pltpu.CompilerParams(vmem_limit_bytes=60 * MIB),
        cost_estimate=BRIEF,
        name="scaled_rows",
    )(here, rank, gate, weight, *blocks, *buffers)


def sibling_kernel(capacity, slots, here_ref, weight_ref, rows_ref, _z, _back, z_ref, back_ref, token_ref, back_scratch, z_sem, back_sem):
    count = 2 * len(slots)
    sources = lane_sources(here_ref[0], slots, 1 - here_ref[0] % 2)
    copies = place_out([(rows_ref.at[i], z_ref.at[source]) for i, source in enumerate(sources)], z_sem)
    flat = rows_ref[...].reshape(count * capacity, rows_ref.shape[2])
    back = lax.dot_general(flat, weight_ref[...], (((1,), (1,)), ((), ())), preferred_element_type=F32)
    back_scratch[...] = back.astype(BF16).reshape(back_scratch.shape)
    copies += place_out([(back_scratch.at[i], back_ref.at[source]) for i, source in enumerate(sources)], back_sem)
    token_ref[...] = jnp.zeros_like(token_ref)
    for copy in copies:
        copy.wait()


def sibling_rows(here, weight, rows, slots, z_rows, back):
    count, capacity, width = rows.shape
    hidden = weight.shape[0]
    vmem, anywhere = pl.BlockSpec(memory_space=pltpu.VMEM), pl.BlockSpec(memory_space=pltpu.HBM)
    return pl.pallas_call(
        functools.partial(sibling_kernel, capacity, slots),
        in_specs=[pl.BlockSpec(memory_space=pltpu.SMEM), vmem, vmem, anywhere, anywhere],
        out_specs=[anywhere, anywhere, vmem],
        out_shape=[
            jax.ShapeDtypeStruct(z_rows.shape, BF16),
            jax.ShapeDtypeStruct(back.shape, BF16),
            jax.ShapeDtypeStruct((8, 128), F32),
        ],
        scratch_shapes=[
            pltpu.VMEM((count, capacity, hidden), BF16),
            pltpu.SemaphoreType.DMA((count,)),
            pltpu.SemaphoreType.DMA((count,)),
        ],
        input_output_aliases={3: 0, 4: 1},
        compiler_params=pltpu.CompilerParams(vmem_limit_bytes=60 * MIB),
        cost_estimate=BRIEF,
        name="sibling_rows",
    )(here, weight, rows, z_rows, back)


def forward_kernel(capacity, slots, turn, here_ref, rank_ref, gate_ref, weight_ref, *refs):
    blocks, out_ref = refs[:-1], refs[-1]
    sources = lane_sources(here_ref[0], slots, (here_ref[0] % 2) ^ turn)
    flat = jnp.concatenate([block[0, 0] for block in blocks], axis=0)
    out = jnp.dot(flat, weight_ref[...], preferred_element_type=F32).astype(BF16).astype(F32)
    for j, source in enumerate(sources):
        gate = gate_column(gate_ref, chosen_rows(rank_ref, 0, source, capacity), 0, source)
        out_ref[j] = (out[j * capacity:(j + 1) * capacity, :] * gate).astype(BF16)


def forward_rows(here, rank, gate, rows_h, weight, slots, turn):
    devices, capacity, hidden = rows_h.shape
    width = weight.shape[1]
    count = 2 * len(slots)

    def block(j):
        return lambda i, here: (lane_sources(here[0], slots, 0)[j] // 2, (here[0] % 2) ^ turn, 0, 0)

    whole = pl.BlockSpec(rank.shape, lambda i, here: (0, 0, 0))
    rows = rows_h.reshape(devices // 2, 2, capacity, hidden)
    return pl.pallas_call(
        functools.partial(forward_kernel, capacity, slots, turn),
        grid_spec=pltpu.PrefetchScalarGridSpec(
            num_scalar_prefetch=1,
            grid=(1,),
            in_specs=[whole, whole, pl.BlockSpec((hidden, width), lambda i, here: (0, 0))]
            + [pl.BlockSpec((1, 1, capacity, hidden), block(j)) for j in range(count)],
            out_specs=pl.BlockSpec((count, capacity, width), lambda i, here: (0, 0, 0)),
        ),
        out_shape=jax.ShapeDtypeStruct((count, capacity, width), BF16),
        compiler_params=pltpu.CompilerParams(vmem_limit_bytes=24 * MIB),
        cost_estimate=BRIEF,
        name="forward_rows",
    )(here, rank, gate, weight, *[rows] * count)


def sum_kernel(capacity, slots, turn, here_ref, rank_ref, own_ref, other_ref, *part_refs):
    for step, slot in enumerate(slots):

        @pl.when(pl.program_id(0) == step)
        def _():
            source = lane_sources(here_ref[0], (slot,), here_ref[0] % 2)[turn]
            both = [one_hot(chosen_rows(rank_ref, side, source, capacity)) for side in range(2)]
            rows = jnp.concatenate([own_ref[0], other_ref[0]], axis=0)
            part = lax.dot_general(
                jnp.concatenate(both, axis=0), rows, (((0,), (0,)), ((), ())), preferred_element_type=F32
            )
            part_refs[step][...] = part.astype(BF16)


def summed(here, rank, own, other, slots, turn):
    _, capacity, width = own.shape
    tokens = rank.shape[2]
    block = pl.BlockSpec((1, capacity, width), lambda i, here: (2 * i + turn, 0, 0))
    return pl.pallas_call(
        functools.partial(sum_kernel, capacity, slots, turn),
        grid_spec=pltpu.PrefetchScalarGridSpec(
            num_scalar_prefetch=1,
            grid=(len(slots),),
            in_specs=[pl.BlockSpec(rank.shape, lambda i, here: (0, 0, 0)), block, block],
            out_specs=[pl.BlockSpec((tokens, width), lambda i, here: (0, 0))] * len(slots),
        ),
        out_shape=[jax.ShapeDtypeStruct((tokens, width), BF16)] * len(slots),
        compiler_params=pltpu.CompilerParams(vmem_limit_bytes=60 * MIB),
        cost_estimate=BRIEF,
        name="summed",
    )(here, rank, own, other)


def added(*values):
    total = values[0].astype(F32)
    for value in values[1:]:
        total = total + value.astype(F32)
    return total.astype(BF16)


def passed(pairs, value):
    return lax.ppermute(value, "expert", [(a * 4 + lane, b * 4 + lane) for a, b in pairs for lane in range(4)])


def swapped_with(value, bit):
    devices = lax.axis_size("expert")
    return lax.ppermute(value, "expert", [(i, i ^ bit) for i in range(devices)])


OUTER, INNER = ((0, 1), (3, 2)), ((1, 2), (2, 1))
ENDS = ((1, 0), (2, 3))


def gate_kernel(*refs):
    pass


def after(values, *waited):
    count = len(values)
    anywhere = pl.BlockSpec(memory_space=pl.ANY)
    return pl.pallas_call(
        gate_kernel,
        in_specs=[anywhere] * (count + len(waited)),
        out_specs=[anywhere] * count,
        out_shape=[jax.ShapeDtypeStruct(value.shape, value.dtype) for value in values],
        input_output_aliases={i: i for i in range(count)},
        compiler_params=pltpu.CompilerParams(vmem_limit_bytes=60 * MIB),
        cost_estimate=BRIEF,
        name="after",
    )(*values, *waited)


def dense_shards(h_rows, gates, expert_ids, cotangent, down_weight, swapped):
    devices = lax.axis_size("expert")
    here = lax.axis_index("expert").reshape(1)
    tokens, top, hidden = h_rows.shape
    capacity = min(tokens, 3 * tokens * top // (2 * devices))
    weight = down_weight[0]
    slot_ids = slots_of(expert_ids, swapped, devices)
    h_flat = h_rows.reshape(-1, hidden)

    routing = jnp.concatenate([slot_ids.T.astype(F32), gates.T], axis=0)
    routing = jnp.broadcast_to(routing, (devices,) + routing.shape)
    place, send_h = pack(slot_ids.reshape(1, -1), h_flat, devices, capacity)

    own = cotangent
    from_end, from_inner, from_near_end = passed(OUTER, own), passed(INNER, own), passed(ENDS, own)
    own_y = swapped_with(own, 2)
    near = added(from_inner, from_near_end)
    start_end, start_inner, near = after((from_end, from_inner, near), own_y)
    from_far, from_middle = passed(INNER, start_end), passed(ENDS, start_inner)
    near_y = swapped_with(near, 2)
    middle = added(from_far, from_middle)
    start_far, middle, routing = after((from_far, middle, routing), near_y, send_h)
    last = added(from_end, passed(ENDS, start_far))
    middle_y = swapped_with(middle, 2)
    routing = lax.all_to_all(routing, "expert", split_axis=0, concat_axis=0, tiled=True)
    rank, gate = route(here, routing, top)
    send_h, last = after((send_h, last), middle_y, rank)
    rows_h = lax.all_to_all(
        send_h.reshape(devices, capacity, hidden), "expert", split_axis=0, concat_axis=0, tiled=True
    )
    last_y = swapped_with(last, 2)

    z_rows, back, sibling = scaled_rows(here, rank, gate, weight, [own, own_y, near, near_y], (0, 1), capacity, [])
    sibling = swapped_with(sibling, 1)
    z_rows, back, _ = sibling_rows(here, weight, sibling, (0, 1), z_rows, back)
    z_rows, back, sibling_last = scaled_rows(
        here, rank, gate, weight, [middle, middle_y, last, last_y], (2, 3), capacity, [z_rows, back]
    )
    sibling_last = swapped_with(sibling_last, 1)
    z_rows, back, ready = sibling_rows(here, weight, sibling_last, (2, 3), z_rows, back)
    back_rows = lax.all_to_all(back, "expert", split_axis=0, concat_axis=0, tiled=True).reshape(-1, hidden)

    rows_h, = after((rows_h,), ready)
    beside, across = [], []
    for slots in ((3, 2), (1, 0)):
        other = swapped_with(forward_rows(here, rank, gate, rows_h, weight, slots, 1), 1)
        mine = forward_rows(here, rank, gate, rows_h, weight, slots, 0)
        across += [swapped_with(part, 2) for part in summed(here, rank, mine, other, slots, 1)]
        beside += summed(here, rank, mine, other, slots, 0)
    grad_sum = lax.dot_general(
        rows_h.reshape(-1, hidden), z_rows.reshape(devices * capacity, -1), (((0,), (0,)), ((), ())),
        preferred_element_type=F32,
    )
    weight_grad = grad_sum.astype(BF16)[None]
    far, mid, close, kept = zip(beside, across)
    far = (*after((far[0],), weight_grad), far[1])
    outer1 = passed(OUTER, added(*far))
    mid = added(*mid, outer1)
    outer2, inner2 = passed(OUTER, mid), passed(INNER, mid)
    close, = after((added(*close, outer2),), back_rows)
    outer3, inner3 = passed(OUTER, close), passed(INNER, close)
    ends3 = passed(ENDS, added(*far, inner2))
    mixed = added(*kept, outer3, inner3, ends3)

    h_grad, gate_grad = unpack(place.reshape(-1, 1), gates.reshape(-1, 1), h_flat, back_rows)
    return (
        mixed,
        gate_grad.reshape(tokens, top),
        h_grad.reshape(tokens, top, hidden),
        weight_grad,
    )


def shards(h_rows, *rest):
    devices = lax.axis_size("expert")
    dense = devices == 16 and devices <= 2 * h_rows.shape[1]
    return (dense_shards if dense else sparse_shards)(h_rows, *rest)


def solution(mesh):
    in_specs = (
        P(("groups", "expert"), None, None),
        P(("groups", "expert"), None),
        P(("groups", "expert"), None),
        P(("groups", "expert"), None),
        P("expert", None, None),
        P(),
    )
    out_specs = (
        P(("groups", "expert"), None),
        P(("groups", "expert"), None),
        P(("groups", "expert"), None, None),
        P(("groups", "expert"), None, None),
    )
    return jax.shard_map(shards, mesh=mesh, in_specs=in_specs, out_specs=out_specs, check_vma=False)
```

```python
import functools

import jax
import jax.numpy as jnp
from jax import lax
from jax.experimental import pallas as pl
from jax.experimental.pallas import tpu as pltpu
from jax.sharding import PartitionSpec as P

F32 = jnp.float32
BF16 = jnp.bfloat16
MIB = 1 << 20
BRIEF = pl.CostEstimate(flops=0, transcendentals=0, bytes_accessed=0)


def slots_of(ids, swapped, devices):
    half_way = devices // 2
    table = jnp.arange(devices, dtype=jnp.int32)
    table = (table + half_way * swapped[table % half_way]) % devices
    return jnp.sum(jnp.where(ids[..., None] == jnp.arange(devices, dtype=jnp.int32), table, 0), axis=-1)


def place_rows(values, target, ranks, devices, capacity):
    buffer = jnp.zeros((devices, capacity, values.shape[-1]), values.dtype)
    return buffer.at[target, ranks].set(values)


def sparse_shards(h_rows, gates, expert_ids, cotangent, down_weight, swapped):
    devices = lax.axis_size("expert")
    tokens_here, top_count, hidden = h_rows.shape
    width = cotangent.shape[1]
    capacity = min(tokens_here, 3 * tokens_here * top_count // (2 * devices))
    experts = jnp.arange(devices, dtype=jnp.int32)
    weight = down_weight[0]
    flat_ids = slots_of(expert_ids.reshape(-1), swapped, devices)
    onehot = (flat_ids[:, None] == experts[None, :]).astype(jnp.int32)
    ranks = jnp.sum((jnp.cumsum(onehot, axis=0) - onehot) * onehot, axis=1)
    send_h = place_rows(h_rows.reshape(-1, hidden), flat_ids, ranks, devices, capacity)
    received = lax.all_to_all(send_h, "expert", split_axis=0, concat_axis=0, tiled=True)
    result = jnp.einsum("sch,hd->scd", received, weight, preferred_element_type=F32)
    results = result.astype(BF16)
    returned = lax.all_to_all(results, "expert", split_axis=0, concat_axis=0, tiled=True)
    out_rows = returned[flat_ids, ranks].reshape(tokens_here, top_count, width)
    mixed = jnp.einsum("tk,tkd->td", gates, out_rows.astype(F32)).astype(BF16)
    gate_grad = jnp.einsum("td,tkd->tk", cotangent, out_rows, preferred_element_type=F32)
    scaled = (gates[:, :, None] * cotangent[:, None, :].astype(F32)).astype(BF16)
    send_z = place_rows(scaled.reshape(-1, width), flat_ids, ranks, devices, capacity)
    recv_z = lax.all_to_all(send_z, "expert", split_axis=0, concat_axis=0, tiled=True)
    flat_z = recv_z.reshape(-1, width)
    flat_h = received.reshape(-1, hidden)
    grad_sum = lax.dot_general(flat_h, flat_z, (((0,), (0,)), ((), ())), preferred_element_type=F32)
    back = lax.dot_general(flat_z, weight, (((1,), (1,)), ((), ())), preferred_element_type=F32).astype(BF16)
    back_rows = lax.all_to_all(
        back.reshape(devices, capacity, hidden), "expert", split_axis=0, concat_axis=0, tiled=True
    )
    h_grad = back_rows[flat_ids, ranks].reshape(tokens_here, top_count, hidden)
    return (mixed, gate_grad, h_grad, grad_sum.astype(BF16)[None])


def upper(size):
    rows = lax.broadcasted_iota(jnp.int32, (size, size), 0)
    columns = lax.broadcasted_iota(jnp.int32, (size, size), 1)
    return (rows < columns).astype(F32).astype(BF16)


def pack_kernel(devices, capacity, ids_ref, h_ref, place_ref, sent_ref, place_scratch):
    pairs = ids_ref.shape[1]
    rows = sent_ref.shape[0]

    @pl.when(pl.program_id(0) == 0)
    def _():
        before = jnp.zeros((devices, 1), F32)
        for tile in range(pairs // 128):
            ids = ids_ref[:, tile * 128:(tile + 1) * 128]
            named = lax.broadcasted_iota(jnp.int32, (devices, 128), 0) == ids
            ones = jnp.where(named, 1.0, 0.0)
            rank = jnp.dot(ones.astype(BF16), upper(128), preferred_element_type=F32) + before
            before = before + jnp.sum(ones, axis=1, keepdims=True)
            rank = jnp.sum(jnp.where(named, rank, 0.0), axis=0, keepdims=True)
            place_scratch[:, tile * 128:(tile + 1) * 128] = ids * capacity + rank.astype(jnp.int32)
        place_ref[...] = place_scratch[...]

    first = pl.program_id(0) * rows
    wanted = lax.broadcasted_iota(jnp.int32, (rows, pairs), 0) + first
    chosen = jnp.where(wanted == place_scratch[...], 1.0, 0.0).astype(BF16)
    sent_ref[...] = jnp.dot(chosen, h_ref[...], preferred_element_type=F32).astype(BF16)


def pack(ids, h_flat, devices, capacity, steps=4):
    pairs, hidden = h_flat.shape
    rows = devices * capacity // steps
    return pl.pallas_call(
        functools.partial(pack_kernel, devices, capacity),
        grid=(steps,),
        in_specs=[
            pl.BlockSpec((1, pairs), lambda i: (0, 0)),
            pl.BlockSpec((pairs, hidden), lambda i: (0, 0)),
        ],
        out_specs=[
            pl.BlockSpec((1, pairs), lambda i: (0, 0)),
            pl.BlockSpec((rows, hidden), lambda i: (i, 0)),
        ],
        out_shape=[
            jax.ShapeDtypeStruct((1, pairs), jnp.int32),
            jax.ShapeDtypeStruct((devices * capacity, hidden), BF16),
        ],
        scratch_shapes=[pltpu.VMEM((1, pairs), jnp.int32)],
        compiler_params=pltpu.CompilerParams(vmem_limit_bytes=60 * MIB),
        cost_estimate=BRIEF,
        name="pack",
    )(ids, h_flat)


def unpack_kernel(slots, place_ref, gate_ref, h_ref, back_ref, grad_ref, gate_grad_ref):
    rows = place_ref.shape[0]
    chosen = lax.broadcasted_iota(jnp.int32, (rows, slots), 1) == place_ref[...]
    grad = jnp.dot(jnp.where(chosen, 1.0, 0.0).astype(BF16), back_ref[...], preferred_element_type=F32)
    grad_ref[...] = grad.astype(BF16)
    gate_grad_ref[...] = jnp.sum(grad * h_ref[...].astype(F32), axis=1, keepdims=True) / gate_ref[...]


def unpack(place, gates, h_flat, back_rows, steps=4):
    pairs, hidden = h_flat.shape
    slots = back_rows.shape[0]
    rows = pairs // steps
    return pl.pallas_call(
        functools.partial(unpack_kernel, slots),
        grid=(steps,),
        in_specs=[
            pl.BlockSpec((rows, 1), lambda i: (i, 0)),
            pl.BlockSpec((rows, 1), lambda i: (i, 0)),
            pl.BlockSpec((rows, hidden), lambda i: (i, 0)),
            pl.BlockSpec((slots, hidden), lambda i: (0, 0)),
        ],
        out_specs=[
            pl.BlockSpec((rows, hidden), lambda i: (i, 0)),
            pl.BlockSpec((rows, 1), lambda i: (i, 0)),
        ],
        out_shape=[
            jax.ShapeDtypeStruct((pairs, hidden), BF16),
            jax.ShapeDtypeStruct((pairs, 1), F32),
        ],
        compiler_params=pltpu.CompilerParams(vmem_limit_bytes=60 * MIB),
        cost_estimate=BRIEF,
        name="unpack",
    )(place, gates, h_flat, back_rows)


def line_slots(position):
    near = jnp.minimum(position, 3 - position)
    turned = (near, near + 1, near + 2, 3 - 3 * near)
    return [jnp.where(position < 2, slot, 3 - slot) for slot in turned]


def route_kernel(devices, top, here_ref, routing_ref, rank_ref, gate_ref):
    for side in range(2):
        mine = (here_ref[0] ^ side).astype(F32)
        marks, picked = [], []
        for source in range(devices):
            ids = routing_ref[source, :top, :]
            gates = routing_ref[source, top:, :]
            named = ids == mine
            marks.append(jnp.sum(jnp.where(named, 1.0, 0.0), axis=0, keepdims=True))
            picked.append(jnp.sum(jnp.where(named, gates, 0.0), axis=0, keepdims=True))
        mark = jnp.concatenate(marks, axis=0)
        rank = jnp.dot(mark.astype(BF16), upper(mark.shape[1]), preferred_element_type=F32)
        rank_ref[side] = jnp.where(mark > 0, rank, -1.0).astype(jnp.int32)
        gate_ref[side] = jnp.concatenate(picked, axis=0)


def route(here, routing, top):
    devices, _, tokens = routing.shape
    return pl.pallas_call(
        functools.partial(route_kernel, devices, top),
        in_specs=[pl.BlockSpec(memory_space=pltpu.SMEM), pl.BlockSpec(memory_space=pltpu.VMEM)],
        out_specs=[pl.BlockSpec(memory_space=pltpu.VMEM)] * 2,
        out_shape=[
            jax.ShapeDtypeStruct((2, devices, tokens), jnp.int32),
            jax.ShapeDtypeStruct((2, devices, tokens), F32),
        ],
        cost_estimate=BRIEF,
        name="route",
    )(here, routing)


def chosen_rows(rank_ref, side, source, capacity):
    rank = rank_ref[side, pl.ds(source, 1), :]
    return lax.broadcasted_iota(jnp.int32, (capacity, rank.shape[1]), 0) == rank


def gate_column(gate_ref, chosen, side, source):
    return jnp.sum(jnp.where(chosen, gate_ref[side, pl.ds(source, 1), :], 0.0), axis=1, keepdims=True)


def one_hot(chosen):
    return jnp.where(chosen, 1.0, 0.0).astype(BF16)


def lane_sources(here, slots, lane):
    line, across = here // 4, (here // 2) % 2
    places = line_slots(line)
    return [places[slot] * 4 + (across ^ turn) * 2 + lane for slot in slots for turn in range(2)]


def place_out(pieces, sem):
    copies = [pltpu.make_async_copy(source, target, sem.at[i]) for i, (source, target) in enumerate(pieces)]
    for copy in copies:
        copy.start()
    return copies


def scale_kernel(capacity, slots, held, here_ref, rank_ref, gate_ref, weight_ref, *refs):
    count = 2 * len(slots)
    blocks, refs = refs[:count], refs[count + held:]
    z_ref, back_ref, sibling_ref, z_scratch, back_scratch, z_sem, back_sem = refs
    sources = lane_sources(here_ref[0], slots, here_ref[0] % 2)
    for i, source in enumerate(sources):
        chosen = [chosen_rows(rank_ref, side, source, capacity) for side in range(2)]
        gates = [gate_column(gate_ref, chosen[side], side, source) for side in range(2)]
        both = jnp.concatenate([one_hot(chosen[0]), one_hot(chosen[1])], axis=0)
        rows = jnp.dot(both, blocks[i][...], preferred_element_type=F32)
        z_scratch[i] = (rows[:capacity] * gates[0]).astype(BF16)
        sibling_ref[i] = (rows[capacity:] * gates[1]).astype(BF16)
    copies = place_out([(z_scratch.at[i], z_ref.at[source]) for i, source in enumerate(sources)], z_sem)
    flat = z_scratch[...].reshape(count * capacity, z_scratch.shape[2])
    back = lax.dot_general(flat, weight_ref[...], (((1,), (1,)), ((), ())), preferred_element_type=F32)
    back_scratch[...] = back.astype(BF16).reshape(back_scratch.shape)
    copies += place_out([(back_scratch.at[i], back_ref.at[source]) for i, source in enumerate(sources)], back_sem)
    for copy in copies:
        copy.wait()


def scaled_rows(here, rank, gate, weight, blocks, slots, capacity, buffers):
    devices = rank.shape[1]
    hidden, width = weight.shape
    count = len(blocks)
    tokens = blocks[0].shape[0]
    vmem, anywhere = pl.BlockSpec(memory_space=pltpu.VMEM), pl.BlockSpec(memory_space=pltpu.HBM)
    return pl.pallas_call(
        functools.partial(scale_kernel, capacity, slots, len(buffers)),
        in_specs=[pl.BlockSpec(memory_space=pltpu.SMEM)] + [vmem] * (3 + count) + [anywhere] * len(buffers),
        out_specs=[anywhere, anywhere, vmem],
        out_shape=[
            jax.ShapeDtypeStruct((devices, capacity, width), BF16),
            jax.ShapeDtypeStruct((devices, capacity, hidden), BF16),
            jax.ShapeDtypeStruct((count, capacity, width), BF16),
        ],
        scratch_shapes=[
            pltpu.VMEM((count, capacity, width), BF16),
            pltpu.VMEM((count, capacity, hidden), BF16),
            pltpu.SemaphoreType.DMA((count,)),
            pltpu.SemaphoreType.DMA((count,)),
        ],
        input_output_aliases={4 + count + i: i for i in range(len(buffers))},
        compiler_params=pltpu.CompilerParams(vmem_limit_bytes=60 * MIB),
        cost_estimate=BRIEF,
        name="scaled_rows",
    )(here, rank, gate, weight, *blocks, *buffers)


def sibling_kernel(capacity, slots, here_ref, weight_ref, rows_ref, _z, _back, z_ref, back_ref, token_ref, back_scratch, z_sem, back_sem):
    count = 2 * len(slots)
    sources = lane_sources(here_ref[0], slots, 1 - here_ref[0] % 2)
    copies = place_out([(rows_ref.at[i], z_ref.at[source]) for i, source in enumerate(sources)], z_sem)
    flat = rows_ref[...].reshape(count * capacity, rows_ref.shape[2])
    back = lax.dot_general(flat, weight_ref[...], (((1,), (1,)), ((), ())), preferred_element_type=F32)
    back_scratch[...] = back.astype(BF16).reshape(back_scratch.shape)
    copies += place_out([(back_scratch.at[i], back_ref.at[source]) for i, source in enumerate(sources)], back_sem)
    token_ref[...] = jnp.zeros_like(token_ref)
    for copy in copies:
        copy.wait()


def sibling_rows(here, weight, rows, slots, z_rows, back):
    count, capacity, width = rows.shape
    hidden = weight.shape[0]
    vmem, anywhere = pl.BlockSpec(memory_space=pltpu.VMEM), pl.BlockSpec(memory_space=pltpu.HBM)
    return pl.pallas_call(
        functools.partial(sibling_kernel, capacity, slots),
        in_specs=[pl.BlockSpec(memory_space=pltpu.SMEM), vmem, vmem, anywhere, anywhere],
        out_specs=[anywhere, anywhere, vmem],
        out_shape=[
            jax.ShapeDtypeStruct(z_rows.shape, BF16),
            jax.ShapeDtypeStruct(back.shape, BF16),
            jax.ShapeDtypeStruct((8, 128), F32),
        ],
        scratch_shapes=[
            pltpu.VMEM((count, capacity, hidden), BF16),
            pltpu.SemaphoreType.DMA((count,)),
            pltpu.SemaphoreType.DMA((count,)),
        ],
        input_output_aliases={3: 0, 4: 1},
        compiler_params=pltpu.CompilerParams(vmem_limit_bytes=60 * MIB),
        cost_estimate=BRIEF,
        name="sibling_rows",
    )(here, weight, rows, z_rows, back)


def forward_kernel(capacity, slots, turn, here_ref, rank_ref, gate_ref, weight_ref, *refs):
    blocks, out_ref = refs[:-1], refs[-1]
    sources = lane_sources(here_ref[0], slots, (here_ref[0] % 2) ^ turn)
    flat = jnp.concatenate([block[0, 0] for block in blocks], axis=0)
    out = jnp.dot(flat, weight_ref[...], preferred_element_type=F32).astype(BF16).astype(F32)
    for j, source in enumerate(sources):
        gate = gate_column(gate_ref, chosen_rows(rank_ref, 0, source, capacity), 0, source)
        out_ref[j] = (out[j * capacity:(j + 1) * capacity, :] * gate).astype(BF16)


def forward_rows(here, rank, gate, rows_h, weight, slots, turn):
    devices, capacity, hidden = rows_h.shape
    width = weight.shape[1]
    count = 2 * len(slots)

    def block(j):
        return lambda i, here: (lane_sources(here[0], slots, 0)[j] // 2, (here[0] % 2) ^ turn, 0, 0)

    whole = pl.BlockSpec(rank.shape, lambda i, here: (0, 0, 0))
    rows = rows_h.reshape(devices // 2, 2, capacity, hidden)
    return pl.pallas_call(
        functools.partial(forward_kernel, capacity, slots, turn),
        grid_spec=pltpu.PrefetchScalarGridSpec(
            num_scalar_prefetch=1,
            grid=(1,),
            in_specs=[whole, whole, pl.BlockSpec((hidden, width), lambda i, here: (0, 0))]
            + [pl.BlockSpec((1, 1, capacity, hidden), block(j)) for j in range(count)],
            out_specs=pl.BlockSpec((count, capacity, width), lambda i, here: (0, 0, 0)),
        ),
        out_shape=jax.ShapeDtypeStruct((count, capacity, width), BF16),
        compiler_params=pltpu.CompilerParams(vmem_limit_bytes=24 * MIB),
        cost_estimate=BRIEF,
        name="forward_rows",
    )(here, rank, gate, weight, *[rows] * count)


def sum_kernel(capacity, slots, turn, here_ref, rank_ref, own_ref, other_ref, *part_refs):
    for step, slot in enumerate(slots):

        @pl.when(pl.program_id(0) == step)
        def _():
            source = lane_sources(here_ref[0], (slot,), here_ref[0] % 2)[turn]
            both = [one_hot(chosen_rows(rank_ref, side, source, capacity)) for side in range(2)]
            rows = jnp.concatenate([own_ref[0], other_ref[0]], axis=0)
            part = lax.dot_general(
                jnp.concatenate(both, axis=0), rows, (((0,), (0,)), ((), ())), preferred_element_type=F32
            )
            part_refs[step][...] = part.astype(BF16)


def summed(here, rank, own, other, slots, turn):
    _, capacity, width = own.shape
    tokens = rank.shape[2]
    block = pl.BlockSpec((1, capacity, width), lambda i, here: (2 * i + turn, 0, 0))
    return pl.pallas_call(
        functools.partial(sum_kernel, capacity, slots, turn),
        grid_spec=pltpu.PrefetchScalarGridSpec(
            num_scalar_prefetch=1,
            grid=(len(slots),),
            in_specs=[pl.BlockSpec(rank.shape, lambda i, here: (0, 0, 0)), block, block],
            out_specs=[pl.BlockSpec((tokens, width), lambda i, here: (0, 0))] * len(slots),
        ),
        out_shape=[jax.ShapeDtypeStruct((tokens, width), BF16)] * len(slots),
        compiler_params=pltpu.CompilerParams(vmem_limit_bytes=24 * MIB),
        cost_estimate=BRIEF,
        name="summed",
    )(here, rank, own, other)


def added(*values):
    total = values[0].astype(F32)
    for value in values[1:]:
        total = total + value.astype(F32)
    return total.astype(BF16)


def passed(pairs, value):
    return lax.ppermute(value, "expert", [(a * 4 + lane, b * 4 + lane) for a, b in pairs for lane in range(4)])


def swapped_with(value, bit):
    devices = lax.axis_size("expert")
    return lax.ppermute(value, "expert", [(i, i ^ bit) for i in range(devices)])


OUTER, INNER = ((0, 1), (3, 2)), ((1, 2), (2, 1))
ENDS = ((1, 0), (2, 3))


def gate_kernel(*refs):
    pass


def after(values, *waited):
    count = len(values)
    anywhere = pl.BlockSpec(memory_space=pl.ANY)
    return pl.pallas_call(
        gate_kernel,
        in_specs=[anywhere] * (count + len(waited)),
        out_specs=[anywhere] * count,
        out_shape=[jax.ShapeDtypeStruct(value.shape, value.dtype) for value in values],
        input_output_aliases={i: i for i in range(count)},
        compiler_params=pltpu.CompilerParams(vmem_limit_bytes=1 * MIB),
        cost_estimate=BRIEF,
        name="after",
    )(*values, *waited)


def dense_shards(h_rows, gates, expert_ids, cotangent, down_weight, swapped):
    devices = lax.axis_size("expert")
    here = lax.axis_index("expert").reshape(1)
    tokens, top, hidden = h_rows.shape
    capacity = min(tokens, 3 * tokens * top // (2 * devices))
    weight = down_weight[0]
    slot_ids = slots_of(expert_ids, swapped, devices)
    h_flat = h_rows.reshape(-1, hidden)

    routing = jnp.concatenate([slot_ids.T.astype(F32), gates.T], axis=0)
    routing = jnp.broadcast_to(routing, (devices,) + routing.shape)
    place, send_h = pack(slot_ids.reshape(1, -1), h_flat, devices, capacity)

    own = cotangent
    from_end, from_inner, from_near_end = passed(OUTER, own), passed(INNER, own), passed(ENDS, own)
    own_y = swapped_with(own, 2)
    near = added(from_inner, from_near_end)
    start_end, start_inner, near = after((from_end, from_inner, near), own_y)
    from_far, from_middle = passed(INNER, start_end), passed(ENDS, start_inner)
    near_y = swapped_with(near, 2)
    middle = added(from_far, from_middle)
    start_far, middle, routing = after((from_far, middle, routing), near_y, send_h)
    last = added(from_end, passed(ENDS, start_far))
    middle_y = swapped_with(middle, 2)
    routing = lax.all_to_all(routing, "expert", split_axis=0, concat_axis=0, tiled=True)
    rank, gate = route(here, routing, top)
    send_h, last = after((send_h, last), middle_y, rank)
    rows_h = lax.all_to_all(
        send_h.reshape(devices, capacity, hidden), "expert", split_axis=0, concat_axis=0, tiled=True
    )
    last_y = swapped_with(last, 2)

    z_rows, back, sibling = scaled_rows(here, rank, gate, weight, [own, own_y, near, near_y], (0, 1), capacity, [])
    sibling = swapped_with(sibling, 1)
    z_rows, back, _ = sibling_rows(here, weight, sibling, (0, 1), z_rows, back)
    z_rows, back, sibling_last = scaled_rows(
        here, rank, gate, weight, [middle, middle_y, last, last_y], (2, 3), capacity, [z_rows, back]
    )
    sibling_last = swapped_with(sibling_last, 1)
    z_rows, back, ready = sibling_rows(here, weight, sibling_last, (2, 3), z_rows, back)
    back_rows = lax.all_to_all(back, "expert", split_axis=0, concat_axis=0, tiled=True).reshape(-1, hidden)

    rows_h, = after((rows_h,), ready)
    beside, across = [], []
    for slots in ((3, 2), (1, 0)):
        other = swapped_with(forward_rows(here, rank, gate, rows_h, weight, slots, 1), 1)
        mine = forward_rows(here, rank, gate, rows_h, weight, slots, 0)
        across += [swapped_with(part, 2) for part in summed(here, rank, mine, other, slots, 1)]
        beside += summed(here, rank, mine, other, slots, 0)
    grad_sum = lax.dot_general(
        rows_h.reshape(-1, hidden), z_rows.reshape(devices * capacity, -1), (((0,), (0,)), ((), ())),
        preferred_element_type=F32,
    )
    weight_grad = grad_sum.astype(BF16)[None]
    far, mid, close, kept = zip(beside, across)
    far = (*after((far[0],), weight_grad), far[1])
    outer1 = passed(OUTER, added(*far))
    mid = added(*mid, outer1)
    outer2, inner2 = passed(OUTER, mid), passed(INNER, mid)
    close, = after((added(*close, outer2),), back_rows)
    outer3, inner3 = passed(OUTER, close), passed(INNER, close)
    ends3 = passed(ENDS, added(*far, inner2))
    mixed = added(*kept, outer3, inner3, ends3)

    h_grad, gate_grad = unpack(place.reshape(-1, 1), gates.reshape(-1, 1), h_flat, back_rows)
    return (
        mixed,
        gate_grad.reshape(tokens, top),
        h_grad.reshape(tokens, top, hidden),
        weight_grad,
    )


def shards(h_rows, *rest):
    devices = lax.axis_size("expert")
    dense = devices == 16 and devices <= 2 * h_rows.shape[1]
    return (dense_shards if dense else sparse_shards)(h_rows, *rest)


def solution(mesh):
    in_specs = (
        P(("groups", "expert"), None, None),
        P(("groups", "expert"), None),
        P(("groups", "expert"), None),
        P(("groups", "expert"), None),
        P("expert", None, None),
        P(),
    )
    out_specs = (
        P(("groups", "expert"), None),
        P(("groups", "expert"), None),
        P(("groups", "expert"), None, None),
        P(("groups", "expert"), None, None),
    )
    return jax.shard_map(shards, mesh=mesh, in_specs=in_specs, out_specs=out_specs, check_vma=False)
```
